32 devices in a mesh: dp: 4 (over z), ctx: 2 (over y), seq: 4 (over x, core).
Axes of the slice: x: 2, y: 2, z: 4, core: 2. Of those that a mesh axis runs over, the one named last changes fastest.
Arguments:
- tokens: bfloat16 [4096, 2048], P(('dp', 'ctx', 'seq')), may hold values from -6 to 6
- w_query: bfloat16 [2048, 2048], P(None, 'seq'), may hold values from -1 to 1, as said below
- w_key: bfloat16 [2048, 2048], P(None, 'seq'), may hold values from -1 to 1, as said below
- w_value: bfloat16 [2048, 2048], P(None, 'seq'), may hold values from -0.125 to 0.125
- gain_query: float32 [2048], P('seq'), may hold values from 1 to 2
- gain_key: float32 [2048], P('seq'), may hold values from 1 to 2
- w_out: bfloat16 [2048, 2048], P('seq'), may hold values from -0.125 to 0.125
- gain_attn: float32 [2048], replicated, may hold values from 0.5 to 1.5
- w_gate: bfloat16 [2048, 8192], P(None, 'seq'), may hold values from -0.125 to 0.125
- w_up: bfloat16 [2048, 8192], P(None, 'seq'), may hold values from -0.125 to 0.125
- w_down: bfloat16 [8192, 2048], P('seq'), may hold values from -0.0625 to 0.0625
- gain_ffn: float32 [2048], replicated, may hold values from 0.5 to 1.5
- cotangent: bfloat16 [4096, 2048], P(('dp', 'ctx', 'seq')), may hold values from -6 to 6
- source_ids: int32 [4], P('dp'), may hold values from 0 to 7
- group_weights: float32 [8], replicated, may hold values from 0.5 to 2
Outputs:
- out_tokens: bfloat16 [4096, 2048], P(('dp', 'ctx', 'seq'))
- grad_tokens: float32 [4096, 2048], P(('dp', 'ctx', 'seq'))
- grad_w_query: float32 [2048, 2048], P(None, 'seq')
- grad_w_key: float32 [2048, 2048], P(None, 'seq')
- grad_w_value: float32 [2048, 2048], P(None, 'seq')
- grad_gain_query: float32 [2048], P('seq')
- grad_gain_key: float32 [2048], P('seq')
- grad_w_out: float32 [2048, 2048], P('seq')
- grad_gain_attn: float32 [2048], replicated
- grad_w_gate: float32 [2048, 8192], P(None, 'seq')
- grad_w_up: float32 [2048, 8192], P(None, 'seq')
- grad_w_down: float32 [8192, 2048], P('seq')
- grad_gain_ffn: float32 [2048], replicated
The draws below stay inside these ranges and needn't reach their ends.
Inputs may be any that keep to these rules, and one draw needn't show every extreme that they name: `w_query`: entries of order one over the square root of 2048. `w_key`: entries of order one over the square root of 2048.
All inputs are finite; a program needn't handle non-finite values.
Results may differ from the reference program's by a relative error of at most 0.025.
Values may be sent and summed in bfloat16 or wider, within the bound.
No kernel may reach another device: no remote copies, remote signals or barrier semaphores. Data moves between devices by JAX's collectives and lax.ppermute only.
A program may use at most 256 MiB of HBM per device.

```python
import math
import jax
import jax.numpy as jnp
from jax import lax

D = 2048
HEADS = 16
HD = 128
FF = 8192
SOURCES = 8
SEQ_LEN = 1024
SEQS = 4
TOKENS = 4096


def column_scaled(key):
    column = jnp.arange(D)
    share = (column // HD).astype(jnp.float32) / max(HEADS - 1, 1)
    base = jax.random.truncated_normal(key, -4.0, 4.0, (D, D), jnp.float32)
    factor = jnp.exp(share * 0.5 * math.log(3.0))
    return (base * factor[None, :] * D ** (-0.5)).astype(jnp.bfloat16)


def draw_w_query(key, part):
    return column_scaled(jax.random.fold_in(key, 11))


def draw_w_key(key, part):
    return column_scaled(jax.random.fold_in(key, 23))


def set_ends(array, own_key, least, top_value):
    extent = array.shape
    index_at = [jax.random.randint(jax.random.fold_in(own_key, axis), (), 0, extent[axis]) for axis in range(len(extent))]
    array = array.at[tuple(index_at)].set(least)
    longest = extent.index(max(extent))
    index_at[longest] = (index_at[longest] + 1) % extent[longest]
    return array.at[tuple(index_at)].set(top_value)


def block_scale(stream_key, extent, shards, low, top_value):
    factor_of, own = 1.0, jax.random.fold_in(stream_key, 6)
    for axis_at, parts in shards:
        draws = jnp.exp(jax.random.uniform(jax.random.fold_in(own, axis_at), (parts,), jnp.float32, low / len(shards), top_value / len(shards)))
        factor_of = factor_of * jnp.repeat(draws, extent[axis_at] // parts).reshape([-1 if axis == axis_at else 1 for axis in range(len(extent))])
    return factor_of


def noise(own_key, dims, scale, bound, shards=(), kind=jnp.bfloat16):
    entries = jax.random.normal(own_key, dims, jnp.float32) * scale
    if len(shards) > 0:
        entries = block_scale(own_key, dims, shards, -0.22, 0.18) * entries
    return jnp.clip(entries, min=-bound, max=bound).astype(kind)


def setup_inputs(seed: int = 0) -> dict:
    arg_keys = jax.random.split(jax.random.key(seed), 16)
    return {
        "tokens": noise(arg_keys[0], (TOKENS, D), 1.0, 6.0, ((0, 32),)),
        "w_query": draw_w_query(jax.random.fold_in(arg_keys[15], 71), 0),
        "w_key": draw_w_key(jax.random.fold_in(arg_keys[15], 71), 0),
        "w_value": noise(arg_keys[3], (D, D), D ** -0.5, 0.125, ((1, 4),)),
        "gain_query": jnp.clip(1.0 + 1.0 * jax.random.uniform(arg_keys[4], (D,), jnp.float32) ** block_scale(arg_keys[4], (D,), ((0, 4),), -0.2, 0.2), 1.0, 2.0),
        "gain_key": jnp.clip(1.0 + 1.0 * jax.random.uniform(arg_keys[5], (D,), jnp.float32) ** block_scale(arg_keys[5], (D,), ((0, 4),), -0.2, 0.2), 1.0, 2.0),
        "w_out": noise(arg_keys[6], (D, D), D ** -0.5, 0.125, ((0, 4),)),
        "gain_attn": jnp.clip(jax.random.uniform(arg_keys[7], (D,), jnp.float32, 0.5, 1.5), 0.5, 1.5),
        "w_gate": noise(arg_keys[8], (D, FF), D ** -0.5, 0.125, ((1, 4),)),
        "w_up": noise(arg_keys[9], (D, FF), D ** -0.5, 0.125, ((1, 4),)),
        "w_down": noise(arg_keys[10], (FF, D), FF ** -0.5, 0.0625, ((0, 4),)),
        "gain_ffn": jnp.clip(jax.random.uniform(arg_keys[11], (D,), jnp.float32, 0.5, 1.5), 0.5, 1.5),
        "cotangent": noise(arg_keys[12], (TOKENS, D), 1.0, 6.0, ((0, 32),)),
        "source_ids": set_ends(jax.random.randint(arg_keys[13], (SEQS,), 0, SOURCES), jax.random.fold_in(arg_keys[13], 1), 0, SOURCES - 1).astype(jnp.int32),
        "group_weights": jnp.clip(jnp.exp(jax.random.uniform(arg_keys[14], (SOURCES,), jnp.float32, math.log(0.5), math.log(2.0))), 0.5, 2.0),
    }


EPS = 1e-06
ROPE_BASE = 500000.0
HIGH = lax.Precision.HIGHEST

@jax.custom_vjp
def low(v):
    return lax.optimization_barrier(v.astype(jnp.bfloat16)).astype(jnp.float32)

@jax.custom_vjp
def low_back(v):
    return v

def low_keep(v):
    return (low(v), None)

def low_pass(kept, grad):
    return (grad,)

def back_keep(v):
    return (v, None)

def back_low(kept, grad):
    return (low(grad),)
low.defvjp(low_keep, low_pass)
low_back.defvjp(back_keep, back_low)

def rms_unit(values_in):
    return values_in * lax.rsqrt(lax.optimization_barrier(jnp.mean(values_in * values_in, axis=-1, keepdims=True)) + EPS)

def matmul(left, right):
    return jnp.dot(left, right, precision=HIGH)

def rope_turn(values_in, cosine, sine, direction):
    half_dim = values_in.shape[-1] // 2
    first = values_in[..., :half_dim]
    second = values_in[..., half_dim:]
    return jnp.concatenate([first * cosine - direction * second * sine, second * cosine + direction * first * sine], axis=-1)

def attend(query_rot, key_rot, value_low):
    block_rows = min(512, SEQ_LEN)
    key_pos = jnp.arange(SEQ_LEN, dtype=jnp.int32)
    row_starts = (jnp.arange(SEQ_LEN // block_rows) * block_rows).astype(jnp.int32)

    def per_head(head_parts):
        query_head, key_head, value_head = head_parts

        def one_block(row_start):
            query_block = lax.dynamic_slice_in_dim(query_head, row_start, block_rows, 0)
            scores = low_back(matmul(query_block, key_head.T) * HD ** (-0.5))
            causal = key_pos[None, :] <= (row_start + jnp.arange(block_rows, dtype=jnp.int32))[:, None]
            probs = low(jax.nn.softmax(jnp.where(causal, scores, -1e+30), axis=-1))
            return matmul(probs, value_head)
        return lax.map(jax.checkpoint(one_block), row_starts).reshape(SEQ_LEN, HD)

    def split_heads(array_in):
        return array_in.reshape(SEQ_LEN, HEADS, HD).transpose(1, 0, 2)
    mixed = lax.map(per_head, (split_heads(query_rot), split_heads(key_rot), split_heads(value_low)))
    return mixed.transpose(1, 0, 2).reshape(SEQ_LEN, D)

def block_forward(inputs, cosine, sine):
    tokens_seq, w_query, w_key, w_value, gain_query, gain_key, w_out, gain_attn, w_gate, w_up, w_down, gain_ffn = inputs
    query_proj = low_back(matmul(tokens_seq, w_query))
    key_proj = low_back(matmul(tokens_seq, w_key))
    value_proj = low_back(matmul(tokens_seq, w_value))
    query_rot = low(rope_turn((rms_unit(query_proj) * gain_query).reshape(SEQ_LEN, HEADS, HD), cosine, sine, 1.0).reshape(SEQ_LEN, D))
    key_rot = low(rope_turn((rms_unit(key_proj) * gain_key).reshape(SEQ_LEN, HEADS, HD), cosine, sine, 1.0).reshape(SEQ_LEN, D))
    value_low = low(value_proj)
    attn = low(low_back(attend(query_rot, key_rot, value_low)))
    proj = low_back(matmul(attn, w_out))
    hidden = tokens_seq + rms_unit(proj) * gain_attn
    hidden_low = low(hidden)
    gate_proj = low_back(matmul(hidden_low, w_gate))
    up_proj = low_back(matmul(hidden_low, w_up))
    inner = low(jax.nn.silu(gate_proj) * up_proj)
    ffn = low_back(matmul(inner, w_down))
    return hidden + rms_unit(ffn) * gain_ffn

def reference(tokens, w_query, w_key, w_value, gain_query, gain_key, w_out, gain_attn, w_gate, w_up, w_down, gain_ffn, cotangent, source_ids, group_weights):
    weights = tuple((weight_arr.astype(jnp.float32) for weight_arr in (w_query, w_key, w_value, gain_query, gain_key, w_out, gain_attn, w_gate, w_up, w_down, gain_ffn)))
    positions = jnp.arange(SEQ_LEN, dtype=jnp.float32)
    half_dim = HD // 2
    inverse = ROPE_BASE ** (-(jnp.arange(half_dim, dtype=jnp.float32) * 2.0 / HD))
    angles = positions[:, None] * inverse[None, :]
    cosine = jnp.cos(angles)[:, None, :]
    sine = jnp.sin(angles)[:, None, :]
    source_range = jnp.arange(SOURCES, dtype=jnp.int32)
    source_weights = group_weights.astype(jnp.float32)

    def one_sequence(totals, seq_item):
        tokens_seq, cot_seq, source = seq_item
        picked = jnp.sum(jnp.where(source_range == source, source_weights, 0.0))
        result, pullback = jax.vjp(lambda *inputs: block_forward(inputs, cosine, sine), tokens_seq, *weights)
        grad_parts = pullback(cot_seq * picked)
        new_totals = tuple((total_part + grad_part for total_part, grad_part in zip(totals, grad_parts[1:])))
        return (new_totals, (result.astype(jnp.bfloat16), grad_parts[0]))
    zero_totals = tuple((jnp.zeros_like(weight_arr) for weight_arr in weights))
    seq_inputs = (tokens.astype(jnp.float32).reshape(SEQS, SEQ_LEN, D), cotangent.astype(jnp.float32).reshape(SEQS, SEQ_LEN, D), source_ids)
    totals, (out_seqs, grad_seqs) = lax.scan(one_sequence, zero_totals, seq_inputs)
    return (out_seqs.reshape(TOKENS, D), grad_seqs.reshape(TOKENS, D), totals[0], totals[1], totals[2], totals[3], totals[4], totals[5], totals[6], totals[7], totals[8], totals[9], totals[10])
```

```python
import functools

import jax
import jax.numpy as jnp
from jax import lax
from jax.experimental import pallas as pl
from jax.experimental.pallas import tpu as pltpu
from jax.sharding import PartitionSpec as P

D = 2048
HD = 128


EPS = 1e-06
ROPE_BASE = 500000.0
NEG_FILL = -1e30
CHUNKS = 4
STREAMS = 2


def flip(value, axis, distance):
    count = lax.axis_size(axis)
    return lax.ppermute(value, axis, [(place, place ^ distance) for place in range(count)])


def distances(axis):
    count = lax.axis_size(axis)
    found = []
    step = 1
    while step < count:
        found.append(step)
        step *= 2
    return found


def gather_rows(own, axis):
    parts = {0: own}
    for distance in reversed(distances(axis)):
        parts.update({o ^ distance: flip(block, axis, distance) for o, block in parts.items()})
    return [parts[o] for o in range(len(parts))]


def gather_both(own, axis):
    mine = gather_rows(own, axis)
    theirs = gather_rows(flip(own, "ctx", 1), axis)
    return jnp.concatenate(mine, axis=0), jnp.concatenate(theirs, axis=0)


def scatter_rows(blocks, axis):
    parts = dict(enumerate(blocks))
    for distance in distances(axis):
        kept = {o: block for o, block in parts.items() if not o & distance}
        for o in sorted(kept, reverse=True):
            sent = parts[o ^ distance].astype(jnp.bfloat16)
            kept[o] = kept[o] + flip(sent, axis, distance).astype(jnp.float32)
        parts = kept
    return parts[0]


def row_blocks(value, count):
    rows = value.shape[0] // count
    return [lax.slice_in_dim(value, o * rows, (o + 1) * rows, axis=0) for o in range(count)]


def norm_back(unit_val, inverse, grad_unit):
    return inverse * (grad_unit - unit_val * jnp.mean(grad_unit * unit_val, axis=-1, keepdims=True))


def contract_rows(left, right):
    return lax.dot_general(
        left, right, (((0,), (0,)), ((), ())), preferred_element_type=jnp.float32
    )


def times_transpose(left, right):
    return lax.dot_general(
        left, right, (((1,), (1,)), ((), ())), preferred_element_type=jnp.float32
    )


def half_columns(value, place):
    width = value.shape[1] // 2
    return lax.dynamic_slice_in_dim(value, place * width, width, axis=1)


def swap_halves(value):
    place = lax.axis_index("ctx")
    return half_columns(value, place), flip(half_columns(value, 1 - place), "ctx", 1)


def turned(values, cosine, sine):
    return values * cosine + pltpu.roll(values, HD // 2, 1) * sine


def attend_kernel(
    query_ref, key_ref, value_ref, inv_query_ref, inv_key_ref, gain_query_ref, gain_key_ref,
    cos_query_ref, sin_query_ref, cos_key_ref, sin_key_ref, at_query_ref, at_key_ref,
    query_low_ref, key_low_ref, mixed_ref, lse_ref,
):
    @pl.when(pl.program_id(1) == 0)
    def _():
        scaled = key_ref[...] * inv_key_ref[...] * gain_key_ref[...]
        key_low_ref[...] = turned(scaled, cos_key_ref[...], sin_key_ref[...]).astype(jnp.bfloat16)

    scaled = query_ref[...] * inv_query_ref[...] * gain_query_ref[...]
    query_low = turned(scaled, cos_query_ref[...], sin_query_ref[...]).astype(jnp.bfloat16)
    query_low_ref[...] = query_low
    scores = HD ** (-0.5) * times_transpose(query_low, key_low_ref[...])
    scores = jnp.where(at_key_ref[...] <= at_query_ref[...], scores, NEG_FILL)
    peak = jnp.max(scores, axis=1, keepdims=True)
    exps = jnp.exp(scores - peak)
    total = jnp.sum(exps, axis=1, keepdims=True)
    probs = (exps * (1.0 / total)).astype(jnp.bfloat16)
    mixed_ref[...] = jnp.dot(
        probs, value_ref[...], preferred_element_type=jnp.float32
    ).astype(jnp.bfloat16)
    lse_ref[0] = peak + jnp.log(total)


def attend_back_kernel(
    query_low_ref, key_low_ref, value_ref, grad_ref, lse_ref,
    cos_query_ref, sin_query_ref, cos_key_ref, sin_key_ref, at_query_ref, at_key_ref,
    grad_query_ref, grad_key_ref, grad_value_ref, prev_key_ref, prev_value_ref,
    key_sum, value_sum,
):
    scale = HD ** (-0.5)
    query_low = query_low_ref[...]
    key_low = key_low_ref[...]
    grad_low = grad_ref[...]
    scores = scale * times_transpose(query_low, key_low)
    allowed = at_key_ref[...] <= at_query_ref[...]
    probs = jnp.exp(jnp.where(allowed, scores, NEG_FILL) - lse_ref[0])
    grad_probs = times_transpose(grad_low, value_ref[...])
    delta = jnp.sum(probs * grad_probs, axis=1, keepdims=True)
    grad_scores = (probs * (grad_probs - delta)).astype(jnp.bfloat16)
    grad_query = scale * jnp.dot(grad_scores, key_low, preferred_element_type=jnp.float32)
    grad_query_ref[...] = turned(grad_query, cos_query_ref[...], -sin_query_ref[...])
    key_part = scale * contract_rows(grad_scores, query_low)
    value_part = contract_rows(probs.astype(jnp.bfloat16), grad_low)

    @pl.when(pl.program_id(1) == 0)
    def _():
        key_sum[...] = key_part
        value_sum[...] = value_part

    @pl.when(pl.program_id(1) > 0)
    def _():
        key_sum[...] += key_part
        value_sum[...] += value_part

    @pl.when(pl.program_id(1) == pl.num_programs(1) - 1)
    def _():
        half = key_sum.shape[0] // 2
        turned_back = turned(key_sum[...], cos_key_ref[...], -sin_key_ref[...])
        grad_key_ref[...] = turned_back[:half]
        prev_key_ref[...] = turned_back[half:].astype(jnp.bfloat16)
        grad_value_ref[...] = value_sum[:half]
        prev_value_ref[...] = value_sum[half:].astype(jnp.bfloat16)


def attention_specs(half_rows, key_rows, block_rows):
    spec = {
        "query": pl.BlockSpec((block_rows, HD), lambda h, i: (i, h)),
        "key": pl.BlockSpec((key_rows, HD), lambda h, i: (0, h)),
        "half": pl.BlockSpec((half_rows, HD), lambda h, i: (0, h)),
        "gain": pl.BlockSpec((1, HD), lambda h, i: (0, h)),
        "query_column": pl.BlockSpec((block_rows, 1), lambda h, i: (i, 0)),
        "key_column": pl.BlockSpec((key_rows, 1), lambda h, i: (0, 0)),
        "key_row": pl.BlockSpec((1, key_rows), lambda h, i: (0, 0)),
        "query_turn": pl.BlockSpec((block_rows, HD), lambda h, i: (i, 0)),
        "key_turn": pl.BlockSpec((key_rows, HD), lambda h, i: (0, 0)),
        "lse": pl.BlockSpec((1, block_rows, 1), lambda h, i: (h, i, 0)),
    }
    return spec


def attend(query, key, value, inv_query, inv_key, gain_query, gain_key, turns, block_rows):
    half_rows, width = query.shape
    key_rows = key.shape[0]
    heads = width // HD
    s = attention_specs(half_rows, key_rows, block_rows)
    return pl.pallas_call(
        attend_kernel,
        grid=(heads, half_rows // block_rows),
        in_specs=[
            s["query"], s["key"], s["key"], s["query_column"], s["key_column"], s["gain"], s["gain"],
            s["query_turn"], s["query_turn"], s["key_turn"], s["key_turn"],
            s["query_column"], s["key_row"],
        ],
        out_specs=[s["query"], s["key"], s["query"], s["lse"]],
        out_shape=[
            jax.ShapeDtypeStruct(query.shape, jnp.bfloat16),
            jax.ShapeDtypeStruct(key.shape, jnp.bfloat16),
            jax.ShapeDtypeStruct(query.shape, jnp.bfloat16),
            jax.ShapeDtypeStruct((heads, half_rows, 1), jnp.float32),
        ],
        name="attend",
    )(query, key, value, inv_query, inv_key, gain_query, gain_key, *turns)


def attend_back(query_low, key_low, value, grad, lse, turns, block_rows):
    half_rows, width = query_low.shape
    key_rows = key_low.shape[0]
    heads = width // HD
    s = attention_specs(half_rows, key_rows, block_rows)
    halves = (half_rows, width)
    return pl.pallas_call(
        attend_back_kernel,
        grid=(heads, half_rows // block_rows),
        in_specs=[
            s["query"], s["key"], s["key"], s["query"], s["lse"],
            s["query_turn"], s["query_turn"], s["key_turn"], s["key_turn"],
            s["query_column"], s["key_row"],
        ],
        out_specs=[s["query"], s["half"], s["half"], s["half"], s["half"]],
        out_shape=[
            jax.ShapeDtypeStruct(halves, jnp.float32),
            jax.ShapeDtypeStruct(halves, jnp.float32),
            jax.ShapeDtypeStruct(halves, jnp.float32),
            jax.ShapeDtypeStruct(halves, jnp.bfloat16),
            jax.ShapeDtypeStruct(halves, jnp.bfloat16),
        ],
        scratch_shapes=[
            pltpu.VMEM((key_rows, HD), jnp.float32),
            pltpu.VMEM((key_rows, HD), jnp.float32),
        ],
        name="attend_back",
    )(query_low, key_low, value, grad, lse, *turns)


def store_kernel(place_ref, mine_ref, theirs_ref, *refs):
    out_ref = refs[-1]

    @pl.when(pl.program_id(0) == 0)
    def _():
        out_ref[...] = mine_ref[...].astype(jnp.float32)

    @pl.when(pl.program_id(0) == 1)
    def _():
        out_ref[...] = theirs_ref[...].astype(jnp.float32)


def store_chunk(buffer, mine, theirs, shape, index, chunks, by_rows):
    place = lax.axis_index("ctx").astype(jnp.int32).reshape(1)
    rows, columns = mine.shape
    if by_rows:
        where_to = lambda i, place_ref: ((place_ref[0] ^ i) * chunks + index, 0)
    else:
        where_to = lambda i, place_ref: (index, place_ref[0] ^ i)
    whole = pl.BlockSpec((rows, columns), lambda i, place_ref: (0, 0))
    operands = [place, mine, theirs]
    in_specs = [whole, whole]
    aliases = {}
    if buffer is not None:
        operands.append(buffer)
        in_specs.append(pl.BlockSpec(memory_space=pl.ANY))
        aliases = {3: 0}
    return pl.pallas_call(
        store_kernel,
        grid_spec=pltpu.PrefetchScalarGridSpec(
            num_scalar_prefetch=1,
            grid=(2,),
            in_specs=in_specs,
            out_specs=pl.BlockSpec((rows, columns), where_to),
        ),
        out_shape=jax.ShapeDtypeStruct(shape, jnp.float32),
        input_output_aliases=aliases,
        name="store",
    )(*operands)


class Gradient:
    def __init__(self, name, shape, chunks, by_rows):
        self.name, self.shape, self.chunks, self.by_rows = name, shape, chunks, by_rows
        self.buffer = None
        self.kept = {}

    def part(self, sides, index):
        left_own, left_other, grad_own, grad_other = sides
        rows = left_own.shape[1] // self.chunks
        cut = functools.partial(
            lax.slice_in_dim, start_index=index * rows, limit_index=(index + 1) * rows, axis=1
        )
        part = contract_rows(cut(left_own), grad_own) + contract_rows(cut(left_other), grad_other)
        return part.astype(jnp.bfloat16)

    def store(self, index, mine, theirs):
        if not self.by_rows and mine.shape[1] % 128:
            self.kept[index] = (mine, theirs)
            return
        self.buffer = store_chunk(
            self.buffer, mine, theirs, self.shape, index, self.chunks, self.by_rows
        )

    def result(self):
        if self.buffer is not None:
            return self.buffer
        first = lax.axis_index("ctx") == 0
        pieces = [
            jnp.concatenate(
                [jnp.where(first, mine, theirs), jnp.where(first, theirs, mine)], axis=1
            )
            for _, (mine, theirs) in sorted(self.kept.items())
        ]
        return jnp.concatenate(pieces, axis=0).astype(jnp.float32)


def added(left, right):
    return (left.astype(jnp.float32) + right.astype(jnp.float32)).astype(left.dtype)


def body(
    tokens,
    w_query,
    w_key,
    w_value,
    gain_query,
    gain_key,
    w_out,
    gain_attn,
    w_gate,
    w_up,
    w_down,
    gain_ffn,
    cotangent,
    source_ids,
    group_weights,
):
    seq_count = lax.axis_size("seq")
    seq_place = lax.axis_index("seq")
    ctx_place = lax.axis_index("ctx")
    dp_place = lax.axis_index("dp")
    middle = jnp.logical_or(dp_place == 1, dp_place == 2)
    tok_rows = tokens.shape[0]
    half_rows = tok_rows * seq_count
    head_width = w_query.shape[1]
    hidden_width = w_gate.shape[1]
    block_rows = min(512, half_rows) if half_rows <= 512 else 256
    owners = jnp.bitwise_xor(jnp.arange(seq_count, dtype=jnp.int32), seq_place)
    row_ids = (owners[:, None] * tok_rows + jnp.arange(tok_rows, dtype=jnp.int32)[None, :]).reshape(
        half_rows
    )
    at_query = (ctx_place * half_rows + row_ids).astype(jnp.float32)
    at_key = jnp.concatenate([at_query, ((1 - ctx_place) * half_rows + row_ids).astype(jnp.float32)])
    lane = jnp.arange(HD, dtype=jnp.int32)
    inverse = ROPE_BASE ** (-((lane % (HD // 2)).astype(jnp.float32) * 2.0 / HD))
    angles = at_key[:, None] * inverse[None, :]
    cosine = jnp.cos(angles)
    sine = jnp.sin(angles) * jnp.where(lane < HD // 2, -1.0, 1.0)[None, :]
    turns = (cosine, sine, cosine, sine, at_query[:, None], at_key[None, :])

    tokens_own, tokens_other = gather_both(tokens, "seq")
    tokens_both = jnp.concatenate([tokens_own, tokens_other], axis=0)
    query_proj = jnp.dot(tokens_own, w_query, preferred_element_type=jnp.float32)
    key_proj = jnp.dot(tokens_both, w_key, preferred_element_type=jnp.float32)
    value_low = jnp.dot(tokens_both, w_value, preferred_element_type=jnp.float32).astype(
        jnp.bfloat16
    )

    def common_rows(parts):
        stacked = jnp.stack(parts).reshape(len(parts), seq_count, tok_rows)
        return jnp.take(stacked, owners, axis=1)

    def own_rows(sums):
        return jnp.take(sums, owners, axis=1).reshape(sums.shape[0], half_rows)

    sq_key = jnp.sum(key_proj * key_proj, axis=1)
    sums = own_rows(
        lax.psum(
            common_rows(
                (jnp.sum(query_proj * query_proj, axis=1), sq_key[:half_rows], sq_key[half_rows:])
            ),
            "seq",
        )
    )
    inv_query = lax.rsqrt(sums[0] / D + EPS)[:, None]
    inv_key_both = lax.rsqrt(sums[1:].reshape(2 * half_rows) / D + EPS)[:, None]
    inv_key = inv_key_both[:half_rows]
    query_low, key_low, attn_low, lse = attend(
        query_proj, key_proj, value_low, inv_query, inv_key_both, gain_query[None, :],
        gain_key[None, :], turns, block_rows,
    )

    def to_owners(partial):
        return scatter_rows(row_blocks(partial, seq_count), "seq")

    attn_proj = to_owners(jnp.dot(attn_low, w_out, preferred_element_type=jnp.float32))
    attn_halves = swap_halves(attn_low)
    inv_attn = lax.rsqrt(jnp.mean(attn_proj * attn_proj, axis=1, keepdims=True) + EPS)
    attn_unit = attn_proj * inv_attn
    hidden = tokens.astype(jnp.float32) + attn_unit * gain_attn
    hidden_own, hidden_other = gather_both(hidden.astype(jnp.bfloat16), "seq")
    gate_proj = jnp.dot(hidden_own, w_gate, preferred_element_type=jnp.float32)
    up_proj = jnp.dot(hidden_own, w_up, preferred_element_type=jnp.float32)
    gate_sig = jax.nn.sigmoid(gate_proj)
    swish = gate_proj * gate_sig
    inner_low = (swish * up_proj).astype(jnp.bfloat16)
    inner_halves = swap_halves(inner_low)
    ffn = to_owners(jnp.dot(inner_low, w_down, preferred_element_type=jnp.float32))
    inv_ffn = lax.rsqrt(jnp.mean(ffn * ffn, axis=1, keepdims=True) + EPS)
    ffn_unit = ffn * inv_ffn
    out_tokens = (hidden + ffn_unit * gain_ffn).astype(jnp.bfloat16)
    picked = jnp.sum(
        jnp.where(
            jnp.arange(group_weights.shape[0], dtype=jnp.int32) == source_ids[0], group_weights, 0.0
        )
    )
    grad_out = cotangent.astype(jnp.float32) * picked
    gain_ffn_part = jnp.sum(grad_out * ffn_unit, axis=0)
    grad_ffn_low = norm_back(ffn_unit, inv_ffn, grad_out * gain_ffn).astype(jnp.bfloat16)
    grad_ffn_own, grad_ffn_other = gather_both(grad_ffn_low, "seq")

    grads = {
        "down": Gradient("down", w_down.shape, CHUNKS, True),
        "gate": Gradient("gate", w_gate.shape, CHUNKS, False),
        "up": Gradient("up", w_up.shape, CHUNKS, False),
        "out": Gradient("out", w_out.shape, 1, True),
        "value": Gradient("value", w_value.shape, 1, False),
        "key": Gradient("key", w_key.shape, 1, False),
        "query": Gradient("query", w_query.shape, 1, False),
    }
    sides = {"down": (*inner_halves, grad_ffn_own, grad_ffn_other)}
    results = {}

    def stages():
        grad_inner = times_transpose(grad_ffn_own, w_down)
        grad_gate = (grad_inner * up_proj * gate_sig * (1.0 + gate_proj * (1.0 - gate_sig))).astype(
            jnp.bfloat16
        )
        grad_up = (grad_inner * swish).astype(jnp.bfloat16)
        grad_gate, grad_up = yield (grad_gate, grad_up)
        gate_halves = swap_halves(grad_gate)
        up_halves = swap_halves(grad_up)
        partial = times_transpose(grad_gate, w_gate) + times_transpose(grad_up, w_up)
        (partial,) = yield (partial,)
        grad_hidden = grad_out + to_owners(partial)
        (grad_hidden,) = yield (grad_hidden,)
        gain_attn_part = jnp.sum(grad_hidden * attn_unit, axis=0)
        grad_proj_low = norm_back(attn_unit, inv_attn, grad_hidden * gain_attn).astype(jnp.bfloat16)
        grad_proj_own, grad_proj_other = gather_both(grad_proj_low, "seq")
        grad_proj_own, grad_proj_other, *gate_halves = yield (
            grad_proj_own, grad_proj_other, *gate_halves
        )
        sides["gate"] = (hidden_own, hidden_other, *gate_halves)
        sides["out"] = (*attn_halves, grad_proj_own, grad_proj_other)
        grad_attn_low = times_transpose(grad_proj_own, w_out).astype(jnp.bfloat16)
        backs = attend_back(query_low, key_low, value_low, grad_attn_low, lse, turns, block_rows)
        *backs, up_own, up_other = yield (*backs, *up_halves)
        sides["up"] = (hidden_own, hidden_other, up_own, up_other)
        grad_query_norm, own_dk, own_dv, prev_dk, prev_dv = backs
        back_dk, back_dv = lax.ppermute((prev_dk, prev_dv), "ctx", [(1, 0)])
        grad_query_norm, own_dk, own_dv, back_dk, back_dv = yield (
            grad_query_norm, own_dk, own_dv, back_dk, back_dv
        )
        grad_value_low = (own_dv + back_dv.astype(jnp.float32)).astype(jnp.bfloat16)
        grad_key_norm = own_dk + back_dk.astype(jnp.float32)
        query_unit = query_proj * inv_query
        key_unit = key_proj[:half_rows] * inv_key
        gain_query_part = jnp.sum(grad_query_norm * query_unit, axis=0)
        gain_key_part = jnp.sum(grad_key_norm * key_unit, axis=0)
        query_scaled = grad_query_norm * gain_query
        key_scaled = grad_key_norm * gain_key
        dots, gain_sums = lax.psum(
            (
                common_rows(
                    (
                        jnp.sum(query_scaled * query_unit, axis=1),
                        jnp.sum(key_scaled * key_unit, axis=1),
                    )
                ),
                jnp.concatenate([gain_attn_part, gain_ffn_part]),
            ),
            "seq",
        )
        dots_query, dots_key = own_rows(dots)
        grad_query_low = (
            inv_query * (query_scaled - query_unit * (dots_query / D)[:, None])
        ).astype(jnp.bfloat16)
        grad_key_low = (inv_key * (key_scaled - key_unit * (dots_key / D)[:, None])).astype(
            jnp.bfloat16
        )
        gains = jnp.concatenate([gain_sums, gain_query_part, gain_key_part]).reshape(-1, 128)
        grad_value_low, grad_key_low, grad_query_low, gains = yield (
            grad_value_low, grad_key_low, grad_query_low, gains
        )
        value_halves = swap_halves(grad_value_low)
        key_halves = swap_halves(grad_key_low)
        query_halves = swap_halves(grad_query_low)
        gains = gains + flip(gains, "ctx", 1)
        partial = (
            times_transpose(grad_query_low, w_query)
            + times_transpose(grad_key_low, w_key)
            + times_transpose(grad_value_low, w_value)
        )
        partial, gains, *halves = yield (
            partial, gains, *value_halves, *key_halves, *query_halves
        )
        sides["value"] = (tokens_own, tokens_other, *halves[0:2])
        sides["key"] = (tokens_own, tokens_other, *halves[2:4])
        sides["query"] = (tokens_own, tokens_other, *halves[4:6])
        results["gains"] = gains
        grad_tokens = grad_hidden + to_owners(partial)
        (grad_tokens,) = yield (grad_tokens,)
        results["tokens"] = grad_tokens

    plan = [(name, index) for name in grads for index in range(grads[name].chunks)]
    count = len(plan)
    rider = count - 1
    pairs = [(0, 1), (1, 0), (2, 3), (3, 2)]
    step = STREAMS
    part, pair, total, final = {}, {}, {}, {}
    got_pair, got_across, got_half = {}, {}, {}
    main = stages()
    state = next(main)

    def rides(index):
        return (results["gains"],) if index == rider else ()

    for tick in range(count + 4 * step):
        before = tick - step
        if before in part:
            pair[before] = jax.tree.map(added, part[before], got_pair[before][1])
        if before - step in part:
            total[before - step] = jax.tree.map(added, pair[before - step], got_across[before])
        if before - 2 * step in part:
            final[before - 2 * step] = jax.tree.map(
                lambda kept, got: jnp.where(middle, kept, got),
                total[before - 2 * step],
                got_pair[before][0],
            )
        if before - 3 * step in part:
            name, index = plan[before - 3 * step]
            grads[name].store(index, final[before - 3 * step][0], got_half[before])
        if tick < count:
            name, index = plan[tick]
            part[tick] = (grads[name].part(sides[name], index),) + rides(tick)
        entering = part.get(tick)
        leaving = total.get(tick - 2 * step)
        crossing = pair.get(tick - step)
        swapping = final.get(tick - 3 * step)
        held = (entering, leaving, crossing, swapping, state)
        entering, leaving, crossing, swapping, state = lax.optimization_barrier(held)
        if entering is not None:
            part[tick] = entering
        if leaving is not None:
            total[tick - 2 * step] = leaving
        if crossing is not None:
            pair[tick - step] = crossing
        if swapping is not None:
            final[tick - 3 * step] = swapping
        arrived_out = arrived_in = None
        alike = entering is not None and leaving is not None
        if alike and [v.shape for v in entering] == [v.shape for v in leaving]:
            sent = jax.tree.map(lambda out, into: jnp.where(middle, out, into), leaving, entering)
            arrived_in = arrived_out = tuple(lax.ppermute(v, "dp", pairs) for v in sent)
        else:
            if entering is not None:
                arrived_in = tuple(lax.ppermute(v, "dp", [(0, 1), (3, 2)]) for v in entering)
            if leaving is not None:
                arrived_out = tuple(lax.ppermute(v, "dp", [(1, 0), (2, 3)]) for v in leaving)
        got_pair[tick] = (arrived_out, arrived_in)
        if crossing is not None:
            got_across[tick] = tuple(lax.ppermute(v, "dp", [(1, 2), (2, 1)]) for v in crossing)
        if swapping is not None:
            got_half[tick] = flip(swapping[0], "ctx", 1)
        try:
            state = main.send(state)
        except StopIteration:
            state = ()

    gains = final[rider][1].reshape(-1)
    grad_gain_attn = gains[:D]
    grad_gain_ffn = gains[D : 2 * D]
    grad_gain_query = gains[2 * D : 2 * D + head_width]
    grad_gain_key = gains[2 * D + head_width :]
    return (
        out_tokens,
        results["tokens"],
        grads["query"].result(),
        grads["key"].result(),
        grads["value"].result(),
        grad_gain_query,
        grad_gain_key,
        grads["out"].result(),
        grad_gain_attn,
        grads["gate"].result(),
        grads["up"].result(),
        grads["down"].result(),
        grad_gain_ffn,
    )


def solution(mesh):
    in_specs = (
        P(("dp", "ctx", "seq"), None),
        P(None, "seq"),
        P(None, "seq"),
        P(None, "seq"),
        P("seq"),
        P("seq"),
        P("seq", None),
        P(),
        P(None, "seq"),
        P(None, "seq"),
        P("seq", None),
        P(),
        P(("dp", "ctx", "seq"), None),
        P("dp"),
        P(),
    )
    out_specs = (
        P(("dp", "ctx", "seq"), None),
        P(("dp", "ctx", "seq"), None),
        P(None, "seq"),
        P(None, "seq"),
        P(None, "seq"),
        P("seq"),
        P("seq"),
        P("seq", None),
        P(),
        P(None, "seq"),
        P(None, "seq"),
        P("seq", None),
        P(),
    )
    return jax.shard_map(body, mesh=mesh, in_specs=in_specs, out_specs=out_specs, check_vma=False)
```

```python
import functools

import jax
import jax.numpy as jnp
from jax import lax
from jax.experimental import pallas as pl
from jax.experimental.pallas import tpu as pltpu
from jax.sharding import PartitionSpec as P

D = 2048
HD = 128


EPS = 1e-06
ROPE_BASE = 500000.0
NEG_FILL = -1e30
CHUNKS = 4
STREAMS = 2


def flip(value, axis, distance):
    count = lax.axis_size(axis)
    return lax.ppermute(value, axis, [(place, place ^ distance) for place in range(count)])


def distances(axis):
    count = lax.axis_size(axis)
    found = []
    step = 1
    while step < count:
        found.append(step)
        step *= 2
    return found


def gather_rows(own, axis):
    parts = {0: own}
    for distance in reversed(distances(axis)):
        parts.update({o ^ distance: flip(block, axis, distance) for o, block in parts.items()})
    return [parts[o] for o in range(len(parts))]


def gather_both(own, axis, early=None):
    swapped = flip(own, "ctx", 1)
    mine, theirs = {0: own}, {0: swapped}
    for far, distance in enumerate(reversed(distances(axis))):
        for o in list(mine):
            mine[o ^ distance] = flip(mine[o], axis, distance)
            if far == 0 and distance > 1:
                rows = own.shape[0] // 2
                theirs[o ^ distance] = jnp.concatenate(
                    [
                        flip(theirs[o][:rows], axis, distance),
                        flip(mine[o ^ distance][rows:], "ctx", 1),
                    ],
                    axis=0,
                )
            else:
                theirs[o ^ distance] = flip(theirs[o], axis, distance)
    return [mine[o] for o in range(len(mine))], [theirs[o] for o in range(len(theirs))]


def stacked(blocks):
    return jnp.concatenate(blocks, axis=0)


def scatter_rows(blocks, axis):
    parts = dict(enumerate(blocks))
    for distance in distances(axis):
        kept = {o: block for o, block in parts.items() if not o & distance}
        for o in sorted(kept, reverse=True):
            sent = parts[o ^ distance].astype(jnp.bfloat16)
            kept[o] = kept[o] + flip(sent, axis, distance).astype(jnp.float32)
        parts = kept
    return parts[0]


def row_blocks(value, count):
    rows = value.shape[0] // count
    return [lax.slice_in_dim(value, o * rows, (o + 1) * rows, axis=0) for o in range(count)]


def norm_back(unit_val, inverse, grad_unit):
    return inverse * (grad_unit - unit_val * jnp.mean(grad_unit * unit_val, axis=-1, keepdims=True))


def contract_rows(left, right):
    return lax.dot_general(
        left, right, (((0,), (0,)), ((), ())), preferred_element_type=jnp.float32
    )


def times_transpose(left, right):
    return lax.dot_general(
        left, right, (((1,), (1,)), ((), ())), preferred_element_type=jnp.float32
    )


def half_columns(value, place):
    width = value.shape[1] // 2
    return lax.dynamic_slice_in_dim(value, place * width, width, axis=1)


def swap_halves(value):
    place = lax.axis_index("ctx")
    return half_columns(value, place), flip(half_columns(value, 1 - place), "ctx", 1)


def turned(values, cosine, sine):
    return values * cosine + pltpu.roll(values, HD // 2, 1) * sine


def project_kernel(*refs, blocks, square, plain):
    rows_ref = refs[blocks + square + plain]
    outs = refs[blocks + square + plain + 1 :]
    weights = refs[blocks : blocks + square + plain]

    @pl.when(pl.program_id(0) == 0)
    def _():
        rows = refs[0].shape[0]
        for o in range(blocks):
            rows_ref[o * rows : (o + 1) * rows, :] = refs[o][...]
        for sum_ref in outs[square + plain :]:
            sum_ref[...] = jnp.zeros_like(sum_ref)

    for k in range(square + plain):
        product = jnp.dot(rows_ref[...], weights[k][...], preferred_element_type=jnp.float32)
        outs[k][...] = product.astype(outs[k].dtype)
        if k < square:
            outs[square + plain + k][...] += jnp.sum(product * product, axis=1, keepdims=True)


def project(blocks, square, plain):
    rows, depth = blocks[0].shape
    count = len(blocks)
    width = square[0].shape[1]
    wide = min(256, width)
    whole = pl.BlockSpec((count * rows, depth), lambda i: (0, 0))
    column = pl.BlockSpec((depth, wide), lambda i: (0, i))
    product = pl.BlockSpec((count * rows, wide), lambda i: (0, i))
    sums = pl.BlockSpec((count * rows, 1), lambda i: (0, 0))
    return pl.pallas_call(
        functools.partial(project_kernel, blocks=count, square=len(square), plain=len(plain)),
        grid=(width // wide,),
        in_specs=[pl.BlockSpec((rows, depth), lambda i: (0, 0))] * count
        + [column] * (len(square) + len(plain)),
        out_specs=[whole] + [product] * (len(square) + len(plain)) + [sums] * len(square),
        out_shape=[jax.ShapeDtypeStruct((count * rows, depth), jnp.bfloat16)]
        + [jax.ShapeDtypeStruct((count * rows, width), jnp.float32)] * len(square)
        + [jax.ShapeDtypeStruct((count * rows, width), jnp.bfloat16)] * len(plain)
        + [jax.ShapeDtypeStruct((count * rows, 1), jnp.float32)] * len(square),
        name="project",
    )(*blocks, *square, *plain)


def attend_kernel(
    query_ref, key_ref, key_other_ref, value_own_ref, value_other_ref,
    inv_query_ref, inv_key_ref, gain_query_ref, gain_key_ref,
    cos_query_ref, sin_query_ref, cos_key_ref, sin_key_ref, at_query_ref, at_key_ref,
    query_low_ref, key_low_ref, value_ref, mixed_ref, lse_ref,
):
    @pl.when(pl.program_id(1) == 0)
    def _():
        half = key_ref.shape[0]
        value_ref[:half] = value_own_ref[...]
        value_ref[half:] = value_other_ref[...]
        for side, ref in ((slice(0, half), key_ref), (slice(half, 2 * half), key_other_ref)):
            scaled = ref[...] * inv_key_ref[side] * gain_key_ref[...]
            key_low_ref[side] = turned(scaled, cos_key_ref[side], sin_key_ref[side]).astype(
                jnp.bfloat16
            )

    scaled = query_ref[...] * inv_query_ref[...] * gain_query_ref[...]
    query_low = turned(scaled, cos_query_ref[...], sin_query_ref[...]).astype(jnp.bfloat16)
    query_low_ref[...] = query_low
    scores = HD ** (-0.5) * times_transpose(query_low, key_low_ref[...])
    scores = jnp.where(at_key_ref[...] <= at_query_ref[...], scores, NEG_FILL)
    peak = jnp.max(scores, axis=1, keepdims=True)
    exps = jnp.exp(scores - peak)
    total = jnp.sum(exps, axis=1, keepdims=True)
    probs = (exps * (1.0 / total)).astype(jnp.bfloat16)
    mixed_ref[...] = jnp.dot(
        probs, value_ref[...], preferred_element_type=jnp.float32
    ).astype(jnp.bfloat16)
    lse_ref[0] = peak + jnp.log(total)


def attend_back_kernel(
    query_low_ref, key_low_ref, value_ref, grad_ref, lse_ref,
    cos_query_ref, sin_query_ref, cos_key_ref, sin_key_ref, at_query_ref, at_key_ref,
    grad_query_ref, grad_key_ref, grad_value_ref, prev_key_ref, prev_value_ref,
    key_sum, value_sum,
):
    scale = HD ** (-0.5)
    query_low = query_low_ref[...]
    key_low = key_low_ref[...]
    grad_low = grad_ref[...]
    scores = scale * times_transpose(query_low, key_low)
    allowed = at_key_ref[...] <= at_query_ref[...]
    probs = jnp.exp(jnp.where(allowed, scores, NEG_FILL) - lse_ref[0])
    grad_probs = times_transpose(grad_low, value_ref[...])
    delta = jnp.sum(probs * grad_probs, axis=1, keepdims=True)
    grad_scores = (probs * (grad_probs - delta)).astype(jnp.bfloat16)
    grad_query = scale * jnp.dot(grad_scores, key_low, preferred_element_type=jnp.float32)
    grad_query_ref[...] = turned(grad_query, cos_query_ref[...], -sin_query_ref[...])
    key_part = scale * contract_rows(grad_scores, query_low)
    value_part = contract_rows(probs.astype(jnp.bfloat16), grad_low)

    @pl.when(pl.program_id(1) == 0)
    def _():
        key_sum[...] = key_part
        value_sum[...] = value_part

    @pl.when(pl.program_id(1) > 0)
    def _():
        key_sum[...] += key_part
        value_sum[...] += value_part

    @pl.when(pl.program_id(1) == pl.num_programs(1) - 1)
    def _():
        half = key_sum.shape[0] // 2
        turned_back = turned(key_sum[...], cos_key_ref[...], -sin_key_ref[...])
        grad_key_ref[...] = turned_back[:half]
        prev_key_ref[...] = turned_back[half:].astype(jnp.bfloat16)
        grad_value_ref[...] = value_sum[:half]
        prev_value_ref[...] = value_sum[half:].astype(jnp.bfloat16)


def attention_specs(half_rows, key_rows, block_rows):
    spec = {
        "query": pl.BlockSpec((block_rows, HD), lambda h, i: (i, h)),
        "key": pl.BlockSpec((key_rows, HD), lambda h, i: (0, h)),
        "half": pl.BlockSpec((half_rows, HD), lambda h, i: (0, h)),
        "gain": pl.BlockSpec((1, HD), lambda h, i: (0, h)),
        "query_column": pl.BlockSpec((block_rows, 1), lambda h, i: (i, 0)),
        "key_column": pl.BlockSpec((key_rows, 1), lambda h, i: (0, 0)),
        "key_row": pl.BlockSpec((1, key_rows), lambda h, i: (0, 0)),
        "query_turn": pl.BlockSpec((block_rows, HD), lambda h, i: (i, 0)),
        "key_turn": pl.BlockSpec((key_rows, HD), lambda h, i: (0, 0)),
        "lse": pl.BlockSpec((1, block_rows, 1), lambda h, i: (h, i, 0)),
    }
    return spec


def attend(query, keys, values, inv_query, inv_key, gain_query, gain_key, turns, block_rows):
    half_rows, width = query.shape
    key_rows = 2 * half_rows
    heads = width // HD
    s = attention_specs(half_rows, key_rows, block_rows)
    return pl.pallas_call(
        attend_kernel,
        grid=(heads, half_rows // block_rows),
        in_specs=[
            s["query"], s["half"], s["half"], s["half"], s["half"],
            s["query_column"], s["key_column"], s["gain"], s["gain"],
            s["query_turn"], s["query_turn"], s["key_turn"], s["key_turn"],
            s["query_column"], s["key_row"],
        ],
        out_specs=[s["query"], s["key"], s["key"], s["query"], s["lse"]],
        out_shape=[
            jax.ShapeDtypeStruct(query.shape, jnp.bfloat16),
            jax.ShapeDtypeStruct((key_rows, width), jnp.bfloat16),
            jax.ShapeDtypeStruct((key_rows, width), jnp.bfloat16),
            jax.ShapeDtypeStruct(query.shape, jnp.bfloat16),
            jax.ShapeDtypeStruct((heads, half_rows, 1), jnp.float32),
        ],
        name="attend",
    )(query, *keys, *values, inv_query, inv_key, gain_query, gain_key, *turns)


def attend_back(query_low, key_low, value, grad, lse, turns, block_rows):
    half_rows, width = query_low.shape
    key_rows = key_low.shape[0]
    heads = width // HD
    s = attention_specs(half_rows, key_rows, block_rows)
    halves = (half_rows, width)
    return pl.pallas_call(
        attend_back_kernel,
        grid=(heads, half_rows // block_rows),
        in_specs=[
            s["query"], s["key"], s["key"], s["query"], s["lse"],
            s["query_turn"], s["query_turn"], s["key_turn"], s["key_turn"],
            s["query_column"], s["key_row"],
        ],
        out_specs=[s["query"], s["half"], s["half"], s["half"], s["half"]],
        out_shape=[
            jax.ShapeDtypeStruct(halves, jnp.float32),
            jax.ShapeDtypeStruct(halves, jnp.float32),
            jax.ShapeDtypeStruct(halves, jnp.float32),
            jax.ShapeDtypeStruct(halves, jnp.bfloat16),
            jax.ShapeDtypeStruct(halves, jnp.bfloat16),
        ],
        scratch_shapes=[
            pltpu.VMEM((key_rows, HD), jnp.float32),
            pltpu.VMEM((key_rows, HD), jnp.float32),
        ],
        name="attend_back",
    )(query_low, key_low, value, grad, lse, *turns)


def store_kernel(place_ref, mine_ref, theirs_ref, *refs):
    out_ref = refs[-1]

    @pl.when(pl.program_id(0) == 0)
    def _():
        out_ref[...] = mine_ref[...].astype(jnp.float32)

    @pl.when(pl.program_id(0) == 1)
    def _():
        out_ref[...] = theirs_ref[...].astype(jnp.float32)


def store_chunk(buffer, mine, theirs, shape, index, chunks, by_rows):
    place = lax.axis_index("ctx").astype(jnp.int32).reshape(1)
    rows, columns = mine.shape
    if by_rows:
        where_to = lambda i, place_ref: ((place_ref[0] ^ i) * chunks + index, 0)
    else:
        where_to = lambda i, place_ref: (index, place_ref[0] ^ i)
    whole = pl.BlockSpec((rows, columns), lambda i, place_ref: (0, 0))
    operands = [place, mine, theirs]
    in_specs = [whole, whole]
    aliases = {}
    if buffer is not None:
        operands.append(buffer)
        in_specs.append(pl.BlockSpec(memory_space=pl.ANY))
        aliases = {3: 0}
    return pl.pallas_call(
        store_kernel,
        grid_spec=pltpu.PrefetchScalarGridSpec(
            num_scalar_prefetch=1,
            grid=(2,),
            in_specs=in_specs,
            out_specs=pl.BlockSpec((rows, columns), where_to),
        ),
        out_shape=jax.ShapeDtypeStruct(shape, jnp.float32),
        input_output_aliases=aliases,
        name="store",
    )(*operands)


class Gradient:
    def __init__(self, name, shape, chunks, by_rows):
        self.name, self.shape, self.chunks, self.by_rows = name, shape, chunks, by_rows
        self.buffer = None
        self.kept = {}

    def part(self, sides, index):
        left_own, left_other, grad_own, grad_other = sides
        rows = left_own.shape[1] // self.chunks
        cut = functools.partial(
            lax.slice_in_dim, start_index=index * rows, limit_index=(index + 1) * rows, axis=1
        )
        part = contract_rows(cut(left_own), grad_own) + contract_rows(cut(left_other), grad_other)
        return part.astype(jnp.bfloat16)

    def store(self, index, mine, theirs):
        if not self.by_rows and mine.shape[1] % 128:
            self.kept[index] = (mine, theirs)
            return
        self.buffer = store_chunk(
            self.buffer, mine, theirs, self.shape, index, self.chunks, self.by_rows
        )

    def result(self):
        if self.buffer is not None:
            return self.buffer
        first = lax.axis_index("ctx") == 0
        pieces = [
            jnp.concatenate(
                [jnp.where(first, mine, theirs), jnp.where(first, theirs, mine)], axis=1
            )
            for _, (mine, theirs) in sorted(self.kept.items())
        ]
        return jnp.concatenate(pieces, axis=0).astype(jnp.float32)


def added(left, right):
    return (left.astype(jnp.float32) + right.astype(jnp.float32)).astype(left.dtype)


def body(
    tokens,
    w_query,
    w_key,
    w_value,
    gain_query,
    gain_key,
    w_out,
    gain_attn,
    w_gate,
    w_up,
    w_down,
    gain_ffn,
    cotangent,
    source_ids,
    group_weights,
):
    seq_count = lax.axis_size("seq")
    seq_place = lax.axis_index("seq")
    ctx_place = lax.axis_index("ctx")
    dp_place = lax.axis_index("dp")
    middle = jnp.logical_or(dp_place == 1, dp_place == 2)
    tok_rows = tokens.shape[0]
    half_rows = tok_rows * seq_count
    head_width = w_query.shape[1]
    hidden_width = w_gate.shape[1]
    block_rows = min(512, half_rows) if half_rows <= 512 else 256
    owners = jnp.bitwise_xor(jnp.arange(seq_count, dtype=jnp.int32), seq_place)
    row_ids = (owners[:, None] * tok_rows + jnp.arange(tok_rows, dtype=jnp.int32)[None, :]).reshape(
        half_rows
    )
    at_query = (ctx_place * half_rows + row_ids).astype(jnp.float32)
    at_key = jnp.concatenate([at_query, ((1 - ctx_place) * half_rows + row_ids).astype(jnp.float32)])
    lane = jnp.arange(HD, dtype=jnp.int32)
    inverse = ROPE_BASE ** (-((lane % (HD // 2)).astype(jnp.float32) * 2.0 / HD))
    angles = at_key[:, None] * inverse[None, :]
    cosine = jnp.cos(angles)
    sine = jnp.sin(angles) * jnp.where(lane < HD // 2, -1.0, 1.0)[None, :]
    turns = (cosine, sine, cosine, sine, at_query[:, None], at_key[None, :])

    own_blocks, other_blocks = gather_both(tokens, "seq")
    tokens_own, query_proj, key_proj, value_own, sq_query, sq_key = project(
        own_blocks, (w_query, w_key), (w_value,)
    )
    tokens_other, key_other, value_other, sq_key_other = project(
        other_blocks, (w_key,), (w_value,)
    )

    def common_rows(parts):
        stacked = jnp.stack(parts).reshape(len(parts), seq_count, tok_rows)
        return jnp.take(stacked, owners, axis=1)

    def own_rows(sums):
        return jnp.take(sums, owners, axis=1).reshape(sums.shape[0], half_rows)

    sums = own_rows(lax.psum(common_rows((sq_query, sq_key, sq_key_other)), "seq"))
    inv_query = lax.rsqrt(sums[0] / D + EPS)[:, None]
    inv_key_both = lax.rsqrt(sums[1:].reshape(2 * half_rows) / D + EPS)[:, None]
    inv_key = inv_key_both[:half_rows]
    query_low, key_low, value_low, attn_low, lse = attend(
        query_proj, (key_proj, key_other), (value_own, value_other), inv_query, inv_key_both, gain_query[None, :],
        gain_key[None, :], turns, block_rows,
    )

    def to_owners(partial):
        return scatter_rows(row_blocks(partial, seq_count), "seq")

    attn_halves = swap_halves(attn_low)
    attn_proj = to_owners(jnp.dot(attn_low, w_out, preferred_element_type=jnp.float32))
    attn_proj, attn_halves = lax.optimization_barrier((attn_proj, attn_halves))
    inv_attn = lax.rsqrt(jnp.mean(attn_proj * attn_proj, axis=1, keepdims=True) + EPS)
    attn_unit = attn_proj * inv_attn
    hidden = tokens.astype(jnp.float32) + attn_unit * gain_attn
    hidden_low = hidden.astype(jnp.bfloat16)
    hidden_own = stacked(gather_rows(hidden_low, "seq"))
    hidden_flip = flip(hidden_low, "ctx", 1)
    hidden_own, hidden_flip = lax.optimization_barrier((hidden_own, hidden_flip))
    hidden_rest = gather_rows(hidden_flip, "seq")
    gate_proj = jnp.dot(hidden_own, w_gate, preferred_element_type=jnp.float32)
    up_proj = jnp.dot(hidden_own, w_up, preferred_element_type=jnp.float32)
    gate_sig = jax.nn.sigmoid(gate_proj)
    swish = gate_proj * gate_sig
    inner_low = (swish * up_proj).astype(jnp.bfloat16)
    inner_low, hidden_rest = lax.optimization_barrier((inner_low, hidden_rest))
    inner_halves = swap_halves(inner_low)
    ffn = to_owners(jnp.dot(inner_low, w_down, preferred_element_type=jnp.float32))
    inv_ffn = lax.rsqrt(jnp.mean(ffn * ffn, axis=1, keepdims=True) + EPS)
    ffn_unit = ffn * inv_ffn
    out_tokens = (hidden + ffn_unit * gain_ffn).astype(jnp.bfloat16)
    picked = jnp.sum(
        jnp.where(
            jnp.arange(group_weights.shape[0], dtype=jnp.int32) == source_ids[0], group_weights, 0.0
        )
    )
    grad_out = cotangent.astype(jnp.float32) * picked
    gain_ffn_part = jnp.sum(grad_out * ffn_unit, axis=0)
    grad_ffn_low = norm_back(ffn_unit, inv_ffn, grad_out * gain_ffn).astype(jnp.bfloat16)
    grad_ffn_low, inner_halves = lax.optimization_barrier((grad_ffn_low, inner_halves))
    grad_ffn_own, grad_ffn_other = map(stacked, gather_both(grad_ffn_low, "seq"))
    hidden_other = stacked(hidden_rest)

    grads = {
        "down": Gradient("down", w_down.shape, CHUNKS, True),
        "gate": Gradient("gate", w_gate.shape, CHUNKS, False),
        "up": Gradient("up", w_up.shape, CHUNKS, False),
        "out": Gradient("out", w_out.shape, 1, True),
        "value": Gradient("value", w_value.shape, 1, False),
        "key": Gradient("key", w_key.shape, 1, False),
        "query": Gradient("query", w_query.shape, 1, False),
    }
    sides = {"down": (*inner_halves, grad_ffn_own, grad_ffn_other)}
    results = {}

    def stages():
        grad_inner = times_transpose(grad_ffn_own, w_down)
        grad_gate = (grad_inner * up_proj * gate_sig * (1.0 + gate_proj * (1.0 - gate_sig))).astype(
            jnp.bfloat16
        )
        grad_up = (grad_inner * swish).astype(jnp.bfloat16)
        grad_gate, grad_up = yield (grad_gate, grad_up)
        gate_halves = swap_halves(grad_gate)
        sides["gate"] = (hidden_own, hidden_other, *gate_halves)
        gate_share = times_transpose(grad_gate, w_gate)
        gate_share, grad_up = yield (gate_share, grad_up)
        up_halves = swap_halves(grad_up)
        sides["up"] = (hidden_own, hidden_other, *up_halves)
        partial = gate_share + times_transpose(grad_up, w_up)
        (partial,) = yield (partial,)
        grad_hidden = grad_out + to_owners(partial)
        (grad_hidden,) = yield (grad_hidden,)
        gain_attn_part = jnp.sum(grad_hidden * attn_unit, axis=0)
        grad_proj_low = norm_back(attn_unit, inv_attn, grad_hidden * gain_attn).astype(jnp.bfloat16)
        grad_proj_flip = flip(grad_proj_low, "ctx", 1)
        grad_proj_own = stacked(gather_rows(grad_proj_low, "seq"))
        grad_proj_own, grad_proj_flip = yield (grad_proj_own, grad_proj_flip)
        grad_proj_rest = gather_rows(grad_proj_flip, "seq")
        grad_attn_low = times_transpose(grad_proj_own, w_out).astype(jnp.bfloat16)
        backs = attend_back(query_low, key_low, value_low, grad_attn_low, lse, turns, block_rows)
        backs, grad_proj_rest = yield (backs, grad_proj_rest)
        sides["out"] = (*attn_halves, grad_proj_own, stacked(grad_proj_rest))
        grad_query_norm, own_dk, own_dv, prev_dk, prev_dv = backs
        back_dk, back_dv = lax.ppermute((prev_dk, prev_dv), "ctx", [(1, 0)])
        grad_query_norm, own_dk, own_dv, back_dk, back_dv = yield (
            grad_query_norm, own_dk, own_dv, back_dk, back_dv
        )
        grad_value_low = (own_dv + back_dv.astype(jnp.float32)).astype(jnp.bfloat16)
        grad_key_norm = own_dk + back_dk.astype(jnp.float32)
        query_unit = query_proj * inv_query
        key_unit = key_proj * inv_key
        gain_query_part = jnp.sum(grad_query_norm * query_unit, axis=0)
        gain_key_part = jnp.sum(grad_key_norm * key_unit, axis=0)
        query_scaled = grad_query_norm * gain_query
        key_scaled = grad_key_norm * gain_key
        dots, gain_sums = lax.psum(
            (
                common_rows(
                    (
                        jnp.sum(query_scaled * query_unit, axis=1),
                        jnp.sum(key_scaled * key_unit, axis=1),
                    )
                ),
                jnp.concatenate([gain_attn_part, gain_ffn_part]),
            ),
            "seq",
        )
        dots_query, dots_key = own_rows(dots)
        grad_query_low = (
            inv_query * (query_scaled - query_unit * (dots_query / D)[:, None])
        ).astype(jnp.bfloat16)
        grad_key_low = (inv_key * (key_scaled - key_unit * (dots_key / D)[:, None])).astype(
            jnp.bfloat16
        )
        gains = jnp.concatenate([gain_sums, gain_query_part, gain_key_part]).reshape(-1, 128)
        grad_value_low, grad_key_low, grad_query_low, gains = yield (
            grad_value_low, grad_key_low, grad_query_low, gains
        )
        value_halves = swap_halves(grad_value_low)
        key_halves = swap_halves(grad_key_low)
        query_halves = swap_halves(grad_query_low)
        sides["value"] = (tokens_own, tokens_other, *value_halves)
        sides["key"] = (tokens_own, tokens_other, *key_halves)
        sides["query"] = (tokens_own, tokens_other, *query_halves)
        gains = gains + flip(gains, "ctx", 1)
        partial = (
            times_transpose(grad_query_low, w_query)
            + times_transpose(grad_key_low, w_key)
            + times_transpose(grad_value_low, w_value)
        )
        partial, gains = yield (partial, gains)
        results["gains"] = gains
        grad_tokens = grad_hidden + to_owners(partial)
        (grad_tokens,) = yield (grad_tokens,)
        results["tokens"] = grad_tokens

    plan = [(name, index) for name in grads for index in range(grads[name].chunks)]
    count = len(plan)
    rider = count - 1
    pairs = [(0, 1), (1, 0), (2, 3), (3, 2)]
    step = STREAMS
    part, pair, total, final = {}, {}, {}, {}
    got_pair, got_across, got_half = {}, {}, {}
    main = stages()
    state = next(main)
    last_name, last_buffer = None, None

    def rides(index):
        return (results["gains"],) if index == rider else ()

    for tick in range(count + 4 * step):
        before = tick - step
        if before in part:
            pair[before] = jax.tree.map(added, part[before], got_pair[before][1])
        if before - step in part:
            total[before - step] = jax.tree.map(added, pair[before - step], got_across[before])
        if before - 2 * step in part:
            final[before - 2 * step] = jax.tree.map(
                lambda kept, got: jnp.where(middle, kept, got),
                total[before - 2 * step],
                got_pair[before][0],
            )
        stored = before - 3 * step
        arrived = got_half.get(before)
        if tick == 0:
            part[0] = (grads[plan[0][0]].part(sides[plan[0][0]], 0),)
        entering = part.get(tick)
        leaving = total.get(tick - 2 * step)
        crossing = pair.get(tick - step)
        swapping = final.get(tick - 3 * step)
        coming = sides.get(plan[tick + 1][0]) if tick + 1 < count else None
        held = (entering, leaving, crossing, swapping, state, arrived, coming, last_buffer)
        entering, leaving, crossing, swapping, state, arrived, coming, last_buffer = (
            lax.optimization_barrier(held)
        )
        if last_name:
            grads[last_name].buffer = last_buffer
        if stored in part:
            last_name, index = plan[stored]
            grads[last_name].store(index, final[stored][0], arrived)
            last_buffer = grads[last_name].buffer
        if entering is not None:
            part[tick] = entering
        if leaving is not None:
            total[tick - 2 * step] = leaving
        if crossing is not None:
            pair[tick - step] = crossing
        if swapping is not None:
            final[tick - 3 * step] = swapping
        arrived_out = arrived_in = None
        alike = entering is not None and leaving is not None
        if alike and [v.shape for v in entering] == [v.shape for v in leaving]:
            sent = jax.tree.map(lambda out, into: jnp.where(middle, out, into), leaving, entering)
            arrived_in = arrived_out = tuple(lax.ppermute(v, "dp", pairs) for v in sent)
        else:
            if entering is not None:
                arrived_in = tuple(lax.ppermute(v, "dp", [(0, 1), (3, 2)]) for v in entering)
            if leaving is not None:
                arrived_out = tuple(lax.ppermute(v, "dp", [(1, 0), (2, 3)]) for v in leaving)
        got_pair[tick] = (arrived_out, arrived_in)
        if crossing is not None:
            got_across[tick] = tuple(lax.ppermute(v, "dp", [(1, 2), (2, 1)]) for v in crossing)
        if swapping is not None:
            got_half[tick] = flip(swapping[0], "ctx", 1)
        try:
            state = main.send(state)
        except StopIteration:
            state = ()
        if tick + 1 < count:
            name, index = plan[tick + 1]
            coming = sides[name] if coming is None else coming
            part[tick + 1] = (grads[name].part(coming, index),) + rides(tick + 1)

    gains = final[rider][1].reshape(-1)
    grad_gain_attn = gains[:D]
    grad_gain_ffn = gains[D : 2 * D]
    grad_gain_query = gains[2 * D : 2 * D + head_width]
    grad_gain_key = gains[2 * D + head_width :]
    return (
        out_tokens,
        results["tokens"],
        grads["query"].result(),
        grads["key"].result(),
        grads["value"].result(),
        grad_gain_query,
        grad_gain_key,
        grads["out"].result(),
        grad_gain_attn,
        grads["gate"].result(),
        grads["up"].result(),
        grads["down"].result(),
        grad_gain_ffn,
    )


def solution(mesh):
    in_specs = (
        P(("dp", "ctx", "seq"), None),
        P(None, "seq"),
        P(None, "seq"),
        P(None, "seq"),
        P("seq"),
        P("seq"),
        P("seq", None),
        P(),
        P(None, "seq"),
        P(None, "seq"),
        P("seq", None),
        P(),
        P(("dp", "ctx", "seq"), None),
        P("dp"),
        P(),
    )
    out_specs = (
        P(("dp", "ctx", "seq"), None),
        P(("dp", "ctx", "seq"), None),
        P(None, "seq"),
        P(None, "seq"),
        P(None, "seq"),
        P("seq"),
        P("seq"),
        P("seq", None),
        P(),
        P(None, "seq"),
        P(None, "seq"),
        P("seq", None),
        P(),
    )
    return jax.shard_map(body, mesh=mesh, in_specs=in_specs, out_specs=out_specs, check_vma=False)
```

```python
import functools

import jax
import jax.numpy as jnp
from jax import lax
from jax.experimental import pallas as pl
from jax.experimental.pallas import tpu as pltpu
from jax.sharding import PartitionSpec as P

D = 2048
HD = 128


EPS = 1e-06
ROPE_BASE = 500000.0
NEG_FILL = -1e30
CHUNKS = 4


def flip(value, axis, distance):
    count = lax.axis_size(axis)
    return lax.ppermute(value, axis, [(place, place ^ distance) for place in range(count)])


def distances(axis):
    count = lax.axis_size(axis)
    found = []
    step = 1
    while step < count:
        found.append(step)
        step *= 2
    return found


def gather_rows(own, axis):
    parts = {0: own}
    for distance in reversed(distances(axis)):
        parts.update({o ^ distance: flip(block, axis, distance) for o, block in parts.items()})
    return [parts[o] for o in range(len(parts))]


def gather_both(own, axis, beside=None):
    mine, theirs = {0: own}, {0: flip(own, "ctx", 1)}
    for far, distance in enumerate(reversed(distances(axis))):
        for o in list(mine):
            mine[o ^ distance] = flip(mine[o], axis, distance)
            if far == 0 and distance > 1:
                rows = own.shape[0] // 2
                theirs[o ^ distance] = stacked(
                    [
                        flip(theirs[o][:rows], axis, distance),
                        flip(mine[o ^ distance][rows:], "ctx", 1),
                    ]
                )
                held = (mine[o ^ distance], beside)
                mine[o ^ distance], beside = lax.optimization_barrier(held)
            else:
                theirs[o ^ distance] = flip(theirs[o], axis, distance)
    blocks = range(len(mine))
    return [mine[o] for o in blocks], [theirs[o] for o in blocks], beside


def gather_beside(own, axis, beside):
    parts = {0: own}
    for distance in reversed(distances(axis)):
        parts.update({o ^ distance: flip(block, axis, distance) for o, block in parts.items()})
        if len(parts) == 2:
            held = (parts[distance], beside)
            parts[distance], beside = lax.optimization_barrier(held)
    return [parts[o] for o in range(len(parts))], beside


def stacked(blocks):
    return jnp.concatenate(blocks, axis=0)


def scatter_rows(blocks, axis):
    parts = dict(enumerate(blocks))
    for distance in distances(axis):
        kept = {o: block for o, block in parts.items() if not o & distance}
        for o in sorted(kept, reverse=True):
            sent = parts[o ^ distance].astype(jnp.bfloat16)
            kept[o] = kept[o] + flip(sent, axis, distance).astype(jnp.float32)
        parts = kept
    return parts[0]


def row_blocks(value, count):
    rows = value.shape[0] // count
    return [lax.slice_in_dim(value, o * rows, (o + 1) * rows, axis=0) for o in range(count)]


def norm_back(unit_val, inverse, grad_unit):
    return inverse * (grad_unit - unit_val * jnp.mean(grad_unit * unit_val, axis=-1, keepdims=True))


def contract_rows(left, right):
    return lax.dot_general(
        left, right, (((0,), (0,)), ((), ())), preferred_element_type=jnp.float32
    )


def times_transpose(left, right):
    return lax.dot_general(
        left, right, (((1,), (1,)), ((), ())), preferred_element_type=jnp.float32
    )


def half_columns(value, place):
    width = value.shape[1] // 2
    return lax.dynamic_slice_in_dim(value, place * width, width, axis=1)


def swap_halves(value):
    place = lax.axis_index("ctx")
    return half_columns(value, place), flip(half_columns(value, 1 - place), "ctx", 1)


def turned(values, cosine, sine):
    return values * cosine + pltpu.roll(values, HD // 2, 1) * sine


def project_kernel(*refs, blocks, square, plain):
    rows_ref = refs[blocks + square + plain]
    outs = refs[blocks + square + plain + 1 :]
    weights = refs[blocks : blocks + square + plain]

    @pl.when(pl.program_id(0) == 0)
    def _():
        rows = refs[0].shape[0]
        for o in range(blocks):
            rows_ref[o * rows : (o + 1) * rows, :] = refs[o][...]
        for sum_ref in outs[square + plain :]:
            sum_ref[...] = jnp.zeros_like(sum_ref)

    for k in range(square + plain):
        product = jnp.dot(rows_ref[...], weights[k][...], preferred_element_type=jnp.float32)
        outs[k][...] = product.astype(outs[k].dtype)
        if k < square:
            outs[square + plain + k][...] += jnp.sum(product * product, axis=1, keepdims=True)


def project(blocks, square, plain):
    rows, depth = blocks[0].shape
    count = len(blocks)
    width = square[0].shape[1]
    wide = min(256, width)
    whole = pl.BlockSpec((count * rows, depth), lambda i: (0, 0))
    column = pl.BlockSpec((depth, wide), lambda i: (0, i))
    product = pl.BlockSpec((count * rows, wide), lambda i: (0, i))
    sums = pl.BlockSpec((count * rows, 1), lambda i: (0, 0))
    return pl.pallas_call(
        functools.partial(project_kernel, blocks=count, square=len(square), plain=len(plain)),
        grid=(width // wide,),
        in_specs=[pl.BlockSpec((rows, depth), lambda i: (0, 0))] * count
        + [column] * (len(square) + len(plain)),
        out_specs=[whole] + [product] * (len(square) + len(plain)) + [sums] * len(square),
        out_shape=[jax.ShapeDtypeStruct((count * rows, depth), jnp.bfloat16)]
        + [jax.ShapeDtypeStruct((count * rows, width), jnp.float32)] * len(square)
        + [jax.ShapeDtypeStruct((count * rows, width), jnp.bfloat16)] * len(plain)
        + [jax.ShapeDtypeStruct((count * rows, 1), jnp.float32)] * len(square),
        name="project",
    )(*blocks, *square, *plain)


def attend_kernel(
    query_ref, key_ref, key_other_ref, value_own_ref, value_other_ref,
    inv_query_ref, inv_key_ref, gain_query_ref, gain_key_ref,
    cos_query_ref, sin_query_ref, cos_key_ref, sin_key_ref, at_query_ref, at_key_ref,
    query_low_ref, key_low_ref, value_ref, mixed_ref, lse_ref,
):
    @pl.when(pl.program_id(1) == 0)
    def _():
        half = key_ref.shape[0]
        value_ref[:half] = value_own_ref[...]
        value_ref[half:] = value_other_ref[...]
        for side, ref in ((slice(0, half), key_ref), (slice(half, 2 * half), key_other_ref)):
            scaled = ref[...] * inv_key_ref[side] * gain_key_ref[...]
            key_low_ref[side] = turned(scaled, cos_key_ref[side], sin_key_ref[side]).astype(
                jnp.bfloat16
            )

    scaled = query_ref[...] * inv_query_ref[...] * gain_query_ref[...]
    query_low = turned(scaled, cos_query_ref[...], sin_query_ref[...]).astype(jnp.bfloat16)
    query_low_ref[...] = query_low
    scores = HD ** (-0.5) * times_transpose(query_low, key_low_ref[...])
    scores = jnp.where(at_key_ref[...] <= at_query_ref[...], scores, NEG_FILL)
    peak = jnp.max(scores, axis=1, keepdims=True)
    exps = jnp.exp(scores - peak)
    total = jnp.sum(exps, axis=1, keepdims=True)
    probs = (exps * (1.0 / total)).astype(jnp.bfloat16)
    mixed_ref[...] = jnp.dot(
        probs, value_ref[...], preferred_element_type=jnp.float32
    ).astype(jnp.bfloat16)
    lse_ref[0] = peak + jnp.log(total)


def attend_back_kernel(
    query_low_ref, key_low_ref, value_ref, grad_ref, lse_ref,
    cos_query_ref, sin_query_ref, cos_key_ref, sin_key_ref, at_query_ref, at_key_ref,
    grad_query_ref, grad_key_ref, grad_value_ref, prev_key_ref, prev_value_ref,
    key_sum, value_sum,
):
    scale = HD ** (-0.5)
    query_low = query_low_ref[...]
    key_low = key_low_ref[...]
    grad_low = grad_ref[...]
    scores = scale * times_transpose(query_low, key_low)
    allowed = at_key_ref[...] <= at_query_ref[...]
    probs = jnp.exp(jnp.where(allowed, scores, NEG_FILL) - lse_ref[0])
    grad_probs = times_transpose(grad_low, value_ref[...])
    delta = jnp.sum(probs * grad_probs, axis=1, keepdims=True)
    grad_scores = (probs * (grad_probs - delta)).astype(jnp.bfloat16)
    grad_query = scale * jnp.dot(grad_scores, key_low, preferred_element_type=jnp.float32)
    grad_query_ref[...] = turned(grad_query, cos_query_ref[...], -sin_query_ref[...])
    key_part = scale * contract_rows(grad_scores, query_low)
    value_part = contract_rows(probs.astype(jnp.bfloat16), grad_low)

    @pl.when(pl.program_id(1) == 0)
    def _():
        key_sum[...] = key_part
        value_sum[...] = value_part

    @pl.when(pl.program_id(1) > 0)
    def _():
        key_sum[...] += key_part
        value_sum[...] += value_part

    @pl.when(pl.program_id(1) == pl.num_programs(1) - 1)
    def _():
        half = key_sum.shape[0] // 2
        turned_back = turned(key_sum[...], cos_key_ref[...], -sin_key_ref[...])
        grad_key_ref[...] = turned_back[:half]
        prev_key_ref[...] = turned_back[half:].astype(jnp.bfloat16)
        grad_value_ref[...] = value_sum[:half]
        prev_value_ref[...] = value_sum[half:].astype(jnp.bfloat16)


def attention_specs(half_rows, key_rows, block_rows):
    spec = {
        "query": pl.BlockSpec((block_rows, HD), lambda h, i: (i, h)),
        "key": pl.BlockSpec((key_rows, HD), lambda h, i: (0, h)),
        "half": pl.BlockSpec((half_rows, HD), lambda h, i: (0, h)),
        "gain": pl.BlockSpec((1, HD), lambda h, i: (0, h)),
        "query_column": pl.BlockSpec((block_rows, 1), lambda h, i: (i, 0)),
        "key_column": pl.BlockSpec((key_rows, 1), lambda h, i: (0, 0)),
        "key_row": pl.BlockSpec((1, key_rows), lambda h, i: (0, 0)),
        "query_turn": pl.BlockSpec((block_rows, HD), lambda h, i: (i, 0)),
        "key_turn": pl.BlockSpec((key_rows, HD), lambda h, i: (0, 0)),
        "lse": pl.BlockSpec((1, block_rows, 1), lambda h, i: (h, i, 0)),
    }
    return spec


def attend(query, keys, values, inv_query, inv_key, gain_query, gain_key, turns, block_rows):
    half_rows, width = query.shape
    key_rows = 2 * half_rows
    heads = width // HD
    s = attention_specs(half_rows, key_rows, block_rows)
    return pl.pallas_call(
        attend_kernel,
        grid=(heads, half_rows // block_rows),
        in_specs=[
            s["query"], s["half"], s["half"], s["half"], s["half"],
            s["query_column"], s["key_column"], s["gain"], s["gain"],
            s["query_turn"], s["query_turn"], s["key_turn"], s["key_turn"],
            s["query_column"], s["key_row"],
        ],
        out_specs=[s["query"], s["key"], s["key"], s["query"], s["lse"]],
        out_shape=[
            jax.ShapeDtypeStruct(query.shape, jnp.bfloat16),
            jax.ShapeDtypeStruct((key_rows, width), jnp.bfloat16),
            jax.ShapeDtypeStruct((key_rows, width), jnp.bfloat16),
            jax.ShapeDtypeStruct(query.shape, jnp.bfloat16),
            jax.ShapeDtypeStruct((heads, half_rows, 1), jnp.float32),
        ],
        name="attend",
    )(query, *keys, *values, inv_query, inv_key, gain_query, gain_key, *turns)


def attend_back(query_low, key_low, value, grad, lse, turns, block_rows):
    half_rows, width = query_low.shape
    key_rows = key_low.shape[0]
    heads = width // HD
    s = attention_specs(half_rows, key_rows, block_rows)
    halves = (half_rows, width)
    return pl.pallas_call(
        attend_back_kernel,
        grid=(heads, half_rows // block_rows),
        in_specs=[
            s["query"], s["key"], s["key"], s["query"], s["lse"],
            s["query_turn"], s["query_turn"], s["key_turn"], s["key_turn"],
            s["query_column"], s["key_row"],
        ],
        out_specs=[s["query"], s["half"], s["half"], s["half"], s["half"]],
        out_shape=[
            jax.ShapeDtypeStruct(halves, jnp.float32),
            jax.ShapeDtypeStruct(halves, jnp.float32),
            jax.ShapeDtypeStruct(halves, jnp.float32),
            jax.ShapeDtypeStruct(halves, jnp.bfloat16),
            jax.ShapeDtypeStruct(halves, jnp.bfloat16),
        ],
        scratch_shapes=[
            pltpu.VMEM((key_rows, HD), jnp.float32),
            pltpu.VMEM((key_rows, HD), jnp.float32),
        ],
        name="attend_back",
    )(query_low, key_low, value, grad, lse, *turns)


def store_kernel(place_ref, mine_ref, theirs_ref, *refs):
    out_ref = refs[-1]

    @pl.when(pl.program_id(0) == 0)
    def _():
        out_ref[...] = mine_ref[...].astype(jnp.float32)

    @pl.when(pl.program_id(0) == 1)
    def _():
        out_ref[...] = theirs_ref[...].astype(jnp.float32)


def store_chunk(buffer, mine, theirs, shape, index, chunks, by_rows):
    place = lax.axis_index("ctx").astype(jnp.int32).reshape(1)
    rows, columns = mine.shape
    if by_rows:
        where_to = lambda i, place_ref: ((place_ref[0] ^ i) * chunks + index, 0)
    else:
        where_to = lambda i, place_ref: (index, place_ref[0] ^ i)
    whole = pl.BlockSpec((rows, columns), lambda i, place_ref: (0, 0))
    operands = [place, mine, theirs]
    in_specs = [whole, whole]
    aliases = {}
    if buffer is not None:
        operands.append(buffer)
        in_specs.append(pl.BlockSpec(memory_space=pl.ANY))
        aliases = {3: 0}
    return pl.pallas_call(
        store_kernel,
        grid_spec=pltpu.PrefetchScalarGridSpec(
            num_scalar_prefetch=1,
            grid=(2,),
            in_specs=in_specs,
            out_specs=pl.BlockSpec((rows, columns), where_to),
        ),
        out_shape=jax.ShapeDtypeStruct(shape, jnp.float32),
        input_output_aliases=aliases,
        name="store",
    )(*operands)


class Gradient:
    def __init__(self, name, shape, chunks, by_rows):
        self.name, self.shape, self.chunks, self.by_rows = name, shape, chunks, by_rows
        self.buffer = None
        self.kept = {}

    def part(self, sides, index):
        left_own, left_other, grad_own, grad_other = sides
        rows = left_own.shape[1] // self.chunks
        cut = functools.partial(
            lax.slice_in_dim, start_index=index * rows, limit_index=(index + 1) * rows, axis=1
        )
        part = contract_rows(cut(left_own), grad_own) + contract_rows(cut(left_other), grad_other)
        return part.astype(jnp.bfloat16)

    def store(self, index, mine, theirs):
        if not self.by_rows and mine.shape[1] % 128:
            self.kept[index] = (mine, theirs)
            return
        self.buffer = store_chunk(
            self.buffer, mine, theirs, self.shape, index, self.chunks, self.by_rows
        )

    def result(self):
        if self.buffer is not None:
            return self.buffer
        first = lax.axis_index("ctx") == 0
        pieces = [
            jnp.concatenate(
                [jnp.where(first, mine, theirs), jnp.where(first, theirs, mine)], axis=1
            )
            for _, (mine, theirs) in sorted(self.kept.items())
        ]
        return jnp.concatenate(pieces, axis=0).astype(jnp.float32)


def added(left, right):
    return (left.astype(jnp.float32) + right.astype(jnp.float32)).astype(left.dtype)


def body(
    tokens,
    w_query,
    w_key,
    w_value,
    gain_query,
    gain_key,
    w_out,
    gain_attn,
    w_gate,
    w_up,
    w_down,
    gain_ffn,
    cotangent,
    source_ids,
    group_weights,
):
    seq_count = lax.axis_size("seq")
    seq_place = lax.axis_index("seq")
    ctx_place = lax.axis_index("ctx")
    dp_place = lax.axis_index("dp")
    middle = jnp.logical_or(dp_place == 1, dp_place == 2)
    tok_rows = tokens.shape[0]
    half_rows = tok_rows * seq_count
    head_width = w_query.shape[1]
    hidden_width = w_gate.shape[1]
    block_rows = min(512, half_rows) if half_rows <= 512 else 256
    owners = jnp.bitwise_xor(jnp.arange(seq_count, dtype=jnp.int32), seq_place)
    row_ids = (owners[:, None] * tok_rows + jnp.arange(tok_rows, dtype=jnp.int32)[None, :]).reshape(
        half_rows
    )
    at_query = (ctx_place * half_rows + row_ids).astype(jnp.float32)
    at_key = jnp.concatenate([at_query, ((1 - ctx_place) * half_rows + row_ids).astype(jnp.float32)])
    lane = jnp.arange(HD, dtype=jnp.int32)
    inverse = ROPE_BASE ** (-((lane % (HD // 2)).astype(jnp.float32) * 2.0 / HD))
    angles = at_key[:, None] * inverse[None, :]
    cosine = jnp.cos(angles)
    sine = jnp.sin(angles) * jnp.where(lane < HD // 2, -1.0, 1.0)[None, :]
    turns = (cosine, sine, cosine, sine, at_query[:, None], at_key[None, :])

    own_blocks, other_blocks, turns = gather_both(tokens, "seq", turns)
    tokens_own, query_proj, key_proj, value_own, sq_query, sq_key = project(
        own_blocks, (w_query, w_key), (w_value,)
    )
    tokens_other, key_other, value_other, sq_key_other = project(
        other_blocks, (w_key,), (w_value,)
    )

    def common_rows(parts):
        stacked = jnp.stack(parts).reshape(len(parts), seq_count, tok_rows)
        return jnp.take(stacked, owners, axis=1)

    def own_rows(sums):
        return jnp.take(sums, owners, axis=1).reshape(sums.shape[0], half_rows)

    sums = own_rows(lax.psum(common_rows((sq_query, sq_key, sq_key_other)), "seq"))
    inv_query = lax.rsqrt(sums[0] / D + EPS)[:, None]
    inv_key_both = lax.rsqrt(sums[1:].reshape(2 * half_rows) / D + EPS)[:, None]
    inv_key = inv_key_both[:half_rows]
    query_low, key_low, value_low, attn_low, lse = attend(
        query_proj, (key_proj, key_other), (value_own, value_other), inv_query, inv_key_both, gain_query[None, :],
        gain_key[None, :], turns, block_rows,
    )

    def to_owners(partial):
        return scatter_rows(row_blocks(partial, seq_count), "seq")

    attn_halves = swap_halves(attn_low)
    attn_proj = to_owners(jnp.dot(attn_low, w_out, preferred_element_type=jnp.float32))
    attn_proj, attn_halves = lax.optimization_barrier((attn_proj, attn_halves))
    inv_attn = lax.rsqrt(jnp.mean(attn_proj * attn_proj, axis=1, keepdims=True) + EPS)
    attn_unit = attn_proj * inv_attn
    hidden = tokens.astype(jnp.float32) + attn_unit * gain_attn
    hidden_low = hidden.astype(jnp.bfloat16)
    hidden_flip = flip(hidden_low, "ctx", 1)
    hidden_blocks, hidden_flip = gather_beside(hidden_low, "seq", hidden_flip)
    hidden_own = stacked(hidden_blocks)
    hidden_rest = gather_rows(hidden_flip, "seq")
    gate_proj = jnp.dot(hidden_own, w_gate, preferred_element_type=jnp.float32)
    up_proj = jnp.dot(hidden_own, w_up, preferred_element_type=jnp.float32)
    gate_sig = jax.nn.sigmoid(gate_proj)
    swish = gate_proj * gate_sig
    inner_low = (swish * up_proj).astype(jnp.bfloat16)
    inner_low, hidden_rest = lax.optimization_barrier((inner_low, hidden_rest))
    inner_halves = swap_halves(inner_low)
    ffn = to_owners(jnp.dot(inner_low, w_down, preferred_element_type=jnp.float32))
    ffn, inner_halves = lax.optimization_barrier((ffn, inner_halves))
    inv_ffn = lax.rsqrt(jnp.mean(ffn * ffn, axis=1, keepdims=True) + EPS)
    ffn_unit = ffn * inv_ffn
    out_tokens = (hidden + ffn_unit * gain_ffn).astype(jnp.bfloat16)
    picked = jnp.sum(
        jnp.where(
            jnp.arange(group_weights.shape[0], dtype=jnp.int32) == source_ids[0], group_weights, 0.0
        )
    )
    grad_out = cotangent.astype(jnp.float32) * picked
    gain_ffn_part = jnp.sum(grad_out * ffn_unit, axis=0)
    grad_ffn_low = norm_back(ffn_unit, inv_ffn, grad_out * gain_ffn).astype(jnp.bfloat16)
    grad_ffn_own, grad_ffn_other, _ = gather_both(grad_ffn_low, "seq")
    grad_ffn_own, grad_ffn_other = stacked(grad_ffn_own), stacked(grad_ffn_other)
    hidden_other = stacked(hidden_rest)

    grads = {
        "down": Gradient("down", w_down.shape, CHUNKS, True),
        "gate": Gradient("gate", w_gate.shape, CHUNKS, False),
        "up": Gradient("up", w_up.shape, CHUNKS, False),
        "out": Gradient("out", w_out.shape, 1, True),
        "value": Gradient("value", w_value.shape, 1, False),
        "key": Gradient("key", w_key.shape, 1, False),
        "query": Gradient("query", w_query.shape, 1, False),
    }
    sides = {"down": (*inner_halves, grad_ffn_own, grad_ffn_other)}
    results = {}

    def stages():
        (grad_ffn,) = yield (grad_ffn_own,)
        grad_inner = times_transpose(grad_ffn, w_down)
        grad_gate = (grad_inner * up_proj * gate_sig * (1.0 + gate_proj * (1.0 - gate_sig))).astype(
            jnp.bfloat16
        )
        grad_up = (grad_inner * swish).astype(jnp.bfloat16)
        grad_gate, grad_up = yield (grad_gate, grad_up)
        gate_halves = swap_halves(grad_gate)
        sides["gate"] = (hidden_own, hidden_other, *gate_halves)
        gate_share = times_transpose(grad_gate, w_gate)
        gate_share, grad_up = yield (gate_share, grad_up)
        up_halves = swap_halves(grad_up)
        sides["up"] = (hidden_own, hidden_other, *up_halves)
        partial = gate_share + times_transpose(grad_up, w_up)
        (partial,) = yield (partial,)
        grad_hidden = grad_out + to_owners(partial)
        (grad_hidden,) = yield (grad_hidden,)
        gain_attn_part = jnp.sum(grad_hidden * attn_unit, axis=0)
        grad_proj_low = norm_back(attn_unit, inv_attn, grad_hidden * gain_attn).astype(jnp.bfloat16)
        grad_proj_flip = flip(grad_proj_low, "ctx", 1)
        grad_proj_own = stacked(gather_rows(grad_proj_low, "seq"))
        grad_proj_own, grad_proj_flip = yield (grad_proj_own, grad_proj_flip)
        grad_proj_rest = gather_rows(grad_proj_flip, "seq")
        grad_attn_low = times_transpose(grad_proj_own, w_out).astype(jnp.bfloat16)
        backs = attend_back(query_low, key_low, value_low, grad_attn_low, lse, turns, block_rows)
        backs, grad_proj_rest = yield (backs, grad_proj_rest)
        sides["out"] = (*attn_halves, grad_proj_own, stacked(grad_proj_rest))
        grad_query_norm, own_dk, own_dv, prev_dk, prev_dv = backs
        back_dk, back_dv = lax.ppermute((prev_dk, prev_dv), "ctx", [(1, 0)])
        grad_query_norm, own_dk, own_dv, back_dk, back_dv = yield (
            grad_query_norm, own_dk, own_dv, back_dk, back_dv
        )
        grad_value_low = (own_dv + back_dv.astype(jnp.float32)).astype(jnp.bfloat16)
        grad_key_norm = own_dk + back_dk.astype(jnp.float32)
        query_unit = query_proj * inv_query
        key_unit = key_proj * inv_key
        gain_query_part = jnp.sum(grad_query_norm * query_unit, axis=0)
        gain_key_part = jnp.sum(grad_key_norm * key_unit, axis=0)
        query_scaled = grad_query_norm * gain_query
        key_scaled = grad_key_norm * gain_key
        dots, gain_sums = lax.psum(
            (
                common_rows(
                    (
                        jnp.sum(query_scaled * query_unit, axis=1),
                        jnp.sum(key_scaled * key_unit, axis=1),
                    )
                ),
                jnp.concatenate([gain_attn_part, gain_ffn_part]),
            ),
            "seq",
        )
        dots_query, dots_key = own_rows(dots)
        grad_query_low = (
            inv_query * (query_scaled - query_unit * (dots_query / D)[:, None])
        ).astype(jnp.bfloat16)
        grad_key_low = (inv_key * (key_scaled - key_unit * (dots_key / D)[:, None])).astype(
            jnp.bfloat16
        )
        gains = jnp.concatenate([gain_sums, gain_query_part, gain_key_part]).reshape(-1, 128)
        grad_value_low, grad_key_low, grad_query_low, gains = yield (
            grad_value_low, grad_key_low, grad_query_low, gains
        )
        value_halves = swap_halves(grad_value_low)
        key_halves = swap_halves(grad_key_low)
        query_halves = swap_halves(grad_query_low)
        sides["value"] = (tokens_own, tokens_other, *value_halves)
        sides["key"] = (tokens_own, tokens_other, *key_halves)
        sides["query"] = (tokens_own, tokens_other, *query_halves)
        gains = gains + flip(gains, "ctx", 1)
        partial = (
            times_transpose(grad_query_low, w_query)
            + times_transpose(grad_key_low, w_key)
            + times_transpose(grad_value_low, w_value)
        )
        partial, gains = yield (partial, gains)
        results["gains"] = gains
        grad_tokens = grad_hidden + to_owners(partial)
        (grad_tokens,) = yield (grad_tokens,)
        results["tokens"] = grad_tokens

    plan = [(name, index) for name in grads for index in range(grads[name].chunks)]
    count = len(plan)
    rider = count - 1
    across_at = {chunk + (2 if chunk else 1): chunk for chunk in range(count)}
    out_at = {tick + 1: chunk for tick, chunk in across_at.items()}
    half_at = {tick + 1: chunk for tick, chunk in out_at.items()}
    store_at = {tick + 1: chunk for tick, chunk in half_at.items()}
    part, pair, total, final = {}, {}, {}, {}
    got_in, got_across, got_out, got_half = {}, {}, {}, {}
    main = stages()
    state = next(main)
    last_name, last_buffer = None, None
    token = picked
    part[0] = (grads[plan[0][0]].part(sides[plan[0][0]], 0),)

    def send(values, axis, pairs):
        return tuple(lax.ppermute(value, axis, pairs) for value in values)

    for tick in range(max(store_at) + 1):
        entering = part.get(tick)
        chunk = across_at.get(tick)
        crossing = None
        if chunk is not None:
            crossing = jax.tree.map(added, part[chunk], got_in[chunk])
        coming = sides.get(plan[tick + 1][0]) if tick + 1 < count else None
        held = (entering, crossing, state, coming, last_buffer, token)
        entering, crossing, state, coming, last_buffer, token = lax.optimization_barrier(held)
        if last_name:
            grads[last_name].buffer = last_buffer
        if crossing is not None:
            pair[chunk] = crossing
            got_across[chunk] = send(crossing, "dp", [(1, 2), (2, 1)])
        if entering is not None:
            part[tick] = entering
            got_in[tick] = send(entering, "dp", [(0, 1), (3, 2)])
        if tick in out_at:
            chunk = out_at[tick]
            leaving = jax.tree.map(added, pair[chunk], got_across[chunk])
            total[chunk], token = lax.optimization_barrier((leaving, token))
            got_out[chunk] = send(total[chunk], "dp", [(1, 0), (2, 3)])
        if tick in half_at:
            chunk = half_at[tick]
            swapping = jax.tree.map(
                lambda kept, got: jnp.where(middle, kept, got), total[chunk], got_out[chunk]
            )
            final[chunk], token = lax.optimization_barrier((swapping, token))
            got_half[chunk] = flip(final[chunk][0], "ctx", 1)
        if tick in store_at:
            chunk = store_at[tick]
            theirs, token = lax.optimization_barrier((got_half[chunk], token))
            last_name, index = plan[chunk]
            grads[last_name].store(index, final[chunk][0], theirs)
            last_buffer = grads[last_name].buffer
        try:
            state = main.send(state)
        except StopIteration:
            state = ()
        if tick + 1 < count:
            name, index = plan[tick + 1]
            coming = sides[name] if coming is None else coming
            rides = (results["gains"],) if tick + 1 == rider else ()
            part[tick + 1] = (grads[name].part(coming, index),) + rides

    gains = final[rider][1].reshape(-1)
    grad_gain_attn = gains[:D]
    grad_gain_ffn = gains[D : 2 * D]
    grad_gain_query = gains[2 * D : 2 * D + head_width]
    grad_gain_key = gains[2 * D + head_width :]
    return (
        out_tokens,
        results["tokens"],
        grads["query"].result(),
        grads["key"].result(),
        grads["value"].result(),
        grad_gain_query,
        grad_gain_key,
        grads["out"].result(),
        grad_gain_attn,
        grads["gate"].result(),
        grads["up"].result(),
        grads["down"].result(),
        grad_gain_ffn,
    )


def solution(mesh):
    in_specs = (
        P(("dp", "ctx", "seq"), None),
        P(None, "seq"),
        P(None, "seq"),
        P(None, "seq"),
        P("seq"),
        P("seq"),
        P("seq", None),
        P(),
        P(None, "seq"),
        P(None, "seq"),
        P("seq", None),
        P(),
        P(("dp", "ctx", "seq"), None),
        P("dp"),
        P(),
    )
    out_specs = (
        P(("dp", "ctx", "seq"), None),
        P(("dp", "ctx", "seq"), None),
        P(None, "seq"),
        P(None, "seq"),
        P(None, "seq"),
        P("seq"),
        P("seq"),
        P("seq", None),
        P(),
        P(None, "seq"),
        P(None, "seq"),
        P("seq", None),
        P(),
    )
    return jax.shard_map(body, mesh=mesh, in_specs=in_specs, out_specs=out_specs, check_vma=False)
```

```python
import functools

import jax
import jax.numpy as jnp
from jax import lax
from jax.experimental import pallas as pl
from jax.experimental.pallas import tpu as pltpu
from jax.sharding import PartitionSpec as P

D = 2048
HD = 128


EPS = 1e-06
ROPE_BASE = 500000.0
NEG_FILL = -1e30
PAIRS = [(0, 1), (1, 0), (2, 3), (3, 2)]
INWARD = [(0, 1), (3, 2)]
OUTWARD = [(1, 0), (2, 3)]
ACROSS = [(1, 2), (2, 1), (0, 0), (3, 3)]


def flip(value, axis, distance):
    count = lax.axis_size(axis)
    return lax.ppermute(value, axis, [(place, place ^ distance) for place in range(count)])


def distances(axis):
    count = lax.axis_size(axis)
    found = []
    step = 1
    while step < count:
        found.append(step)
        step *= 2
    return found


def gather_rows(own, axis):
    parts = {0: own}
    for distance in reversed(distances(axis)):
        parts.update({o ^ distance: flip(block, axis, distance) for o, block in parts.items()})
    return [parts[o] for o in range(len(parts))]


def gather_both(own, axis, beside=None):
    mine, theirs = {0: own}, {0: flip(own, "ctx", 1)}
    for far, distance in enumerate(reversed(distances(axis))):
        for o in list(mine):
            mine[o ^ distance] = flip(mine[o], axis, distance)
            if far == 0 and distance > 1:
                rows = own.shape[0] // 2
                theirs[o ^ distance] = stacked(
                    [
                        flip(theirs[o][:rows], axis, distance),
                        flip(mine[o ^ distance][rows:], "ctx", 1),
                    ]
                )
                held = (mine[o ^ distance], beside)
                mine[o ^ distance], beside = lax.optimization_barrier(held)
            else:
                theirs[o ^ distance] = flip(theirs[o], axis, distance)
    blocks = range(len(mine))
    return [mine[o] for o in blocks], [theirs[o] for o in blocks], beside


def gather_beside(own, axis, beside):
    parts = {0: own}
    for distance in reversed(distances(axis)):
        parts.update({o ^ distance: flip(block, axis, distance) for o, block in parts.items()})
        if len(parts) == 2:
            held = (parts[distance], beside)
            parts[distance], beside = lax.optimization_barrier(held)
    return [parts[o] for o in range(len(parts))], beside


def stacked(blocks):
    return jnp.concatenate(blocks, axis=0)


def scatter_rows(blocks, axis):
    parts = dict(enumerate(blocks))
    for distance in distances(axis):
        kept = {o: block for o, block in parts.items() if not o & distance}
        for o in sorted(kept, reverse=True):
            sent = parts[o ^ distance].astype(jnp.bfloat16)
            kept[o] = kept[o] + flip(sent, axis, distance).astype(jnp.float32)
        parts = kept
    return parts[0]


def row_blocks(value, count):
    rows = value.shape[0] // count
    return [lax.slice_in_dim(value, o * rows, (o + 1) * rows, axis=0) for o in range(count)]


def norm_back(unit_val, inverse, grad_unit):
    return inverse * (grad_unit - unit_val * jnp.mean(grad_unit * unit_val, axis=-1, keepdims=True))


def contract_rows(left, right):
    return lax.dot_general(
        left, right, (((0,), (0,)), ((), ())), preferred_element_type=jnp.float32
    )


def times_transpose(left, right):
    return lax.dot_general(
        left, right, (((1,), (1,)), ((), ())), preferred_element_type=jnp.float32
    )


def half_columns(value, place):
    width = value.shape[1] // 2
    return lax.dynamic_slice_in_dim(value, place * width, width, axis=1)


def both_halves(value):
    place = lax.axis_index("ctx")
    return half_columns(value, place), flip(half_columns(value, 1 - place), "ctx", 1)


def turned(values, cosine, sine):
    return values * cosine + pltpu.roll(values, HD // 2, 1) * sine


def project_kernel(*refs, blocks, square, plain):
    rows_ref = refs[blocks + square + plain]
    outs = refs[blocks + square + plain + 1 :]
    weights = refs[blocks : blocks + square + plain]

    @pl.when(pl.program_id(0) == 0)
    def _():
        rows = refs[0].shape[0]
        for o in range(blocks):
            rows_ref[o * rows : (o + 1) * rows, :] = refs[o][...]
        for sum_ref in outs[square + plain :]:
            sum_ref[...] = jnp.zeros_like(sum_ref)

    for k in range(square + plain):
        product = jnp.dot(rows_ref[...], weights[k][...], preferred_element_type=jnp.float32)
        outs[k][...] = product.astype(outs[k].dtype)
        if k < square:
            outs[square + plain + k][...] += jnp.sum(product * product, axis=1, keepdims=True)


def project(blocks, square, plain):
    rows, depth = blocks[0].shape
    count = len(blocks)
    width = square[0].shape[1]
    wide = min(256, width)
    whole = pl.BlockSpec((count * rows, depth), lambda i: (0, 0))
    column = pl.BlockSpec((depth, wide), lambda i: (0, i))
    product = pl.BlockSpec((count * rows, wide), lambda i: (0, i))
    sums = pl.BlockSpec((count * rows, 1), lambda i: (0, 0))
    return pl.pallas_call(
        functools.partial(project_kernel, blocks=count, square=len(square), plain=len(plain)),
        grid=(width // wide,),
        in_specs=[pl.BlockSpec((rows, depth), lambda i: (0, 0))] * count
        + [column] * (len(square) + len(plain)),
        out_specs=[whole] + [product] * (len(square) + len(plain)) + [sums] * len(square),
        out_shape=[jax.ShapeDtypeStruct((count * rows, depth), jnp.bfloat16)]
        + [jax.ShapeDtypeStruct((count * rows, width), jnp.float32)] * len(square)
        + [jax.ShapeDtypeStruct((count * rows, width), jnp.bfloat16)] * len(plain)
        + [jax.ShapeDtypeStruct((count * rows, 1), jnp.float32)] * len(square),
        name="project",
    )(*blocks, *square, *plain)


def attend_kernel(
    query_ref, key_ref, key_other_ref, value_own_ref, value_other_ref,
    inv_query_ref, inv_key_ref, gain_query_ref, gain_key_ref,
    cos_query_ref, sin_query_ref, cos_key_ref, sin_key_ref, at_query_ref, at_key_ref,
    query_low_ref, key_low_ref, value_ref, mixed_ref, lse_ref,
):
    @pl.when(pl.program_id(1) == 0)
    def _():
        half = key_ref.shape[0]
        value_ref[:half] = value_own_ref[...]
        value_ref[half:] = value_other_ref[...]
        for side, ref in ((slice(0, half), key_ref), (slice(half, 2 * half), key_other_ref)):
            scaled = ref[...] * inv_key_ref[side] * gain_key_ref[...]
            key_low_ref[side] = turned(scaled, cos_key_ref[side], sin_key_ref[side]).astype(
                jnp.bfloat16
            )

    scaled = query_ref[...] * inv_query_ref[...] * gain_query_ref[...]
    query_low = turned(scaled, cos_query_ref[...], sin_query_ref[...]).astype(jnp.bfloat16)
    query_low_ref[...] = query_low
    scores = HD ** (-0.5) * times_transpose(query_low, key_low_ref[...])
    scores = jnp.where(at_key_ref[...] <= at_query_ref[...], scores, NEG_FILL)
    peak = jnp.max(scores, axis=1, keepdims=True)
    exps = jnp.exp(scores - peak)
    total = jnp.sum(exps, axis=1, keepdims=True)
    probs = (exps * (1.0 / total)).astype(jnp.bfloat16)
    mixed_ref[...] = jnp.dot(
        probs, value_ref[...], preferred_element_type=jnp.float32
    ).astype(jnp.bfloat16)
    lse_ref[0] = peak + jnp.log(total)


def attend_back_kernel(
    query_low_ref, key_low_ref, value_ref, grad_ref, lse_ref,
    cos_query_ref, sin_query_ref, cos_key_ref, sin_key_ref, at_query_ref, at_key_ref,
    grad_query_ref, grad_key_ref, grad_value_ref, prev_key_ref, prev_value_ref,
    key_sum, value_sum,
):
    scale = HD ** (-0.5)
    query_low = query_low_ref[...]
    key_low = key_low_ref[...]
    grad_low = grad_ref[...]
    scores = scale * times_transpose(query_low, key_low)
    allowed = at_key_ref[...] <= at_query_ref[...]
    probs = jnp.exp(jnp.where(allowed, scores, NEG_FILL) - lse_ref[0])
    grad_probs = times_transpose(grad_low, value_ref[...])
    delta = jnp.sum(probs * grad_probs, axis=1, keepdims=True)
    grad_scores = (probs * (grad_probs - delta)).astype(jnp.bfloat16)
    grad_query = scale * jnp.dot(grad_scores, key_low, preferred_element_type=jnp.float32)
    grad_query_ref[...] = turned(grad_query, cos_query_ref[...], -sin_query_ref[...])
    key_part = scale * contract_rows(grad_scores, query_low)
    value_part = contract_rows(probs.astype(jnp.bfloat16), grad_low)

    @pl.when(pl.program_id(1) == 0)
    def _():
        key_sum[...] = key_part
        value_sum[...] = value_part

    @pl.when(pl.program_id(1) > 0)
    def _():
        key_sum[...] += key_part
        value_sum[...] += value_part

    @pl.when(pl.program_id(1) == pl.num_programs(1) - 1)
    def _():
        half = key_sum.shape[0] // 2
        turned_back = turned(key_sum[...], cos_key_ref[...], -sin_key_ref[...])
        grad_key_ref[...] = turned_back[:half]
        prev_key_ref[...] = turned_back[half:].astype(jnp.bfloat16)
        grad_value_ref[...] = value_sum[:half]
        prev_value_ref[...] = value_sum[half:].astype(jnp.bfloat16)


def attention_specs(half_rows, key_rows, block_rows):
    spec = {
        "query": pl.BlockSpec((block_rows, HD), lambda h, i: (i, h)),
        "key": pl.BlockSpec((key_rows, HD), lambda h, i: (0, h)),
        "half": pl.BlockSpec((half_rows, HD), lambda h, i: (0, h)),
        "gain": pl.BlockSpec((1, HD), lambda h, i: (0, h)),
        "query_column": pl.BlockSpec((block_rows, 1), lambda h, i: (i, 0)),
        "key_column": pl.BlockSpec((key_rows, 1), lambda h, i: (0, 0)),
        "key_row": pl.BlockSpec((1, key_rows), lambda h, i: (0, 0)),
        "query_turn": pl.BlockSpec((block_rows, HD), lambda h, i: (i, 0)),
        "key_turn": pl.BlockSpec((key_rows, HD), lambda h, i: (0, 0)),
        "lse": pl.BlockSpec((1, block_rows, 1), lambda h, i: (h, i, 0)),
    }
    return spec


def attend(query, keys, values, inv_query, inv_key, gain_query, gain_key, turns, block_rows):
    half_rows, width = query.shape
    key_rows = 2 * half_rows
    heads = width // HD
    s = attention_specs(half_rows, key_rows, block_rows)
    return pl.pallas_call(
        attend_kernel,
        grid=(heads, half_rows // block_rows),
        in_specs=[
            s["query"], s["half"], s["half"], s["half"], s["half"],
            s["query_column"], s["key_column"], s["gain"], s["gain"],
            s["query_turn"], s["query_turn"], s["key_turn"], s["key_turn"],
            s["query_column"], s["key_row"],
        ],
        out_specs=[s["query"], s["key"], s["key"], s["query"], s["lse"]],
        out_shape=[
            jax.ShapeDtypeStruct(query.shape, jnp.bfloat16),
            jax.ShapeDtypeStruct((key_rows, width), jnp.bfloat16),
            jax.ShapeDtypeStruct((key_rows, width), jnp.bfloat16),
            jax.ShapeDtypeStruct(query.shape, jnp.bfloat16),
            jax.ShapeDtypeStruct((heads, half_rows, 1), jnp.float32),
        ],
        name="attend",
    )(query, *keys, *values, inv_query, inv_key, gain_query, gain_key, *turns)


def attend_back(query_low, key_low, value, grad, lse, turns, block_rows):
    half_rows, width = query_low.shape
    key_rows = key_low.shape[0]
    heads = width // HD
    s = attention_specs(half_rows, key_rows, block_rows)
    halves = (half_rows, width)
    return pl.pallas_call(
        attend_back_kernel,
        grid=(heads, half_rows // block_rows),
        in_specs=[
            s["query"], s["key"], s["key"], s["query"], s["lse"],
            s["query_turn"], s["query_turn"], s["key_turn"], s["key_turn"],
            s["query_column"], s["key_row"],
        ],
        out_specs=[s["query"], s["half"], s["half"], s["half"], s["half"]],
        out_shape=[
            jax.ShapeDtypeStruct(halves, jnp.float32),
            jax.ShapeDtypeStruct(halves, jnp.float32),
            jax.ShapeDtypeStruct(halves, jnp.float32),
            jax.ShapeDtypeStruct(halves, jnp.bfloat16),
            jax.ShapeDtypeStruct(halves, jnp.bfloat16),
        ],
        scratch_shapes=[
            pltpu.VMEM((key_rows, HD), jnp.float32),
            pltpu.VMEM((key_rows, HD), jnp.float32),
        ],
        name="attend_back",
    )(query_low, key_low, value, grad, lse, *turns)


def store_kernel(place_ref, mine_ref, theirs_ref, *refs, outs):
    width = mine_ref.shape[1] // outs
    for side, half_ref in enumerate((mine_ref, theirs_ref)):

        @pl.when(pl.program_id(0) == side)
        def _():
            for k, out_ref in enumerate(refs[-outs:]):
                out_ref[...] = half_ref[:, k * width : (k + 1) * width].astype(jnp.float32)


def store_chunk(buffers, mine, theirs, shapes, where_to):
    place = lax.axis_index("ctx").astype(jnp.int32).reshape(1)
    rows, columns = mine.shape
    outs = len(shapes)
    block = min(128, rows)
    steps = rows // block
    operands = [place, mine, theirs]
    in_specs = [
        pl.BlockSpec((block, columns), lambda i, r, p: (r * (1 - i) + (steps - 1) * i, 0)),
        pl.BlockSpec((block, columns), lambda i, r, p: (r * i, 0)),
    ]
    aliases = {}
    if buffers is not None:
        operands.extend(buffers)
        in_specs.extend([pl.BlockSpec(memory_space=pl.ANY)] * outs)
        aliases = {3 + k: k for k in range(outs)}

    def out_at(i, r, p):
        row, column = where_to(p[0] ^ i)
        return row * steps + r, column

    return pl.pallas_call(
        functools.partial(store_kernel, outs=outs),
        grid_spec=pltpu.PrefetchScalarGridSpec(
            num_scalar_prefetch=1,
            grid=(2, steps),
            in_specs=in_specs,
            out_specs=[pl.BlockSpec((block, columns // outs), out_at)] * outs,
        ),
        out_shape=[jax.ShapeDtypeStruct(shape, jnp.float32) for shape in shapes],
        input_output_aliases=aliases,
        name="store",
    )(*operands)


class Gradients:
    def __init__(self, shapes, row_chunks, column_chunks, by_rows):
        self.shapes, self.by_rows = shapes, by_rows
        self.row_chunks, self.column_chunks = row_chunks, column_chunks
        self.chunks = row_chunks * column_chunks
        self.buffers = None
        self.kept = []

    def part(self, sides, index):
        left, grad = sides
        row, column = divmod(index, self.column_chunks)
        rows, columns = left.shape[1] // self.row_chunks, grad.shape[1] // self.column_chunks
        left = lax.slice_in_dim(left, row * rows, (row + 1) * rows, axis=1)
        grad = lax.slice_in_dim(grad, column * columns, (column + 1) * columns, axis=1)
        return contract_rows(left, grad).astype(jnp.bfloat16)

    def store(self, index, mine, theirs):
        row, column = divmod(index, self.column_chunks)
        if (mine.shape[1] // len(self.shapes)) % 128:
            self.kept.append((mine, theirs))
            return
        if self.by_rows:
            where_to = lambda half: (half * self.row_chunks + row, column)
        else:
            where_to = lambda half: (row, half)
        self.buffers = store_chunk(self.buffers, mine, theirs, self.shapes, where_to)

    def results(self):
        if self.buffers is not None:
            return self.buffers
        first = lax.axis_index("ctx") == 0
        width = self.kept[0][0].shape[1] // len(self.shapes)
        found = []
        for k in range(len(self.shapes)):
            cut = lambda value: value[:, k * width : (k + 1) * width]
            pieces = [
                jnp.concatenate(
                    [
                        jnp.where(first, cut(mine), cut(theirs)),
                        jnp.where(first, cut(theirs), cut(mine)),
                    ],
                    axis=1,
                )
                for mine, theirs in self.kept
            ]
            found.append(jnp.concatenate(pieces, axis=0).astype(jnp.float32))
        return found


def added(left, right):
    return (left.astype(jnp.float32) + right.astype(jnp.float32)).astype(left.dtype)


def body(
    tokens,
    w_query,
    w_key,
    w_value,
    gain_query,
    gain_key,
    w_out,
    gain_attn,
    w_gate,
    w_up,
    w_down,
    gain_ffn,
    cotangent,
    source_ids,
    group_weights,
):
    seq_count = lax.axis_size("seq")
    seq_place = lax.axis_index("seq")
    ctx_place = lax.axis_index("ctx")
    dp_place = lax.axis_index("dp")
    middle = jnp.logical_or(dp_place == 1, dp_place == 2)
    tok_rows = tokens.shape[0]
    half_rows = tok_rows * seq_count
    head_width = w_query.shape[1]
    hidden_width = w_gate.shape[1]
    block_rows = min(512, half_rows) if half_rows <= 512 else 256
    owners = jnp.bitwise_xor(jnp.arange(seq_count, dtype=jnp.int32), seq_place)
    row_ids = (owners[:, None] * tok_rows + jnp.arange(tok_rows, dtype=jnp.int32)[None, :]).reshape(
        half_rows
    )
    at_query = (ctx_place * half_rows + row_ids).astype(jnp.float32)
    at_key = jnp.concatenate([at_query, ((1 - ctx_place) * half_rows + row_ids).astype(jnp.float32)])
    lane = jnp.arange(HD, dtype=jnp.int32)
    inverse = ROPE_BASE ** (-((lane % (HD // 2)).astype(jnp.float32) * 2.0 / HD))
    angles = at_key[:, None] * inverse[None, :]
    cosine = jnp.cos(angles)
    sine = jnp.sin(angles) * jnp.where(lane < HD // 2, -1.0, 1.0)[None, :]
    turns = (cosine, sine, cosine, sine, at_query[:, None], at_key[None, :])

    own_blocks, other_blocks, turns = gather_both(tokens, "seq", turns)
    tokens_own, query_proj, key_proj, value_own, sq_query, sq_key = project(
        own_blocks, (w_query, w_key), (w_value,)
    )
    tokens_other, key_other, value_other, sq_key_other = project(
        other_blocks, (w_key,), (w_value,)
    )

    def common_rows(parts):
        stacked = jnp.stack(parts).reshape(len(parts), seq_count, tok_rows)
        return jnp.take(stacked, owners, axis=1)

    def own_rows(sums):
        return jnp.take(sums, owners, axis=1).reshape(sums.shape[0], half_rows)

    sums = own_rows(lax.psum(common_rows((sq_query, sq_key, sq_key_other)), "seq"))
    inv_query = lax.rsqrt(sums[0] / D + EPS)[:, None]
    inv_key_both = lax.rsqrt(sums[1:].reshape(2 * half_rows) / D + EPS)[:, None]
    inv_key = inv_key_both[:half_rows]
    query_low, key_low, value_low, attn_low, lse = attend(
        query_proj, (key_proj, key_other), (value_own, value_other), inv_query, inv_key_both, gain_query[None, :],
        gain_key[None, :], turns, block_rows,
    )

    def to_owners(partial):
        return scatter_rows(row_blocks(partial, seq_count), "seq")

    attn_other = flip(attn_low, "ctx", 1)
    attn_proj = to_owners(jnp.dot(attn_low, w_out, preferred_element_type=jnp.float32))
    attn_proj, attn_other = lax.optimization_barrier((attn_proj, attn_other))
    inv_attn = lax.rsqrt(jnp.mean(attn_proj * attn_proj, axis=1, keepdims=True) + EPS)
    attn_unit = attn_proj * inv_attn
    hidden = tokens.astype(jnp.float32) + attn_unit * gain_attn
    hidden_low = hidden.astype(jnp.bfloat16)
    hidden_flip = flip(hidden_low, "ctx", 1)
    hidden_blocks, hidden_flip = gather_beside(hidden_low, "seq", hidden_flip)
    hidden_own = lax.optimization_barrier(stacked(hidden_blocks))
    hidden_rest = gather_rows(hidden_flip, "seq")
    gate_proj = jnp.dot(hidden_own, w_gate, preferred_element_type=jnp.float32)
    up_proj = jnp.dot(hidden_own, w_up, preferred_element_type=jnp.float32)
    gate_sig = jax.nn.sigmoid(gate_proj)
    swish = gate_proj * gate_sig
    inner_low = (swish * up_proj).astype(jnp.bfloat16)
    inner_low, hidden_rest = lax.optimization_barrier((inner_low, hidden_rest))
    inner_halves = both_halves(inner_low)
    ffn = to_owners(jnp.dot(inner_low, w_down, preferred_element_type=jnp.float32))
    ffn, inner_halves = lax.optimization_barrier((ffn, inner_halves))
    inv_ffn = lax.rsqrt(jnp.mean(ffn * ffn, axis=1, keepdims=True) + EPS)
    ffn_unit = ffn * inv_ffn
    out_tokens = (hidden + ffn_unit * gain_ffn).astype(jnp.bfloat16)
    picked = jnp.sum(
        jnp.where(
            jnp.arange(group_weights.shape[0], dtype=jnp.int32) == source_ids[0], group_weights, 0.0
        )
    )
    grad_out = cotangent.astype(jnp.float32) * picked
    gain_ffn_part = jnp.sum(grad_out * ffn_unit, axis=0)
    grad_ffn_low = norm_back(ffn_unit, inv_ffn, grad_out * gain_ffn).astype(jnp.bfloat16)
    grad_ffn_own, grad_ffn_other, _ = gather_both(grad_ffn_low, "seq")
    grad_ffn_both = stacked(grad_ffn_own + grad_ffn_other)

    grads = {
        "down": Gradients([w_down.shape], 2, 2, True),
        "gate": Gradients([w_gate.shape], 4, 1, False),
        "up": Gradients([w_up.shape], 4, 1, False),
        "out": Gradients([w_out.shape], 1, 1, False),
        "in": Gradients([w_query.shape, w_key.shape, w_value.shape], 4, 1, False),
    }
    sides = {"down": (stacked(inner_halves), grad_ffn_both)}
    results = {}

    def stages():
        (grad_ffn,) = yield (grad_ffn_both[:half_rows],)
        grad_inner = times_transpose(grad_ffn, w_down)
        grad_gate = (grad_inner * up_proj * gate_sig * (1.0 + gate_proj * (1.0 - gate_sig))).astype(
            jnp.bfloat16
        )
        grad_up = (grad_inner * swish).astype(jnp.bfloat16)
        grad_gate, grad_up = yield (grad_gate, grad_up)
        hidden_both = stacked([hidden_own] + hidden_rest)
        sides["gate"] = (hidden_both, stacked(both_halves(grad_gate)))
        gate_share = times_transpose(grad_gate, w_gate)
        gate_share, grad_up = yield (gate_share, grad_up)
        sides["up"] = (hidden_both, stacked(both_halves(grad_up)))
        partial = gate_share + times_transpose(grad_up, w_up)
        (partial,) = yield (partial,)
        grad_hidden = grad_out + to_owners(partial)
        (grad_hidden,) = yield (grad_hidden,)
        gain_attn_part = jnp.sum(grad_hidden * attn_unit, axis=0)
        grad_proj_low = norm_back(attn_unit, inv_attn, grad_hidden * gain_attn).astype(jnp.bfloat16)
        grad_proj_own = stacked(gather_rows(grad_proj_low, "seq"))
        (grad_proj_own,) = yield (grad_proj_own,)
        sides["out"] = (stacked([attn_low, attn_other]), stacked(both_halves(grad_proj_own)))
        grad_attn_low = times_transpose(grad_proj_own, w_out).astype(jnp.bfloat16)
        backs = attend_back(query_low, key_low, value_low, grad_attn_low, lse, turns, block_rows)
        backs = yield backs
        grad_query_norm, own_dk, own_dv, prev_dk, prev_dv = backs
        back_dk, back_dv = lax.ppermute((prev_dk, prev_dv), "ctx", [(1, 0)])
        grad_query_norm, own_dk, own_dv, back_dk, back_dv = yield (
            grad_query_norm, own_dk, own_dv, back_dk, back_dv
        )
        grad_value_low = (own_dv + back_dv.astype(jnp.float32)).astype(jnp.bfloat16)
        grad_key_norm = own_dk + back_dk.astype(jnp.float32)
        query_unit = query_proj * inv_query
        key_unit = key_proj * inv_key
        gain_query_part = jnp.sum(grad_query_norm * query_unit, axis=0)
        gain_key_part = jnp.sum(grad_key_norm * key_unit, axis=0)
        query_scaled = grad_query_norm * gain_query
        key_scaled = grad_key_norm * gain_key
        dots, gain_sums = lax.psum(
            (
                common_rows(
                    (
                        jnp.sum(query_scaled * query_unit, axis=1),
                        jnp.sum(key_scaled * key_unit, axis=1),
                    )
                ),
                jnp.concatenate([gain_attn_part, gain_ffn_part]),
            ),
            "seq",
        )
        dots_query, dots_key = own_rows(dots)
        grad_query_low = (
            inv_query * (query_scaled - query_unit * (dots_query / D)[:, None])
        ).astype(jnp.bfloat16)
        grad_key_low = (inv_key * (key_scaled - key_unit * (dots_key / D)[:, None])).astype(
            jnp.bfloat16
        )
        gains = jnp.concatenate([gain_sums, gain_query_part, gain_key_part]).reshape(-1, 128)
        grad_value_low, grad_key_low, grad_query_low, gains = yield (
            grad_value_low, grad_key_low, grad_query_low, gains
        )
        place = ctx_place
        lows = (grad_query_low, grad_key_low, grad_value_low)
        mine = jnp.concatenate([half_columns(low, place) for low in lows], axis=1)
        given = jnp.concatenate([half_columns(low, 1 - place) for low in lows], axis=1)
        sides["in"] = (
            stacked([tokens_own, tokens_other]),
            stacked([mine, flip(given, "ctx", 1)]),
        )
        gains_other = flip(gains, "ctx", 1)
        partial = (
            times_transpose(grad_query_low, w_query)
            + times_transpose(grad_key_low, w_key)
            + times_transpose(grad_value_low, w_value)
        )
        partial, gains, gains_other = yield (partial, gains, gains_other)
        gains = gains + gains_other
        gains_pair = lax.ppermute(gains, "dp", PAIRS)
        grad_tokens = grad_hidden + to_owners(partial)
        grad_tokens, gains, gains_pair = yield (grad_tokens, gains, gains_pair)
        results["tokens"] = grad_tokens
        gains = gains + gains_pair
        gains_across = lax.ppermute(gains, "dp", ACROSS)
        gains, gains_across = yield (gains, gains_across)
        gains = gains + gains_across
        gains_out = lax.ppermute(gains, "dp", PAIRS)
        gains, gains_out = yield (gains, gains_out)
        results["gains"] = jnp.where(middle, gains, gains_out)

    plan = [(name, index) for name in grads for index in range(grads[name].chunks)]
    count = len(plan)
    part, pair, sent, final = {}, {}, {}, {}
    got_in, got_across, got_out, got_half = {}, {}, {}, {}
    main = stages()
    state = next(main)
    last_name, last_buffers = None, None
    token = picked
    part[0] = grads[plan[0][0]].part(sides[plan[0][0]], 0)

    for tick in range(count + 5):
        crossing = None
        if tick - 1 in part:
            crossing = added(part[tick - 1], got_in[tick - 1])
        coming = sides.get(plan[tick + 1][0]) if tick + 1 < count else None
        held = (crossing, state, coming, last_buffers, token)
        crossing, state, coming, last_buffers, token = lax.optimization_barrier(held)
        if last_name:
            grads[last_name].buffers = last_buffers
        if crossing is not None:
            pair[tick - 1] = crossing
            got_across[tick - 1] = lax.ppermute(crossing, "dp", ACROSS)
        entering = part.get(tick)
        leaving = None
        if tick - 2 in pair:
            leaving = added(pair[tick - 2], got_across[tick - 2])
        if entering is not None and leaving is not None and entering.shape == leaving.shape:
            held = (jnp.where(middle, leaving, entering), token)
            sent[tick - 2], token = lax.optimization_barrier(held)
            got_in[tick] = got_out[tick - 2] = lax.ppermute(sent[tick - 2], "dp", PAIRS)
        else:
            entering, leaving, token = lax.optimization_barrier((entering, leaving, token))
            if entering is not None:
                part[tick] = entering
                got_in[tick] = lax.ppermute(entering, "dp", PAIRS if leaving is None else INWARD)
            if leaving is not None:
                sent[tick - 2] = leaving
                got_out[tick - 2] = lax.ppermute(
                    leaving, "dp", PAIRS if entering is None else OUTWARD
                )
        if tick - 3 in sent:
            swapping = jnp.where(middle, sent[tick - 3], got_out[tick - 3])
            final[tick - 3], token = lax.optimization_barrier((swapping, token))
            got_half[tick - 3] = flip(final[tick - 3], "ctx", 1)
        if tick - 4 in final:
            theirs, token = lax.optimization_barrier((got_half[tick - 4], token))
            last_name, index = plan[tick - 4]
            grads[last_name].store(index, final[tick - 4], theirs)
            last_buffers = grads[last_name].buffers
        try:
            state = main.send(state)
        except StopIteration:
            state = ()
        if tick + 1 < count:
            name, index = plan[tick + 1]
            coming = sides[name] if coming is None else coming
            part[tick + 1] = grads[name].part(coming, index)

    gains = results["gains"].reshape(-1)
    grad_w_query, grad_w_key, grad_w_value = grads["in"].results()
    grad_gain_attn = gains[:D]
    grad_gain_ffn = gains[D : 2 * D]
    grad_gain_query = gains[2 * D : 2 * D + head_width]
    grad_gain_key = gains[2 * D + head_width :]
    return (
        out_tokens,
        results["tokens"],
        grad_w_query,
        grad_w_key,
        grad_w_value,
        grad_gain_query,
        grad_gain_key,
        *grads["out"].results(),
        grad_gain_attn,
        *grads["gate"].results(),
        *grads["up"].results(),
        *grads["down"].results(),
        grad_gain_ffn,
    )


def solution(mesh):
    in_specs = (
        P(("dp", "ctx", "seq"), None),
        P(None, "seq"),
        P(None, "seq"),
        P(None, "seq"),
        P("seq"),
        P("seq"),
        P("seq", None),
        P(),
        P(None, "seq"),
        P(None, "seq"),
        P("seq", None),
        P(),
        P(("dp", "ctx", "seq"), None),
        P("dp"),
        P(),
    )
    out_specs = (
        P(("dp", "ctx", "seq"), None),
        P(("dp", "ctx", "seq"), None),
        P(None, "seq"),
        P(None, "seq"),
        P(None, "seq"),
        P("seq"),
        P("seq"),
        P("seq", None),
        P(),
        P(None, "seq"),
        P(None, "seq"),
        P("seq", None),
        P(),
    )
    return jax.shard_map(body, mesh=mesh, in_specs=in_specs, out_specs=out_specs, check_vma=False)
```

```python
import functools

import jax
import jax.numpy as jnp
from jax import lax
from jax.experimental import pallas as pl
from jax.experimental.pallas import tpu as pltpu
from jax.sharding import PartitionSpec as P

D = 2048
HD = 128


EPS = 1e-06
ROPE_BASE = 500000.0
NEG_FILL = -1e30
PAIRS = [(0, 1), (1, 0), (2, 3), (3, 2)]
INWARD = [(0, 1), (3, 2)]
OUTWARD = [(1, 0), (2, 3)]
ACROSS = [(1, 2), (2, 1)]


def flip(value, axis, distance):
    count = lax.axis_size(axis)
    return lax.ppermute(value, axis, [(place, place ^ distance) for place in range(count)])


def distances(axis):
    count = lax.axis_size(axis)
    found = []
    step = 1
    while step < count:
        found.append(step)
        step *= 2
    return found


def gather_rows(own, axis):
    parts = {0: own}
    for distance in reversed(distances(axis)):
        parts.update({o ^ distance: flip(block, axis, distance) for o, block in parts.items()})
    return [parts[o] for o in range(len(parts))]


def gather_both(own, axis, beside=None):
    mine, theirs = {0: own}, {0: flip(own, "ctx", 1)}
    for far, distance in enumerate(reversed(distances(axis))):
        for o in list(mine):
            mine[o ^ distance] = flip(mine[o], axis, distance)
            if far == 0 and distance > 1:
                rows = own.shape[0] // 2
                theirs[o ^ distance] = stacked(
                    [
                        flip(theirs[o][:rows], axis, distance),
                        flip(mine[o ^ distance][rows:], "ctx", 1),
                    ]
                )
                held = (mine[o ^ distance], beside)
                mine[o ^ distance], beside = lax.optimization_barrier(held)
            else:
                theirs[o ^ distance] = flip(theirs[o], axis, distance)
    blocks = range(len(mine))
    return [mine[o] for o in blocks], [theirs[o] for o in blocks], beside


def gather_beside(own, axis, beside):
    parts = {0: own}
    for distance in reversed(distances(axis)):
        parts.update({o ^ distance: flip(block, axis, distance) for o, block in parts.items()})
        if len(parts) == 2:
            held = (parts[distance], beside)
            parts[distance], beside = lax.optimization_barrier(held)
    return [parts[o] for o in range(len(parts))], beside


def stacked(blocks):
    return jnp.concatenate(blocks, axis=0)


def scatter_rows(blocks, axis):
    parts = dict(enumerate(blocks))
    for distance in distances(axis):
        kept = {o: block for o, block in parts.items() if not o & distance}
        for o in sorted(kept, reverse=True):
            sent = parts[o ^ distance].astype(jnp.bfloat16)
            kept[o] = kept[o] + flip(sent, axis, distance).astype(jnp.float32)
        parts = kept
    return parts[0]


def row_blocks(value, count):
    rows = value.shape[0] // count
    return [lax.slice_in_dim(value, o * rows, (o + 1) * rows, axis=0) for o in range(count)]


def norm_back(unit_val, inverse, grad_unit):
    return inverse * (grad_unit - unit_val * jnp.mean(grad_unit * unit_val, axis=-1, keepdims=True))


def contract_rows(left, right):
    return lax.dot_general(
        left, right, (((0,), (0,)), ((), ())), preferred_element_type=jnp.float32
    )


def times_transpose(left, right):
    return lax.dot_general(
        left, right, (((1,), (1,)), ((), ())), preferred_element_type=jnp.float32
    )


def half_columns(value, place):
    width = value.shape[1] // 2
    return lax.dynamic_slice_in_dim(value, place * width, width, axis=1)


def both_halves(value):
    place = lax.axis_index("ctx")
    return half_columns(value, place), flip(half_columns(value, 1 - place), "ctx", 1)


def turned(values, cosine, sine):
    return values * cosine + pltpu.roll(values, HD // 2, 1) * sine


def project_kernel(*refs, blocks, square, plain):
    rows_ref = refs[blocks + square + plain]
    outs = refs[blocks + square + plain + 1 :]
    weights = refs[blocks : blocks + square + plain]

    @pl.when(pl.program_id(0) == 0)
    def _():
        rows = refs[0].shape[0]
        for o in range(blocks):
            rows_ref[o * rows : (o + 1) * rows, :] = refs[o][...]
        for sum_ref in outs[square + plain :]:
            sum_ref[...] = jnp.zeros_like(sum_ref)

    for k in range(square + plain):
        product = jnp.dot(rows_ref[...], weights[k][...], preferred_element_type=jnp.float32)
        outs[k][...] = product.astype(outs[k].dtype)
        if k < square:
            outs[square + plain + k][...] += jnp.sum(product * product, axis=1, keepdims=True)


def project(blocks, square, plain):
    rows, depth = blocks[0].shape
    count = len(blocks)
    width = square[0].shape[1]
    wide = min(256, width)
    whole = pl.BlockSpec((count * rows, depth), lambda i: (0, 0))
    column = pl.BlockSpec((depth, wide), lambda i: (0, i))
    product = pl.BlockSpec((count * rows, wide), lambda i: (0, i))
    sums = pl.BlockSpec((count * rows, 1), lambda i: (0, 0))
    return pl.pallas_call(
        functools.partial(project_kernel, blocks=count, square=len(square), plain=len(plain)),
        grid=(width // wide,),
        in_specs=[pl.BlockSpec((rows, depth), lambda i: (0, 0))] * count
        + [column] * (len(square) + len(plain)),
        out_specs=[whole] + [product] * (len(square) + len(plain)) + [sums] * len(square),
        out_shape=[jax.ShapeDtypeStruct((count * rows, depth), jnp.bfloat16)]
        + [jax.ShapeDtypeStruct((count * rows, width), jnp.float32)] * len(square)
        + [jax.ShapeDtypeStruct((count * rows, width), jnp.bfloat16)] * len(plain)
        + [jax.ShapeDtypeStruct((count * rows, 1), jnp.float32)] * len(square),
        name="project",
    )(*blocks, *square, *plain)


def attend_kernel(
    query_ref, key_ref, key_other_ref, value_own_ref, value_other_ref,
    inv_query_ref, inv_key_ref, gain_query_ref, gain_key_ref,
    cos_query_ref, sin_query_ref, cos_key_ref, sin_key_ref, at_query_ref, at_key_ref,
    query_low_ref, key_low_ref, value_ref, mixed_ref, lse_ref,
):
    @pl.when(pl.program_id(1) == 0)
    def _():
        half = key_ref.shape[0]
        value_ref[:half] = value_own_ref[...]
        value_ref[half:] = value_other_ref[...]
        for side, ref in ((slice(0, half), key_ref), (slice(half, 2 * half), key_other_ref)):
            scaled = ref[...] * inv_key_ref[side] * gain_key_ref[...]
            key_low_ref[side] = turned(scaled, cos_key_ref[side], sin_key_ref[side]).astype(
                jnp.bfloat16
            )

    scaled = query_ref[...] * inv_query_ref[...] * gain_query_ref[...]
    query_low = turned(scaled, cos_query_ref[...], sin_query_ref[...]).astype(jnp.bfloat16)
    query_low_ref[...] = query_low
    scores = HD ** (-0.5) * times_transpose(query_low, key_low_ref[...])
    scores = jnp.where(at_key_ref[...] <= at_query_ref[...], scores, NEG_FILL)
    peak = jnp.max(scores, axis=1, keepdims=True)
    exps = jnp.exp(scores - peak)
    total = jnp.sum(exps, axis=1, keepdims=True)
    probs = (exps * (1.0 / total)).astype(jnp.bfloat16)
    mixed_ref[...] = jnp.dot(
        probs, value_ref[...], preferred_element_type=jnp.float32
    ).astype(jnp.bfloat16)
    lse_ref[0] = peak + jnp.log(total)


def attend_back_kernel(
    query_low_ref, key_low_ref, value_ref, grad_ref, lse_ref,
    cos_query_ref, sin_query_ref, cos_key_ref, sin_key_ref, at_query_ref, at_key_ref,
    grad_query_ref, grad_key_ref, grad_value_ref, prev_key_ref, prev_value_ref,
    key_sum, value_sum,
):
    scale = HD ** (-0.5)
    query_low = query_low_ref[...]
    key_low = key_low_ref[...]
    grad_low = grad_ref[...]
    scores = scale * times_transpose(query_low, key_low)
    allowed = at_key_ref[...] <= at_query_ref[...]
    probs = jnp.exp(jnp.where(allowed, scores, NEG_FILL) - lse_ref[0])
    grad_probs = times_transpose(grad_low, value_ref[...])
    delta = jnp.sum(probs * grad_probs, axis=1, keepdims=True)
    grad_scores = (probs * (grad_probs - delta)).astype(jnp.bfloat16)
    grad_query = scale * jnp.dot(grad_scores, key_low, preferred_element_type=jnp.float32)
    grad_query_ref[...] = turned(grad_query, cos_query_ref[...], -sin_query_ref[...])
    key_part = scale * contract_rows(grad_scores, query_low)
    value_part = contract_rows(probs.astype(jnp.bfloat16), grad_low)

    @pl.when(pl.program_id(1) == 0)
    def _():
        key_sum[...] = key_part
        value_sum[...] = value_part

    @pl.when(pl.program_id(1) > 0)
    def _():
        key_sum[...] += key_part
        value_sum[...] += value_part

    @pl.when(pl.program_id(1) == pl.num_programs(1) - 1)
    def _():
        half = key_sum.shape[0] // 2
        turned_back = turned(key_sum[...], cos_key_ref[...], -sin_key_ref[...])
        grad_key_ref[...] = turned_back[:half]
        prev_key_ref[...] = turned_back[half:].astype(jnp.bfloat16)
        grad_value_ref[...] = value_sum[:half]
        prev_value_ref[...] = value_sum[half:].astype(jnp.bfloat16)


def attention_specs(half_rows, key_rows, block_rows):
    spec = {
        "query": pl.BlockSpec((block_rows, HD), lambda h, i: (i, h)),
        "key": pl.BlockSpec((key_rows, HD), lambda h, i: (0, h)),
        "half": pl.BlockSpec((half_rows, HD), lambda h, i: (0, h)),
        "gain": pl.BlockSpec((1, HD), lambda h, i: (0, h)),
        "query_column": pl.BlockSpec((block_rows, 1), lambda h, i: (i, 0)),
        "key_column": pl.BlockSpec((key_rows, 1), lambda h, i: (0, 0)),
        "key_row": pl.BlockSpec((1, key_rows), lambda h, i: (0, 0)),
        "query_turn": pl.BlockSpec((block_rows, HD), lambda h, i: (i, 0)),
        "key_turn": pl.BlockSpec((key_rows, HD), lambda h, i: (0, 0)),
        "lse": pl.BlockSpec((1, block_rows, 1), lambda h, i: (h, i, 0)),
    }
    return spec


def attend(query, keys, values, inv_query, inv_key, gain_query, gain_key, turns, block_rows):
    half_rows, width = query.shape
    key_rows = 2 * half_rows
    heads = width // HD
    s = attention_specs(half_rows, key_rows, block_rows)
    return pl.pallas_call(
        attend_kernel,
        grid=(heads, half_rows // block_rows),
        in_specs=[
            s["query"], s["half"], s["half"], s["half"], s["half"],
            s["query_column"], s["key_column"], s["gain"], s["gain"],
            s["query_turn"], s["query_turn"], s["key_turn"], s["key_turn"],
            s["query_column"], s["key_row"],
        ],
        out_specs=[s["query"], s["key"], s["key"], s["query"], s["lse"]],
        out_shape=[
            jax.ShapeDtypeStruct(query.shape, jnp.bfloat16),
            jax.ShapeDtypeStruct((key_rows, width), jnp.bfloat16),
            jax.ShapeDtypeStruct((key_rows, width), jnp.bfloat16),
            jax.ShapeDtypeStruct(query.shape, jnp.bfloat16),
            jax.ShapeDtypeStruct((heads, half_rows, 1), jnp.float32),
        ],
        name="attend",
    )(query, *keys, *values, inv_query, inv_key, gain_query, gain_key, *turns)


def attend_back(query_low, key_low, value, grad, lse, turns, block_rows):
    half_rows, width = query_low.shape
    key_rows = key_low.shape[0]
    heads = width // HD
    s = attention_specs(half_rows, key_rows, block_rows)
    halves = (half_rows, width)
    return pl.pallas_call(
        attend_back_kernel,
        grid=(heads, half_rows // block_rows),
        in_specs=[
            s["query"], s["key"], s["key"], s["query"], s["lse"],
            s["query_turn"], s["query_turn"], s["key_turn"], s["key_turn"],
            s["query_column"], s["key_row"],
        ],
        out_specs=[s["query"], s["half"], s["half"], s["half"], s["half"]],
        out_shape=[
            jax.ShapeDtypeStruct(halves, jnp.float32),
            jax.ShapeDtypeStruct(halves, jnp.float32),
            jax.ShapeDtypeStruct(halves, jnp.float32),
            jax.ShapeDtypeStruct(halves, jnp.bfloat16),
            jax.ShapeDtypeStruct(halves, jnp.bfloat16),
        ],
        scratch_shapes=[
            pltpu.VMEM((key_rows, HD), jnp.float32),
            pltpu.VMEM((key_rows, HD), jnp.float32),
        ],
        name="attend_back",
    )(query_low, key_low, value, grad, lse, *turns)


def store_kernel(place_ref, mine_ref, theirs_ref, *refs, outs):
    width = mine_ref.shape[1] // outs
    for side, half_ref in enumerate((mine_ref, theirs_ref)):

        @pl.when(pl.program_id(0) == side)
        def _():
            for k, out_ref in enumerate(refs[-outs:]):
                out_ref[...] = half_ref[:, k * width : (k + 1) * width].astype(jnp.float32)


def store_chunk(buffers, mine, theirs, shapes, where_to):
    place = lax.axis_index("ctx").astype(jnp.int32).reshape(1)
    rows, columns = mine.shape
    outs = len(shapes)
    block = min(512, rows)
    steps = rows // block
    operands = [place, mine, theirs]
    in_specs = [
        pl.BlockSpec((block, columns), lambda i, r, p: (r * (1 - i) + (steps - 1) * i, 0)),
        pl.BlockSpec((block, columns), lambda i, r, p: (r * i, 0)),
    ]
    aliases = {}
    if buffers is not None:
        operands.extend(buffers)
        in_specs.extend([pl.BlockSpec(memory_space=pl.ANY)] * outs)
        aliases = {3 + k: k for k in range(outs)}

    def out_at(i, r, p):
        row, column = where_to(p[0] ^ i)
        return row * steps + r, column

    return pl.pallas_call(
        functools.partial(store_kernel, outs=outs),
        grid_spec=pltpu.PrefetchScalarGridSpec(
            num_scalar_prefetch=1,
            grid=(2, steps),
            in_specs=in_specs,
            out_specs=[pl.BlockSpec((block, columns // outs), out_at)] * outs,
        ),
        out_shape=[jax.ShapeDtypeStruct(shape, jnp.float32) for shape in shapes],
        input_output_aliases=aliases,
        name="store",
    )(*operands)


class Gradients:
    def __init__(self, shapes, row_chunks, column_chunks, by_rows):
        self.shapes, self.by_rows = shapes, by_rows
        self.row_chunks, self.column_chunks = row_chunks, column_chunks
        self.chunks = row_chunks * column_chunks
        self.buffers = None
        self.kept = []

    def part(self, sides, index):
        left, grad = sides
        row, column = divmod(index, self.column_chunks)
        rows, columns = left.shape[1] // self.row_chunks, grad.shape[1] // self.column_chunks
        left = lax.slice_in_dim(left, row * rows, (row + 1) * rows, axis=1)
        grad = lax.slice_in_dim(grad, column * columns, (column + 1) * columns, axis=1)
        return contract_rows(left, grad).astype(jnp.bfloat16)

    def store(self, index, mine, theirs):
        row, column = divmod(index, self.column_chunks)
        if (mine.shape[1] // len(self.shapes)) % 128:
            self.kept.append((mine, theirs))
            return
        if self.by_rows:
            where_to = lambda half: (half * self.row_chunks + row, column)
        else:
            where_to = lambda half: (row, half)
        self.buffers = store_chunk(self.buffers, mine, theirs, self.shapes, where_to)

    def results(self):
        if self.buffers is not None:
            return self.buffers
        first = lax.axis_index("ctx") == 0
        width = self.kept[0][0].shape[1] // len(self.shapes)
        found = []
        for k in range(len(self.shapes)):
            cut = lambda value: value[:, k * width : (k + 1) * width]
            pieces = [
                jnp.concatenate(
                    [
                        jnp.where(first, cut(mine), cut(theirs)),
                        jnp.where(first, cut(theirs), cut(mine)),
                    ],
                    axis=1,
                )
                for mine, theirs in self.kept
            ]
            found.append(jnp.concatenate(pieces, axis=0).astype(jnp.float32))
        return found


def added(left, right):
    return (left.astype(jnp.float32) + right.astype(jnp.float32)).astype(left.dtype)


def combine_kernel(
    middle_ref, part_ref, got_ref, pair_ref, across_ref, sent_ref, next_ref,
    pair_out_ref, sent_out_ref, final_out_ref,
):
    @pl.when(middle_ref[0] == 1)
    def _():
        pair_out_ref[...] = added(part_ref[...], got_ref[...])
        sent_out_ref[...] = added(pair_ref[...], across_ref[...])
        final_out_ref[...] = sent_ref[...]

    @pl.when(middle_ref[0] == 0)
    def _():
        pair_out_ref[...] = part_ref[...]
        sent_out_ref[...] = next_ref[...]
        final_out_ref[...] = got_ref[...]


def combine(middle, part, got, pair, across, sent, coming):
    rows, columns = part.shape
    block = min(256, rows)
    every = pl.BlockSpec((block, columns), lambda r, m: (r, 0))
    middles = pl.BlockSpec((block, columns), lambda r, m: (r * m[0], 0))
    ends = pl.BlockSpec((block, columns), lambda r, m: (r * (1 - m[0]), 0))
    return pl.pallas_call(
        combine_kernel,
        grid_spec=pltpu.PrefetchScalarGridSpec(
            num_scalar_prefetch=1,
            grid=(rows // block,),
            in_specs=[every, every, middles, middles, middles, ends],
            out_specs=[every] * 3,
        ),
        out_shape=[jax.ShapeDtypeStruct(part.shape, part.dtype)] * 3,
        name="combine",
    )(middle.astype(jnp.int32).reshape(1), part, got, pair, across, sent, coming)


def body(
    tokens,
    w_query,
    w_key,
    w_value,
    gain_query,
    gain_key,
    w_out,
    gain_attn,
    w_gate,
    w_up,
    w_down,
    gain_ffn,
    cotangent,
    source_ids,
    group_weights,
):
    seq_count = lax.axis_size("seq")
    seq_place = lax.axis_index("seq")
    ctx_place = lax.axis_index("ctx")
    dp_place = lax.axis_index("dp")
    middle = jnp.logical_or(dp_place == 1, dp_place == 2)
    tok_rows = tokens.shape[0]
    half_rows = tok_rows * seq_count
    head_width = w_query.shape[1]
    hidden_width = w_gate.shape[1]
    block_rows = min(512, half_rows) if half_rows <= 512 else 256
    owners = jnp.bitwise_xor(jnp.arange(seq_count, dtype=jnp.int32), seq_place)
    row_ids = (owners[:, None] * tok_rows + jnp.arange(tok_rows, dtype=jnp.int32)[None, :]).reshape(
        half_rows
    )
    at_query = (ctx_place * half_rows + row_ids).astype(jnp.float32)
    at_key = jnp.concatenate([at_query, ((1 - ctx_place) * half_rows + row_ids).astype(jnp.float32)])
    lane = jnp.arange(HD, dtype=jnp.int32)
    inverse = ROPE_BASE ** (-((lane % (HD // 2)).astype(jnp.float32) * 2.0 / HD))
    angles = at_key[:, None] * inverse[None, :]
    cosine = jnp.cos(angles)
    sine = jnp.sin(angles) * jnp.where(lane < HD // 2, -1.0, 1.0)[None, :]
    turns = (cosine, sine, cosine, sine, at_query[:, None], at_key[None, :])

    own_blocks, other_blocks, turns = gather_both(tokens, "seq", turns)
    tokens_own, query_proj, key_proj, value_own, sq_query, sq_key = project(
        own_blocks, (w_query, w_key), (w_value,)
    )
    tokens_other, key_other, value_other, sq_key_other = project(
        other_blocks, (w_key,), (w_value,)
    )

    def common_rows(parts):
        stacked = jnp.stack(parts).reshape(len(parts), seq_count, tok_rows)
        return jnp.take(stacked, owners, axis=1)

    def own_rows(sums):
        return jnp.take(sums, owners, axis=1).reshape(sums.shape[0], half_rows)

    sums = own_rows(lax.psum(common_rows((sq_query, sq_key, sq_key_other)), "seq"))
    inv_query = lax.rsqrt(sums[0] / D + EPS)[:, None]
    inv_key_both = lax.rsqrt(sums[1:].reshape(2 * half_rows) / D + EPS)[:, None]
    inv_key = inv_key_both[:half_rows]
    query_low, key_low, value_low, attn_low, lse = attend(
        query_proj, (key_proj, key_other), (value_own, value_other), inv_query, inv_key_both, gain_query[None, :],
        gain_key[None, :], turns, block_rows,
    )

    def to_owners(partial):
        return scatter_rows(row_blocks(partial, seq_count), "seq")

    attn_other = flip(attn_low, "ctx", 1)
    attn_proj = to_owners(jnp.dot(attn_low, w_out, preferred_element_type=jnp.float32))
    attn_proj, attn_other = lax.optimization_barrier((attn_proj, attn_other))
    inv_attn = lax.rsqrt(jnp.mean(attn_proj * attn_proj, axis=1, keepdims=True) + EPS)
    attn_unit = attn_proj * inv_attn
    hidden = tokens.astype(jnp.float32) + attn_unit * gain_attn
    hidden_low = hidden.astype(jnp.bfloat16)
    hidden_flip = flip(hidden_low, "ctx", 1)
    hidden_blocks, hidden_flip = gather_beside(hidden_low, "seq", hidden_flip)
    hidden_own = lax.optimization_barrier(stacked(hidden_blocks))
    hidden_rest = gather_rows(hidden_flip, "seq")
    gate_proj = jnp.dot(hidden_own, w_gate, preferred_element_type=jnp.float32)
    up_proj = jnp.dot(hidden_own, w_up, preferred_element_type=jnp.float32)
    gate_sig = jax.nn.sigmoid(gate_proj)
    swish = gate_proj * gate_sig
    inner_low = (swish * up_proj).astype(jnp.bfloat16)
    inner_low, hidden_rest = lax.optimization_barrier((inner_low, hidden_rest))
    inner_halves = both_halves(inner_low)
    ffn = to_owners(jnp.dot(inner_low, w_down, preferred_element_type=jnp.float32))
    ffn, inner_halves = lax.optimization_barrier((ffn, inner_halves))
    inv_ffn = lax.rsqrt(jnp.mean(ffn * ffn, axis=1, keepdims=True) + EPS)
    ffn_unit = ffn * inv_ffn
    out_tokens = (hidden + ffn_unit * gain_ffn).astype(jnp.bfloat16)
    picked = jnp.sum(
        jnp.where(
            jnp.arange(group_weights.shape[0], dtype=jnp.int32) == source_ids[0], group_weights, 0.0
        )
    )
    grad_out = cotangent.astype(jnp.float32) * picked
    gain_ffn_part = jnp.sum(grad_out * ffn_unit, axis=0)
    grad_ffn_low = norm_back(ffn_unit, inv_ffn, grad_out * gain_ffn).astype(jnp.bfloat16)
    grad_ffn_own, grad_ffn_other, _ = gather_both(grad_ffn_low, "seq")
    grad_ffn_both = stacked(grad_ffn_own + grad_ffn_other)

    grads = {
        "down": Gradients([w_down.shape], 1, 2, True),
        "gate": Gradients([w_gate.shape], 2, 1, False),
        "up": Gradients([w_up.shape], 2, 1, False),
        "out": Gradients([w_out.shape], 1, 1, False),
        "in": Gradients([w_query.shape, w_key.shape, w_value.shape], 4, 1, False),
    }
    sides = {"down": (stacked(inner_halves), grad_ffn_both)}
    results = {}

    def stages():
        (grad_ffn,) = yield (grad_ffn_both[:half_rows],)
        grad_inner = times_transpose(grad_ffn, w_down)
        grad_gate = (grad_inner * up_proj * gate_sig * (1.0 + gate_proj * (1.0 - gate_sig))).astype(
            jnp.bfloat16
        )
        grad_up = (grad_inner * swish).astype(jnp.bfloat16)
        hidden_both = stacked([hidden_own] + hidden_rest)
        sides["gate"] = (hidden_both, stacked(both_halves(grad_gate)))
        gate_share = times_transpose(grad_gate, w_gate)
        sides["up"] = (hidden_both, stacked(both_halves(grad_up)))
        partial = gate_share + times_transpose(grad_up, w_up)
        (partial,) = yield (partial,)
        grad_hidden = grad_out + to_owners(partial)
        gain_attn_part = jnp.sum(grad_hidden * attn_unit, axis=0)
        grad_proj_low = norm_back(attn_unit, inv_attn, grad_hidden * gain_attn).astype(jnp.bfloat16)
        grad_proj_own = stacked(gather_rows(grad_proj_low, "seq"))
        (grad_proj_own,) = yield (grad_proj_own,)
        sides["out"] = (stacked([attn_low, attn_other]), stacked(both_halves(grad_proj_own)))
        grad_attn_low = times_transpose(grad_proj_own, w_out).astype(jnp.bfloat16)
        backs = attend_back(query_low, key_low, value_low, grad_attn_low, lse, turns, block_rows)
        grad_query_norm, own_dk, own_dv, prev_dk, prev_dv = backs
        back_dk, back_dv = lax.ppermute((prev_dk, prev_dv), "ctx", [(1, 0)])
        grad_query_norm, own_dk, own_dv, back_dk, back_dv = yield (
            grad_query_norm, own_dk, own_dv, back_dk, back_dv
        )
        grad_value_low = (own_dv + back_dv.astype(jnp.float32)).astype(jnp.bfloat16)
        grad_key_norm = own_dk + back_dk.astype(jnp.float32)
        query_unit = query_proj * inv_query
        key_unit = key_proj * inv_key
        gain_query_part = jnp.sum(grad_query_norm * query_unit, axis=0)
        gain_key_part = jnp.sum(grad_key_norm * key_unit, axis=0)
        query_scaled = grad_query_norm * gain_query
        key_scaled = grad_key_norm * gain_key
        dots, gain_sums = lax.psum(
            (
                common_rows(
                    (
                        jnp.sum(query_scaled * query_unit, axis=1),
                        jnp.sum(key_scaled * key_unit, axis=1),
                    )
                ),
                jnp.concatenate([gain_attn_part, gain_ffn_part]),
            ),
            "seq",
        )
        dots_query, dots_key = own_rows(dots)
        grad_query_low = (
            inv_query * (query_scaled - query_unit * (dots_query / D)[:, None])
        ).astype(jnp.bfloat16)
        grad_key_low = (inv_key * (key_scaled - key_unit * (dots_key / D)[:, None])).astype(
            jnp.bfloat16
        )
        gains = jnp.concatenate([gain_sums, gain_query_part, gain_key_part]).reshape(-1, 128)
        place = ctx_place
        lows = (grad_query_low, grad_key_low, grad_value_low)
        mine = jnp.concatenate([half_columns(low, place) for low in lows], axis=1)
        given = jnp.concatenate([half_columns(low, 1 - place) for low in lows], axis=1)
        sides["in"] = (
            stacked([tokens_own, tokens_other]),
            stacked([mine, flip(given, "ctx", 1)]),
        )
        gains_other = flip(gains, "ctx", 1)
        partial = (
            times_transpose(grad_query_low, w_query)
            + times_transpose(grad_key_low, w_key)
            + times_transpose(grad_value_low, w_value)
        )
        partial, gains, gains_other = yield (partial, gains, gains_other)
        gains = gains + gains_other
        gains_pair = lax.ppermute(gains, "dp", PAIRS)
        grad_tokens = grad_hidden + to_owners(partial)
        grad_tokens, gains, gains_pair = yield (grad_tokens, gains, gains_pair)
        results["tokens"] = grad_tokens
        gains = gains + gains_pair
        gains_across = lax.ppermute(gains, "dp", ACROSS)
        gains, gains_across = yield (gains, gains_across)
        gains = gains + gains_across
        gains_out = lax.ppermute(gains, "dp", PAIRS)
        gains, gains_out = yield (gains, gains_out)
        results["gains"] = jnp.where(middle, gains, gains_out)

    plan = [(name, index) for name in grads for index in range(grads[name].chunks)]
    count = len(plan)
    part, pair, sent, final = {}, {}, {}, {}
    got_in, got_across, got_out, got_half = {}, {}, {}, {}
    main = stages()
    state = next(main)
    last_name, last_buffers = None, None
    token = picked
    part[0] = grads[plan[0][0]].part(sides[plan[0][0]], 0)

    for tick in range(count + 5):
        coming = sides.get(plan[tick + 1][0]) if tick + 1 < count else None
        arrived = (got_in.get(tick - 1), got_out.get(tick - 3), got_across.get(tick - 2))
        if tick - 1 in got_in and got_in[tick - 1] is arrived[1]:
            arrived = (arrived[0], None, arrived[2])
        held = (arrived, part.get(tick), state, coming, last_buffers, token)
        arrived, entering, state, coming, last_buffers, token = lax.optimization_barrier(held)
        if last_name:
            grads[last_name].buffers = last_buffers
        if entering is not None:
            part[tick] = entering
        if tick - 1 in part:
            got_in[tick - 1] = arrived[0]
        if tick - 3 in sent:
            got_out[tick - 3] = arrived[0] if arrived[1] is None else arrived[1]
        if tick - 2 in pair:
            got_across[tick - 2] = arrived[2]
        alike = entering is not None and tick - 2 in pair and entering.shape == pair[tick - 2].shape
        if alike and tick - 3 in sent and arrived[1] is None and arrived[0].shape == entering.shape:
            pair[tick - 1], sent[tick - 2], final[tick - 3] = combine(
                middle, part[tick - 1], arrived[0], pair[tick - 2], arrived[2], sent[tick - 3],
                entering,
            )
        else:
            if tick - 1 in part:
                pair[tick - 1] = added(part[tick - 1], got_in[tick - 1])
            if tick - 2 in pair:
                leaving = added(pair[tick - 2], got_across[tick - 2])
                sent[tick - 2] = jnp.where(middle, leaving, entering) if alike else leaving
            if tick - 3 in sent:
                final[tick - 3] = jnp.where(middle, sent[tick - 3], got_out[tick - 3])
        held = (pair.get(tick - 1), sent.get(tick - 2), final.get(tick - 3), state, token)
        crossing, leaving, swapping, state, token = lax.optimization_barrier(held)
        if crossing is not None:
            pair[tick - 1] = crossing
            got_across[tick - 1] = lax.ppermute(crossing, "dp", ACROSS)
        if leaving is not None:
            sent[tick - 2] = leaving
        if alike:
            got_in[tick] = got_out[tick - 2] = lax.ppermute(leaving, "dp", PAIRS)
        else:
            if entering is not None:
                got_in[tick] = lax.ppermute(entering, "dp", PAIRS if leaving is None else INWARD)
            if leaving is not None:
                got_out[tick - 2] = lax.ppermute(
                    leaving, "dp", PAIRS if entering is None else OUTWARD
                )
        if swapping is not None:
            final[tick - 3] = swapping
            got_half[tick - 3] = flip(swapping, "ctx", 1)
        if tick - 4 in final:
            theirs, token = lax.optimization_barrier((got_half[tick - 4], token))
            last_name, index = plan[tick - 4]
            grads[last_name].store(index, final[tick - 4], theirs)
            last_buffers = grads[last_name].buffers
        try:
            state = main.send(state)
        except StopIteration:
            state = ()
        if tick + 1 < count:
            name, index = plan[tick + 1]
            coming = sides[name] if coming is None else coming
            part[tick + 1] = grads[name].part(coming, index)

    gains = results["gains"].reshape(-1)
    grad_w_query, grad_w_key, grad_w_value = grads["in"].results()
    grad_gain_attn = gains[:D]
    grad_gain_ffn = gains[D : 2 * D]
    grad_gain_query = gains[2 * D : 2 * D + head_width]
    grad_gain_key = gains[2 * D + head_width :]
    return (
        out_tokens,
        results["tokens"],
        grad_w_query,
        grad_w_key,
        grad_w_value,
        grad_gain_query,
        grad_gain_key,
        *grads["out"].results(),
        grad_gain_attn,
        *grads["gate"].results(),
        *grads["up"].results(),
        *grads["down"].results(),
        grad_gain_ffn,
    )


def solution(mesh):
    in_specs = (
        P(("dp", "ctx", "seq"), None),
        P(None, "seq"),
        P(None, "seq"),
        P(None, "seq"),
        P("seq"),
        P("seq"),
        P("seq", None),
        P(),
        P(None, "seq"),
        P(None, "seq"),
        P("seq", None),
        P(),
        P(("dp", "ctx", "seq"), None),
        P("dp"),
        P(),
    )
    out_specs = (
        P(("dp", "ctx", "seq"), None),
        P(("dp", "ctx", "seq"), None),
        P(None, "seq"),
        P(None, "seq"),
        P(None, "seq"),
        P("seq"),
        P("seq"),
        P("seq", None),
        P(),
        P(None, "seq"),
        P(None, "seq"),
        P("seq", None),
        P(),
    )
    return jax.shard_map(body, mesh=mesh, in_specs=in_specs, out_specs=out_specs, check_vma=False)
```

```python
import functools

import jax
import jax.numpy as jnp
from jax import lax
from jax.experimental import pallas as pl
from jax.experimental.pallas import tpu as pltpu
from jax.sharding import PartitionSpec as P

D = 2048
HD = 128


EPS = 1e-06
STEP = 2
ROPE_BASE = 500000.0
NEG_FILL = -1e30
PAIRS = [(0, 1), (1, 0), (2, 3), (3, 2)]
INWARD = [(0, 1), (3, 2)]
OUTWARD = [(1, 0), (2, 3)]
ACROSS = [(1, 2), (2, 1)]


def flip(value, axis, distance):
    count = lax.axis_size(axis)
    return lax.ppermute(value, axis, [(place, place ^ distance) for place in range(count)])


def distances(axis):
    count = lax.axis_size(axis)
    found = []
    step = 1
    while step < count:
        found.append(step)
        step *= 2
    return found


def gather_rows(own, axis):
    parts = {0: own}
    for distance in reversed(distances(axis)):
        parts.update({o ^ distance: flip(block, axis, distance) for o, block in parts.items()})
    return [parts[o] for o in range(len(parts))]


def gather_both(own, axis, beside=None):
    mine, theirs = {0: own}, {0: flip(own, "ctx", 1)}
    for far, distance in enumerate(reversed(distances(axis))):
        for o in list(mine):
            mine[o ^ distance] = flip(mine[o], axis, distance)
            if far == 0 and distance > 1:
                rows = own.shape[0] // 2
                theirs[o ^ distance] = stacked(
                    [
                        flip(theirs[o][:rows], axis, distance),
                        flip(mine[o ^ distance][rows:], "ctx", 1),
                    ]
                )
                held = (mine[o ^ distance], beside)
                mine[o ^ distance], beside = lax.optimization_barrier(held)
            else:
                theirs[o ^ distance] = flip(theirs[o], axis, distance)
    blocks = range(len(mine))
    return [mine[o] for o in blocks], [theirs[o] for o in blocks], beside


def gather_beside(own, axis, beside):
    parts = {0: own}
    for distance in reversed(distances(axis)):
        parts.update({o ^ distance: flip(block, axis, distance) for o, block in parts.items()})
        if len(parts) == 2:
            held = (parts[distance], beside)
            parts[distance], beside = lax.optimization_barrier(held)
    return [parts[o] for o in range(len(parts))], beside


def stacked(blocks):
    return jnp.concatenate(blocks, axis=0)


def scatter_rows(blocks, axis):
    parts = dict(enumerate(blocks))
    for distance in distances(axis):
        kept = {o: block for o, block in parts.items() if not o & distance}
        for o in sorted(kept, reverse=True):
            sent = parts[o ^ distance].astype(jnp.bfloat16)
            kept[o] = kept[o] + flip(sent, axis, distance).astype(jnp.float32)
        parts = kept
    return parts[0]


def row_blocks(value, count):
    rows = value.shape[0] // count
    return [lax.slice_in_dim(value, o * rows, (o + 1) * rows, axis=0) for o in range(count)]


def norm_back(unit_val, inverse, grad_unit):
    return inverse * (grad_unit - unit_val * jnp.mean(grad_unit * unit_val, axis=-1, keepdims=True))


def contract_rows(left, right):
    return lax.dot_general(
        left, right, (((0,), (0,)), ((), ())), preferred_element_type=jnp.float32
    )


def times_transpose(left, right):
    return lax.dot_general(
        left, right, (((1,), (1,)), ((), ())), preferred_element_type=jnp.float32
    )


def half_columns(value, place):
    width = value.shape[1] // 2
    return lax.dynamic_slice_in_dim(value, place * width, width, axis=1)


def both_halves(value):
    place = lax.axis_index("ctx")
    return half_columns(value, place), flip(half_columns(value, 1 - place), "ctx", 1)


def turned(values, cosine, sine):
    return values * cosine + pltpu.roll(values, HD // 2, 1) * sine


def project_kernel(*refs, blocks, square, plain):
    rows_ref = refs[blocks + square + plain]
    outs = refs[blocks + square + plain + 1 :]
    weights = refs[blocks : blocks + square + plain]

    @pl.when(pl.program_id(0) == 0)
    def _():
        rows = refs[0].shape[0]
        for o in range(blocks):
            rows_ref[o * rows : (o + 1) * rows, :] = refs[o][...]
        for sum_ref in outs[square + plain :]:
            sum_ref[...] = jnp.zeros_like(sum_ref)

    for k in range(square + plain):
        product = jnp.dot(rows_ref[...], weights[k][...], preferred_element_type=jnp.float32)
        outs[k][...] = product.astype(outs[k].dtype)
        if k < square:
            outs[square + plain + k][...] += jnp.sum(product * product, axis=1, keepdims=True)


def project(blocks, square, plain):
    rows, depth = blocks[0].shape
    count = len(blocks)
    width = square[0].shape[1]
    wide = min(256, width)
    whole = pl.BlockSpec((count * rows, depth), lambda i: (0, 0))
    column = pl.BlockSpec((depth, wide), lambda i: (0, i))
    product = pl.BlockSpec((count * rows, wide), lambda i: (0, i))
    sums = pl.BlockSpec((count * rows, 1), lambda i: (0, 0))
    return pl.pallas_call(
        functools.partial(project_kernel, blocks=count, square=len(square), plain=len(plain)),
        grid=(width // wide,),
        in_specs=[pl.BlockSpec((rows, depth), lambda i: (0, 0))] * count
        + [column] * (len(square) + len(plain)),
        out_specs=[whole] + [product] * (len(square) + len(plain)) + [sums] * len(square),
        out_shape=[jax.ShapeDtypeStruct((count * rows, depth), jnp.bfloat16)]
        + [jax.ShapeDtypeStruct((count * rows, width), jnp.float32)] * len(square)
        + [jax.ShapeDtypeStruct((count * rows, width), jnp.bfloat16)] * len(plain)
        + [jax.ShapeDtypeStruct((count * rows, 1), jnp.float32)] * len(square),
        name="project",
    )(*blocks, *square, *plain)


def attend_kernel(
    query_ref, key_ref, key_other_ref, value_own_ref, value_other_ref,
    inv_query_ref, inv_key_ref, gain_query_ref, gain_key_ref,
    cos_query_ref, sin_query_ref, cos_key_ref, sin_key_ref, at_query_ref, at_key_ref,
    query_low_ref, key_low_ref, value_ref, mixed_ref, lse_ref,
):
    @pl.when(pl.program_id(1) == 0)
    def _():
        half = key_ref.shape[0]
        value_ref[:half] = value_own_ref[...]
        value_ref[half:] = value_other_ref[...]
        for side, ref in ((slice(0, half), key_ref), (slice(half, 2 * half), key_other_ref)):
            scaled = ref[...] * inv_key_ref[side] * gain_key_ref[...]
            key_low_ref[side] = turned(scaled, cos_key_ref[side], sin_key_ref[side]).astype(
                jnp.bfloat16
            )

    scaled = query_ref[...] * inv_query_ref[...] * gain_query_ref[...]
    query_low = turned(scaled, cos_query_ref[...], sin_query_ref[...]).astype(jnp.bfloat16)
    query_low_ref[...] = query_low
    scores = HD ** (-0.5) * times_transpose(query_low, key_low_ref[...])
    scores = jnp.where(at_key_ref[...] <= at_query_ref[...], scores, NEG_FILL)
    peak = jnp.max(scores, axis=1, keepdims=True)
    exps = jnp.exp(scores - peak)
    total = jnp.sum(exps, axis=1, keepdims=True)
    probs = (exps * (1.0 / total)).astype(jnp.bfloat16)
    mixed_ref[...] = jnp.dot(
        probs, value_ref[...], preferred_element_type=jnp.float32
    ).astype(jnp.bfloat16)
    lse_ref[0] = peak + jnp.log(total)


def attend_back_kernel(
    query_low_ref, key_low_ref, value_ref, grad_ref, lse_ref,
    cos_query_ref, sin_query_ref, cos_key_ref, sin_key_ref, at_query_ref, at_key_ref,
    grad_query_ref, grad_key_ref, grad_value_ref, prev_key_ref, prev_value_ref,
    key_sum, value_sum,
):
    scale = HD ** (-0.5)
    query_low = query_low_ref[...]
    key_low = key_low_ref[...]
    grad_low = grad_ref[...]
    scores = scale * times_transpose(query_low, key_low)
    allowed = at_key_ref[...] <= at_query_ref[...]
    probs = jnp.exp(jnp.where(allowed, scores, NEG_FILL) - lse_ref[0])
    grad_probs = times_transpose(grad_low, value_ref[...])
    delta = jnp.sum(probs * grad_probs, axis=1, keepdims=True)
    grad_scores = (probs * (grad_probs - delta)).astype(jnp.bfloat16)
    grad_query = scale * jnp.dot(grad_scores, key_low, preferred_element_type=jnp.float32)
    grad_query_ref[...] = turned(grad_query, cos_query_ref[...], -sin_query_ref[...])
    key_part = scale * contract_rows(grad_scores, query_low)
    value_part = contract_rows(probs.astype(jnp.bfloat16), grad_low)

    @pl.when(pl.program_id(1) == 0)
    def _():
        key_sum[...] = key_part
        value_sum[...] = value_part

    @pl.when(pl.program_id(1) > 0)
    def _():
        key_sum[...] += key_part
        value_sum[...] += value_part

    @pl.when(pl.program_id(1) == pl.num_programs(1) - 1)
    def _():
        half = key_sum.shape[0] // 2
        turned_back = turned(key_sum[...], cos_key_ref[...], -sin_key_ref[...])
        grad_key_ref[...] = turned_back[:half]
        prev_key_ref[...] = turned_back[half:].astype(jnp.bfloat16)
        grad_value_ref[...] = value_sum[:half]
        prev_value_ref[...] = value_sum[half:].astype(jnp.bfloat16)


def attention_specs(half_rows, key_rows, block_rows):
    spec = {
        "query": pl.BlockSpec((block_rows, HD), lambda h, i: (i, h)),
        "key": pl.BlockSpec((key_rows, HD), lambda h, i: (0, h)),
        "half": pl.BlockSpec((half_rows, HD), lambda h, i: (0, h)),
        "gain": pl.BlockSpec((1, HD), lambda h, i: (0, h)),
        "query_column": pl.BlockSpec((block_rows, 1), lambda h, i: (i, 0)),
        "key_column": pl.BlockSpec((key_rows, 1), lambda h, i: (0, 0)),
        "key_row": pl.BlockSpec((1, key_rows), lambda h, i: (0, 0)),
        "query_turn": pl.BlockSpec((block_rows, HD), lambda h, i: (i, 0)),
        "key_turn": pl.BlockSpec((key_rows, HD), lambda h, i: (0, 0)),
        "lse": pl.BlockSpec((1, block_rows, 1), lambda h, i: (h, i, 0)),
    }
    return spec


def attend(query, keys, values, inv_query, inv_key, gain_query, gain_key, turns, block_rows):
    half_rows, width = query.shape
    key_rows = 2 * half_rows
    heads = width // HD
    s = attention_specs(half_rows, key_rows, block_rows)
    return pl.pallas_call(
        attend_kernel,
        grid=(heads, half_rows // block_rows),
        in_specs=[
            s["query"], s["half"], s["half"], s["half"], s["half"],
            s["query_column"], s["key_column"], s["gain"], s["gain"],
            s["query_turn"], s["query_turn"], s["key_turn"], s["key_turn"],
            s["query_column"], s["key_row"],
        ],
        out_specs=[s["query"], s["key"], s["key"], s["query"], s["lse"]],
        out_shape=[
            jax.ShapeDtypeStruct(query.shape, jnp.bfloat16),
            jax.ShapeDtypeStruct((key_rows, width), jnp.bfloat16),
            jax.ShapeDtypeStruct((key_rows, width), jnp.bfloat16),
            jax.ShapeDtypeStruct(query.shape, jnp.bfloat16),
            jax.ShapeDtypeStruct((heads, half_rows, 1), jnp.float32),
        ],
        name="attend",
    )(query, *keys, *values, inv_query, inv_key, gain_query, gain_key, *turns)


def attend_back(query_low, key_low, value, grad, lse, turns, block_rows):
    half_rows, width = query_low.shape
    key_rows = key_low.shape[0]
    heads = width // HD
    s = attention_specs(half_rows, key_rows, block_rows)
    halves = (half_rows, width)
    return pl.pallas_call(
        attend_back_kernel,
        grid=(heads, half_rows // block_rows),
        in_specs=[
            s["query"], s["key"], s["key"], s["query"], s["lse"],
            s["query_turn"], s["query_turn"], s["key_turn"], s["key_turn"],
            s["query_column"], s["key_row"],
        ],
        out_specs=[s["query"], s["half"], s["half"], s["half"], s["half"]],
        out_shape=[
            jax.ShapeDtypeStruct(halves, jnp.float32),
            jax.ShapeDtypeStruct(halves, jnp.float32),
            jax.ShapeDtypeStruct(halves, jnp.float32),
            jax.ShapeDtypeStruct(halves, jnp.bfloat16),
            jax.ShapeDtypeStruct(halves, jnp.bfloat16),
        ],
        scratch_shapes=[
            pltpu.VMEM((key_rows, HD), jnp.float32),
            pltpu.VMEM((key_rows, HD), jnp.float32),
        ],
        name="attend_back",
    )(query_low, key_low, value, grad, lse, *turns)


def store_kernel(place_ref, mine_ref, theirs_ref, *refs, outs):
    width = mine_ref.shape[1] // outs
    for side, half_ref in enumerate((mine_ref, theirs_ref)):

        @pl.when(pl.program_id(0) == side)
        def _():
            for k, out_ref in enumerate(refs[-outs:]):
                out_ref[...] = half_ref[:, k * width : (k + 1) * width].astype(jnp.float32)


def store_chunk(buffers, mine, theirs, shapes, where_to):
    place = lax.axis_index("ctx").astype(jnp.int32).reshape(1)
    rows, columns = mine.shape
    outs = len(shapes)
    block = min(512, rows)
    steps = rows // block
    operands = [place, mine, theirs]
    in_specs = [
        pl.BlockSpec((block, columns), lambda i, r, p: (r * (1 - i) + (steps - 1) * i, 0)),
        pl.BlockSpec((block, columns), lambda i, r, p: (r * i, 0)),
    ]
    aliases = {}
    if buffers is not None:
        operands.extend(buffers)
        in_specs.extend([pl.BlockSpec(memory_space=pl.ANY)] * outs)
        aliases = {3 + k: k for k in range(outs)}

    def out_at(i, r, p):
        row, column = where_to(p[0] ^ i)
        return row * steps + r, column

    return pl.pallas_call(
        functools.partial(store_kernel, outs=outs),
        grid_spec=pltpu.PrefetchScalarGridSpec(
            num_scalar_prefetch=1,
            grid=(2, steps),
            in_specs=in_specs,
            out_specs=[pl.BlockSpec((block, columns // outs), out_at)] * outs,
        ),
        out_shape=[jax.ShapeDtypeStruct(shape, jnp.float32) for shape in shapes],
        input_output_aliases=aliases,
        name="store",
    )(*operands)


class Gradients:
    def __init__(self, shapes, row_chunks, column_chunks, by_rows):
        self.shapes, self.by_rows = shapes, by_rows
        self.row_chunks, self.column_chunks = row_chunks, column_chunks
        self.chunks = row_chunks * column_chunks
        self.buffers = None
        self.kept = []

    def part(self, sides, index):
        left, grad = sides
        row, column = divmod(index, self.column_chunks)
        rows, columns = left.shape[1] // self.row_chunks, grad.shape[1] // self.column_chunks
        left = lax.slice_in_dim(left, row * rows, (row + 1) * rows, axis=1)
        grad = lax.slice_in_dim(grad, column * columns, (column + 1) * columns, axis=1)
        return contract_rows(left, grad).astype(jnp.bfloat16)

    def store(self, index, mine, theirs):
        row, column = divmod(index, self.column_chunks)
        if (mine.shape[1] // len(self.shapes)) % 128:
            self.kept.append((mine, theirs))
            return
        if self.by_rows:
            where_to = lambda half: (half * self.row_chunks + row, column)
        else:
            where_to = lambda half: (row, half)
        self.buffers = store_chunk(self.buffers, mine, theirs, self.shapes, where_to)

    def results(self):
        if self.buffers is not None:
            return self.buffers
        first = lax.axis_index("ctx") == 0
        width = self.kept[0][0].shape[1] // len(self.shapes)
        found = []
        for k in range(len(self.shapes)):
            cut = lambda value: value[:, k * width : (k + 1) * width]
            pieces = [
                jnp.concatenate(
                    [
                        jnp.where(first, cut(mine), cut(theirs)),
                        jnp.where(first, cut(theirs), cut(mine)),
                    ],
                    axis=1,
                )
                for mine, theirs in self.kept
            ]
            found.append(jnp.concatenate(pieces, axis=0).astype(jnp.float32))
        return found


def added(left, right):
    return (left.astype(jnp.float32) + right.astype(jnp.float32)).astype(left.dtype)


def combine_kernel(
    middle_ref, part_ref, got_ref, pair_ref, across_ref, sent_ref, next_ref,
    pair_out_ref, sent_out_ref, final_out_ref,
):
    @pl.when(middle_ref[0] == 1)
    def _():
        pair_out_ref[...] = added(part_ref[...], got_ref[...])
        sent_out_ref[...] = added(pair_ref[...], across_ref[...])
        final_out_ref[...] = sent_ref[...]

    @pl.when(middle_ref[0] == 0)
    def _():
        pair_out_ref[...] = part_ref[...]
        sent_out_ref[...] = next_ref[...]
        final_out_ref[...] = got_ref[...]


def combine(middle, part, got, pair, across, sent, coming):
    rows, columns = part.shape
    block = min(256, rows)
    every = pl.BlockSpec((block, columns), lambda r, m: (r, 0))
    middles = pl.BlockSpec((block, columns), lambda r, m: (r * m[0], 0))
    ends = pl.BlockSpec((block, columns), lambda r, m: (r * (1 - m[0]), 0))
    return pl.pallas_call(
        combine_kernel,
        grid_spec=pltpu.PrefetchScalarGridSpec(
            num_scalar_prefetch=1,
            grid=(rows // block,),
            in_specs=[every, every, middles, middles, middles, ends],
            out_specs=[every] * 3,
        ),
        out_shape=[jax.ShapeDtypeStruct(part.shape, part.dtype)] * 3,
        name="combine",
    )(middle.astype(jnp.int32).reshape(1), part, got, pair, across, sent, coming)


def body(
    tokens,
    w_query,
    w_key,
    w_value,
    gain_query,
    gain_key,
    w_out,
    gain_attn,
    w_gate,
    w_up,
    w_down,
    gain_ffn,
    cotangent,
    source_ids,
    group_weights,
):
    seq_count = lax.axis_size("seq")
    seq_place = lax.axis_index("seq")
    ctx_place = lax.axis_index("ctx")
    dp_place = lax.axis_index("dp")
    middle = jnp.logical_or(dp_place == 1, dp_place == 2)
    tok_rows = tokens.shape[0]
    half_rows = tok_rows * seq_count
    head_width = w_query.shape[1]
    hidden_width = w_gate.shape[1]
    block_rows = min(512, half_rows) if half_rows <= 512 else 256
    owners = jnp.bitwise_xor(jnp.arange(seq_count, dtype=jnp.int32), seq_place)
    row_ids = (owners[:, None] * tok_rows + jnp.arange(tok_rows, dtype=jnp.int32)[None, :]).reshape(
        half_rows
    )
    at_query = (ctx_place * half_rows + row_ids).astype(jnp.float32)
    at_key = jnp.concatenate([at_query, ((1 - ctx_place) * half_rows + row_ids).astype(jnp.float32)])
    lane = jnp.arange(HD, dtype=jnp.int32)
    inverse = ROPE_BASE ** (-((lane % (HD // 2)).astype(jnp.float32) * 2.0 / HD))
    angles = at_key[:, None] * inverse[None, :]
    cosine = jnp.cos(angles)
    sine = jnp.sin(angles) * jnp.where(lane < HD // 2, -1.0, 1.0)[None, :]
    turns = (cosine, sine, cosine, sine, at_query[:, None], at_key[None, :])

    own_blocks, other_blocks, turns = gather_both(tokens, "seq", turns)
    tokens_own, query_proj, key_proj, value_own, sq_query, sq_key = project(
        own_blocks, (w_query, w_key), (w_value,)
    )
    tokens_other, key_other, value_other, sq_key_other = project(
        other_blocks, (w_key,), (w_value,)
    )

    def common_rows(parts):
        stacked = jnp.stack(parts).reshape(len(parts), seq_count, tok_rows)
        return jnp.take(stacked, owners, axis=1)

    def own_rows(sums):
        return jnp.take(sums, owners, axis=1).reshape(sums.shape[0], half_rows)

    sums = own_rows(lax.psum(common_rows((sq_query, sq_key, sq_key_other)), "seq"))
    inv_query = lax.rsqrt(sums[0] / D + EPS)[:, None]
    inv_key_both = lax.rsqrt(sums[1:].reshape(2 * half_rows) / D + EPS)[:, None]
    inv_key = inv_key_both[:half_rows]
    query_low, key_low, value_low, attn_low, lse = attend(
        query_proj, (key_proj, key_other), (value_own, value_other), inv_query, inv_key_both, gain_query[None, :],
        gain_key[None, :], turns, block_rows,
    )

    def to_owners(partial):
        return scatter_rows(row_blocks(partial, seq_count), "seq")

    attn_other = flip(attn_low, "ctx", 1)
    attn_proj = to_owners(jnp.dot(attn_low, w_out, preferred_element_type=jnp.float32))
    attn_proj, attn_other = lax.optimization_barrier((attn_proj, attn_other))
    inv_attn = lax.rsqrt(jnp.mean(attn_proj * attn_proj, axis=1, keepdims=True) + EPS)
    attn_unit = attn_proj * inv_attn
    hidden = tokens.astype(jnp.float32) + attn_unit * gain_attn
    hidden_low = hidden.astype(jnp.bfloat16)
    hidden_flip = flip(hidden_low, "ctx", 1)
    hidden_blocks, hidden_flip = gather_beside(hidden_low, "seq", hidden_flip)
    hidden_own = lax.optimization_barrier(stacked(hidden_blocks))
    hidden_rest = gather_rows(hidden_flip, "seq")
    gate_proj = jnp.dot(hidden_own, w_gate, preferred_element_type=jnp.float32)
    up_proj = jnp.dot(hidden_own, w_up, preferred_element_type=jnp.float32)
    gate_sig = jax.nn.sigmoid(gate_proj)
    swish = gate_proj * gate_sig
    inner_low = (swish * up_proj).astype(jnp.bfloat16)
    inner_low, hidden_rest = lax.optimization_barrier((inner_low, hidden_rest))
    inner_halves = both_halves(inner_low)
    ffn = to_owners(jnp.dot(inner_low, w_down, preferred_element_type=jnp.float32))
    ffn, inner_halves = lax.optimization_barrier((ffn, inner_halves))
    inv_ffn = lax.rsqrt(jnp.mean(ffn * ffn, axis=1, keepdims=True) + EPS)
    ffn_unit = ffn * inv_ffn
    out_tokens = (hidden + ffn_unit * gain_ffn).astype(jnp.bfloat16)
    picked = jnp.sum(
        jnp.where(
            jnp.arange(group_weights.shape[0], dtype=jnp.int32) == source_ids[0], group_weights, 0.0
        )
    )
    grad_out = cotangent.astype(jnp.float32) * picked
    gain_ffn_part = jnp.sum(grad_out * ffn_unit, axis=0)
    grad_ffn_low = norm_back(ffn_unit, inv_ffn, grad_out * gain_ffn).astype(jnp.bfloat16)
    grad_ffn_own, grad_ffn_other, _ = gather_both(grad_ffn_low, "seq")
    grad_ffn_both = stacked(grad_ffn_own + grad_ffn_other)

    grads = {
        "down": Gradients([w_down.shape], 2, 2, True),
        "gate": Gradients([w_gate.shape], 4, 1, False),
        "up": Gradients([w_up.shape], 4, 1, False),
        "out": Gradients([w_out.shape], 1, 1, False),
        "in": Gradients([w_query.shape, w_key.shape, w_value.shape], 4, 1, False),
    }
    sides = {"down": (stacked(inner_halves), grad_ffn_both)}
    results = {}

    def stages():
        (grad_ffn,) = yield (grad_ffn_both[:half_rows],)
        grad_inner = times_transpose(grad_ffn, w_down)
        grad_gate = (grad_inner * up_proj * gate_sig * (1.0 + gate_proj * (1.0 - gate_sig))).astype(
            jnp.bfloat16
        )
        grad_up = (grad_inner * swish).astype(jnp.bfloat16)
        grad_gate, grad_up = yield (grad_gate, grad_up)
        gate_halves = both_halves(grad_gate)
        up_halves = both_halves(grad_up)
        gate_share = times_transpose(grad_gate, w_gate)
        gate_share, gate_halves = yield (gate_share, gate_halves)
        hidden_both = stacked([hidden_own] + hidden_rest)
        sides["gate"] = (hidden_both, stacked(gate_halves))
        partial = gate_share + times_transpose(grad_up, w_up)
        (partial,) = yield (partial,)
        grad_hidden = grad_out + to_owners(partial)
        grad_hidden, up_halves = yield (grad_hidden, up_halves)
        sides["up"] = (hidden_both, stacked(up_halves))
        gain_attn_part = jnp.sum(grad_hidden * attn_unit, axis=0)
        grad_proj_low = norm_back(attn_unit, inv_attn, grad_hidden * gain_attn).astype(jnp.bfloat16)
        grad_proj_own = stacked(gather_rows(grad_proj_low, "seq"))
        (grad_proj_own,) = yield (grad_proj_own,)
        proj_halves = both_halves(grad_proj_own)
        grad_attn_low = times_transpose(grad_proj_own, w_out).astype(jnp.bfloat16)
        backs = attend_back(query_low, key_low, value_low, grad_attn_low, lse, turns, block_rows)
        backs = yield backs
        grad_query_norm, own_dk, own_dv, prev_dk, prev_dv = backs
        back_dk, back_dv = lax.ppermute((prev_dk, prev_dv), "ctx", [(1, 0)])
        grad_query_norm, own_dk, own_dv, back_dk, back_dv, proj_halves = yield (
            grad_query_norm, own_dk, own_dv, back_dk, back_dv, proj_halves
        )
        sides["out"] = (stacked([attn_low, attn_other]), stacked(proj_halves))
        grad_value_low = (own_dv + back_dv.astype(jnp.float32)).astype(jnp.bfloat16)
        grad_key_norm = own_dk + back_dk.astype(jnp.float32)
        query_unit = query_proj * inv_query
        key_unit = key_proj * inv_key
        gain_query_part = jnp.sum(grad_query_norm * query_unit, axis=0)
        gain_key_part = jnp.sum(grad_key_norm * key_unit, axis=0)
        query_scaled = grad_query_norm * gain_query
        key_scaled = grad_key_norm * gain_key
        dots, gain_sums = lax.psum(
            (
                common_rows(
                    (
                        jnp.sum(query_scaled * query_unit, axis=1),
                        jnp.sum(key_scaled * key_unit, axis=1),
                    )
                ),
                jnp.concatenate([gain_attn_part, gain_ffn_part]),
            ),
            "seq",
        )
        dots_query, dots_key = own_rows(dots)
        grad_query_low = (
            inv_query * (query_scaled - query_unit * (dots_query / D)[:, None])
        ).astype(jnp.bfloat16)
        grad_key_low = (inv_key * (key_scaled - key_unit * (dots_key / D)[:, None])).astype(
            jnp.bfloat16
        )
        gains = jnp.concatenate([gain_sums, gain_query_part, gain_key_part]).reshape(-1, 128)
        grad_value_low, grad_key_low, grad_query_low, gains = yield (
            grad_value_low, grad_key_low, grad_query_low, gains
        )
        lows = (grad_query_low, grad_key_low, grad_value_low)
        mine = jnp.concatenate([half_columns(low, ctx_place) for low in lows], axis=1)
        given = jnp.concatenate([half_columns(low, 1 - ctx_place) for low in lows], axis=1)
        theirs = flip(given, "ctx", 1)
        gains_other = flip(gains, "ctx", 1)
        partial = (
            times_transpose(grad_query_low, w_query)
            + times_transpose(grad_key_low, w_key)
            + times_transpose(grad_value_low, w_value)
        )
        partial, gains, gains_other = yield (partial, gains, gains_other)
        gains = gains + gains_other
        gains_pair = lax.ppermute(gains, "dp", PAIRS)
        grad_tokens = grad_hidden + to_owners(partial)
        grad_tokens, gains, gains_pair, theirs = yield (grad_tokens, gains, gains_pair, theirs)
        sides["in"] = (stacked([tokens_own, tokens_other]), stacked([mine, theirs]))
        results["tokens"] = grad_tokens
        gains = gains + gains_pair
        gains_across = lax.ppermute(gains, "dp", ACROSS)
        gains, gains_across = yield (gains, gains_across)
        gains = gains + gains_across
        gains_out = lax.ppermute(gains, "dp", PAIRS)
        gains, gains_out = yield (gains, gains_out)
        results["gains"] = jnp.where(middle, gains, gains_out)

    plan = [(name, index) for name in grads for index in range(grads[name].chunks)]
    count = len(plan)
    part, pair, sent, final = {}, {}, {}, {}
    got_in, got_across, got_out, got_half = {}, {}, {}, {}
    main = stages()
    state = next(main)
    last_name, last_buffers = None, None
    token = picked
    part[0] = grads[plan[0][0]].part(sides[plan[0][0]], 0)

    for tick in range(count + 4 * STEP + 1):
        coming = sides.get(plan[tick + 1][0]) if tick + 1 < count else None
        arrived = (got_in.get(tick - STEP), got_out.get(tick - 3 * STEP), got_across.get(tick - 2 * STEP))
        if tick - STEP in got_in and got_in[tick - STEP] is arrived[1]:
            arrived = (arrived[0], None, arrived[2])
        held = (arrived, part.get(tick), state, coming, last_buffers, token)
        arrived, entering, state, coming, last_buffers, token = lax.optimization_barrier(held)
        if last_name:
            grads[last_name].buffers = last_buffers
        if entering is not None:
            part[tick] = entering
        if tick - STEP in part:
            got_in[tick - STEP] = arrived[0]
        if tick - 3 * STEP in sent:
            got_out[tick - 3 * STEP] = arrived[0] if arrived[1] is None else arrived[1]
        if tick - 2 * STEP in pair:
            got_across[tick - 2 * STEP] = arrived[2]
        alike = entering is not None and tick - 2 * STEP in pair and entering.shape == pair[tick - 2 * STEP].shape
        if alike and tick - 3 * STEP in sent and arrived[1] is None and arrived[0].shape == entering.shape:
            pair[tick - STEP], sent[tick - 2 * STEP], final[tick - 3 * STEP] = combine(
                middle, part[tick - STEP], arrived[0], pair[tick - 2 * STEP], arrived[2], sent[tick - 3 * STEP],
                entering,
            )
        else:
            if tick - STEP in part:
                pair[tick - STEP] = added(part[tick - STEP], got_in[tick - STEP])
            if tick - 2 * STEP in pair:
                leaving = added(pair[tick - 2 * STEP], got_across[tick - 2 * STEP])
                sent[tick - 2 * STEP] = jnp.where(middle, leaving, entering) if alike else leaving
            if tick - 3 * STEP in sent:
                final[tick - 3 * STEP] = jnp.where(middle, sent[tick - 3 * STEP], got_out[tick - 3 * STEP])
        held = (pair.get(tick - STEP), sent.get(tick - 2 * STEP), final.get(tick - 3 * STEP), state, token)
        crossing, leaving, swapping, state, token = lax.optimization_barrier(held)
        if crossing is not None:
            pair[tick - STEP] = crossing
            got_across[tick - STEP] = lax.ppermute(crossing, "dp", ACROSS)
        if leaving is not None:
            sent[tick - 2 * STEP] = leaving
        if alike:
            got_in[tick] = got_out[tick - 2 * STEP] = lax.ppermute(leaving, "dp", PAIRS)
        else:
            if entering is not None:
                got_in[tick] = lax.ppermute(entering, "dp", PAIRS if leaving is None else INWARD)
            if leaving is not None:
                got_out[tick - 2 * STEP] = lax.ppermute(
                    leaving, "dp", PAIRS if entering is None else OUTWARD
                )
        if swapping is not None:
            final[tick - 3 * STEP] = swapping
            got_half[tick - 3 * STEP] = flip(swapping, "ctx", 1)
        if tick - 4 * STEP in final:
            theirs, token = lax.optimization_barrier((got_half[tick - 4 * STEP], token))
            last_name, index = plan[tick - 4 * STEP]
            grads[last_name].store(index, final[tick - 4 * STEP], theirs)
            last_buffers = grads[last_name].buffers
        try:
            state = main.send(state)
        except StopIteration:
            state = ()
        if tick + 1 < count:
            name, index = plan[tick + 1]
            coming = sides[name] if coming is None else coming
            part[tick + 1] = grads[name].part(coming, index)

    gains = results["gains"].reshape(-1)
    grad_w_query, grad_w_key, grad_w_value = grads["in"].results()
    grad_gain_attn = gains[:D]
    grad_gain_ffn = gains[D : 2 * D]
    grad_gain_query = gains[2 * D : 2 * D + head_width]
    grad_gain_key = gains[2 * D + head_width :]
    return (
        out_tokens,
        results["tokens"],
        grad_w_query,
        grad_w_key,
        grad_w_value,
        grad_gain_query,
        grad_gain_key,
        *grads["out"].results(),
        grad_gain_attn,
        *grads["gate"].results(),
        *grads["up"].results(),
        *grads["down"].results(),
        grad_gain_ffn,
    )


def solution(mesh):
    in_specs = (
        P(("dp", "ctx", "seq"), None),
        P(None, "seq"),
        P(None, "seq"),
        P(None, "seq"),
        P("seq"),
        P("seq"),
        P("seq", None),
        P(),
        P(None, "seq"),
        P(None, "seq"),
        P("seq", None),
        P(),
        P(("dp", "ctx", "seq"), None),
        P("dp"),
        P(),
    )
    out_specs = (
        P(("dp", "ctx", "seq"), None),
        P(("dp", "ctx", "seq"), None),
        P(None, "seq"),
        P(None, "seq"),
        P(None, "seq"),
        P("seq"),
        P("seq"),
        P("seq", None),
        P(),
        P(None, "seq"),
        P(None, "seq"),
        P("seq", None),
        P(),
    )
    return jax.shard_map(body, mesh=mesh, in_specs=in_specs, out_specs=out_specs, check_vma=False)
```

```python
import functools

import jax
import jax.numpy as jnp
from jax import lax
from jax.experimental import pallas as pl
from jax.experimental.pallas import tpu as pltpu
from jax.sharding import PartitionSpec as P

D = 2048
HD = 128


EPS = 1e-06
STEP = 2
ROPE_BASE = 500000.0
NEG_FILL = -1e30
PAIRS = [(0, 1), (1, 0), (2, 3), (3, 2)]
INWARD = [(0, 1), (3, 2)]
OUTWARD = [(1, 0), (2, 3)]
ACROSS = [(1, 2), (2, 1)]


def flip(value, axis, distance):
    count = lax.axis_size(axis)
    return lax.ppermute(value, axis, [(place, place ^ distance) for place in range(count)])


def distances(axis):
    count = lax.axis_size(axis)
    found = []
    step = 1
    while step < count:
        found.append(step)
        step *= 2
    return found


def gather_rows(own, axis):
    parts = {0: own}
    for distance in reversed(distances(axis)):
        parts.update({o ^ distance: flip(block, axis, distance) for o, block in parts.items()})
    return [parts[o] for o in range(len(parts))]


def gather_both(own, axis, beside=None):
    mine, theirs = {0: own}, {0: flip(own, "ctx", 1)}
    for far, distance in enumerate(reversed(distances(axis))):
        for o in list(mine):
            mine[o ^ distance] = flip(mine[o], axis, distance)
            if far == 0 and distance > 1:
                rows = own.shape[0] // 2
                theirs[o ^ distance] = stacked(
                    [
                        flip(theirs[o][:rows], axis, distance),
                        flip(mine[o ^ distance][rows:], "ctx", 1),
                    ]
                )
                held = (mine[o ^ distance], beside)
                mine[o ^ distance], beside = lax.optimization_barrier(held)
            else:
                theirs[o ^ distance] = flip(theirs[o], axis, distance)
    blocks = range(len(mine))
    return [mine[o] for o in blocks], [theirs[o] for o in blocks], beside


def gather_beside(own, axis, beside):
    parts = {0: own}
    for distance in reversed(distances(axis)):
        parts.update({o ^ distance: flip(block, axis, distance) for o, block in parts.items()})
        if len(parts) == 2:
            held = (parts[distance], beside)
            parts[distance], beside = lax.optimization_barrier(held)
    return [parts[o] for o in range(len(parts))], beside


def stacked(blocks):
    return jnp.concatenate(blocks, axis=0)


def scatter_rows(blocks, axis):
    parts = dict(enumerate(blocks))
    for distance in distances(axis):
        kept = {o: block for o, block in parts.items() if not o & distance}
        for o in sorted(kept, reverse=True):
            sent = parts[o ^ distance].astype(jnp.bfloat16)
            kept[o] = kept[o] + flip(sent, axis, distance).astype(jnp.float32)
        parts = kept
    return parts[0]


def row_blocks(value, count):
    rows = value.shape[0] // count
    return [lax.slice_in_dim(value, o * rows, (o + 1) * rows, axis=0) for o in range(count)]


def norm_back(unit_val, inverse, grad_unit):
    return inverse * (grad_unit - unit_val * jnp.mean(grad_unit * unit_val, axis=-1, keepdims=True))


def contract_rows(left, right):
    return lax.dot_general(
        left, right, (((0,), (0,)), ((), ())), preferred_element_type=jnp.float32
    )


def times_transpose(left, right):
    return lax.dot_general(
        left, right, (((1,), (1,)), ((), ())), preferred_element_type=jnp.float32
    )


def half_columns(value, place):
    width = value.shape[1] // 2
    return lax.dynamic_slice_in_dim(value, place * width, width, axis=1)


def both_halves(value):
    place = lax.axis_index("ctx")
    return half_columns(value, place), flip(half_columns(value, 1 - place), "ctx", 1)


def turned(values, cosine, sine):
    return values * cosine + pltpu.roll(values, HD // 2, 1) * sine


def project_kernel(*refs, blocks, square, plain):
    rows_ref = refs[blocks + square + plain]
    outs = refs[blocks + square + plain + 1 :]
    weights = refs[blocks : blocks + square + plain]

    @pl.when(pl.program_id(0) == 0)
    def _():
        rows = refs[0].shape[0]
        for o in range(blocks):
            rows_ref[o * rows : (o + 1) * rows, :] = refs[o][...]
        for sum_ref in outs[square + plain :]:
            sum_ref[...] = jnp.zeros_like(sum_ref)

    for k in range(square + plain):
        product = jnp.dot(rows_ref[...], weights[k][...], preferred_element_type=jnp.float32)
        outs[k][...] = product.astype(outs[k].dtype)
        if k < square:
            outs[square + plain + k][...] += jnp.sum(product * product, axis=1, keepdims=True)


def project(blocks, square, plain):
    rows, depth = blocks[0].shape
    count = len(blocks)
    width = square[0].shape[1]
    wide = min(256, width)
    whole = pl.BlockSpec((count * rows, depth), lambda i: (0, 0))
    column = pl.BlockSpec((depth, wide), lambda i: (0, i))
    product = pl.BlockSpec((count * rows, wide), lambda i: (0, i))
    sums = pl.BlockSpec((count * rows, 1), lambda i: (0, 0))
    return pl.pallas_call(
        functools.partial(project_kernel, blocks=count, square=len(square), plain=len(plain)),
        grid=(width // wide,),
        in_specs=[pl.BlockSpec((rows, depth), lambda i: (0, 0))] * count
        + [column] * (len(square) + len(plain)),
        out_specs=[whole] + [product] * (len(square) + len(plain)) + [sums] * len(square),
        out_shape=[jax.ShapeDtypeStruct((count * rows, depth), jnp.bfloat16)]
        + [jax.ShapeDtypeStruct((count * rows, width), jnp.float32)] * len(square)
        + [jax.ShapeDtypeStruct((count * rows, width), jnp.bfloat16)] * len(plain)
        + [jax.ShapeDtypeStruct((count * rows, 1), jnp.float32)] * len(square),
        name="project",
    )(*blocks, *square, *plain)


def attend_kernel(
    query_ref, key_ref, key_other_ref, value_own_ref, value_other_ref,
    inv_query_ref, inv_key_ref, gain_query_ref, gain_key_ref,
    cos_query_ref, sin_query_ref, cos_key_ref, sin_key_ref, at_query_ref, at_key_ref,
    query_low_ref, key_low_ref, value_ref, mixed_ref, lse_ref,
):
    @pl.when(pl.program_id(1) == 0)
    def _():
        half = key_ref.shape[0]
        value_ref[:half] = value_own_ref[...]
        value_ref[half:] = value_other_ref[...]
        for side, ref in ((slice(0, half), key_ref), (slice(half, 2 * half), key_other_ref)):
            scaled = ref[...] * inv_key_ref[side] * gain_key_ref[...]
            key_low_ref[side] = turned(scaled, cos_key_ref[side], sin_key_ref[side]).astype(
                jnp.bfloat16
            )

    scaled = query_ref[...] * inv_query_ref[...] * gain_query_ref[...]
    query_low = turned(scaled, cos_query_ref[...], sin_query_ref[...]).astype(jnp.bfloat16)
    query_low_ref[...] = query_low
    scores = HD ** (-0.5) * times_transpose(query_low, key_low_ref[...])
    scores = jnp.where(at_key_ref[...] <= at_query_ref[...], scores, NEG_FILL)
    peak = jnp.max(scores, axis=1, keepdims=True)
    exps = jnp.exp(scores - peak)
    total = jnp.sum(exps, axis=1, keepdims=True)
    probs = (exps * (1.0 / total)).astype(jnp.bfloat16)
    mixed_ref[...] = jnp.dot(
        probs, value_ref[...], preferred_element_type=jnp.float32
    ).astype(jnp.bfloat16)
    lse_ref[0] = peak + jnp.log(total)


def attend_back_kernel(
    query_low_ref, key_low_ref, value_ref, grad_ref, lse_ref,
    cos_query_ref, sin_query_ref, cos_key_ref, sin_key_ref, at_query_ref, at_key_ref,
    grad_query_ref, grad_key_ref, grad_value_ref, prev_key_ref, prev_value_ref,
    key_sum, value_sum,
):
    scale = HD ** (-0.5)
    query_low = query_low_ref[...]
    key_low = key_low_ref[...]
    grad_low = grad_ref[...]
    scores = scale * times_transpose(query_low, key_low)
    allowed = at_key_ref[...] <= at_query_ref[...]
    probs = jnp.exp(jnp.where(allowed, scores, NEG_FILL) - lse_ref[0])
    grad_probs = times_transpose(grad_low, value_ref[...])
    delta = jnp.sum(probs * grad_probs, axis=1, keepdims=True)
    grad_scores = (probs * (grad_probs - delta)).astype(jnp.bfloat16)
    grad_query = scale * jnp.dot(grad_scores, key_low, preferred_element_type=jnp.float32)
    grad_query_ref[...] = turned(grad_query, cos_query_ref[...], -sin_query_ref[...])
    key_part = scale * contract_rows(grad_scores, query_low)
    value_part = contract_rows(probs.astype(jnp.bfloat16), grad_low)

    @pl.when(pl.program_id(1) == 0)
    def _():
        key_sum[...] = key_part
        value_sum[...] = value_part

    @pl.when(pl.program_id(1) > 0)
    def _():
        key_sum[...] += key_part
        value_sum[...] += value_part

    @pl.when(pl.program_id(1) == pl.num_programs(1) - 1)
    def _():
        half = key_sum.shape[0] // 2
        turned_back = turned(key_sum[...], cos_key_ref[...], -sin_key_ref[...])
        grad_key_ref[...] = turned_back[:half]
        prev_key_ref[...] = turned_back[half:].astype(jnp.bfloat16)
        grad_value_ref[...] = value_sum[:half]
        prev_value_ref[...] = value_sum[half:].astype(jnp.bfloat16)


def attention_specs(half_rows, key_rows, block_rows):
    spec = {
        "query": pl.BlockSpec((block_rows, HD), lambda h, i: (i, h)),
        "key": pl.BlockSpec((key_rows, HD), lambda h, i: (0, h)),
        "half": pl.BlockSpec((half_rows, HD), lambda h, i: (0, h)),
        "gain": pl.BlockSpec((1, HD), lambda h, i: (0, h)),
        "query_column": pl.BlockSpec((block_rows, 1), lambda h, i: (i, 0)),
        "key_column": pl.BlockSpec((key_rows, 1), lambda h, i: (0, 0)),
        "key_row": pl.BlockSpec((1, key_rows), lambda h, i: (0, 0)),
        "query_turn": pl.BlockSpec((block_rows, HD), lambda h, i: (i, 0)),
        "key_turn": pl.BlockSpec((key_rows, HD), lambda h, i: (0, 0)),
        "lse": pl.BlockSpec((1, block_rows, 1), lambda h, i: (h, i, 0)),
    }
    return spec


def attend(query, keys, values, inv_query, inv_key, gain_query, gain_key, turns, block_rows):
    half_rows, width = query.shape
    key_rows = 2 * half_rows
    heads = width // HD
    s = attention_specs(half_rows, key_rows, block_rows)
    return pl.pallas_call(
        attend_kernel,
        grid=(heads, half_rows // block_rows),
        in_specs=[
            s["query"], s["half"], s["half"], s["half"], s["half"],
            s["query_column"], s["key_column"], s["gain"], s["gain"],
            s["query_turn"], s["query_turn"], s["key_turn"], s["key_turn"],
            s["query_column"], s["key_row"],
        ],
        out_specs=[s["query"], s["key"], s["key"], s["query"], s["lse"]],
        out_shape=[
            jax.ShapeDtypeStruct(query.shape, jnp.bfloat16),
            jax.ShapeDtypeStruct((key_rows, width), jnp.bfloat16),
            jax.ShapeDtypeStruct((key_rows, width), jnp.bfloat16),
            jax.ShapeDtypeStruct(query.shape, jnp.bfloat16),
            jax.ShapeDtypeStruct((heads, half_rows, 1), jnp.float32),
        ],
        name="attend",
    )(query, *keys, *values, inv_query, inv_key, gain_query, gain_key, *turns)


def attend_back(query_low, key_low, value, grad, lse, turns, block_rows):
    half_rows, width = query_low.shape
    key_rows = key_low.shape[0]
    heads = width // HD
    s = attention_specs(half_rows, key_rows, block_rows)
    halves = (half_rows, width)
    return pl.pallas_call(
        attend_back_kernel,
        grid=(heads, half_rows // block_rows),
        in_specs=[
            s["query"], s["key"], s["key"], s["query"], s["lse"],
            s["query_turn"], s["query_turn"], s["key_turn"], s["key_turn"],
            s["query_column"], s["key_row"],
        ],
        out_specs=[s["query"], s["half"], s["half"], s["half"], s["half"]],
        out_shape=[
            jax.ShapeDtypeStruct(halves, jnp.float32),
            jax.ShapeDtypeStruct(halves, jnp.float32),
            jax.ShapeDtypeStruct(halves, jnp.float32),
            jax.ShapeDtypeStruct(halves, jnp.bfloat16),
            jax.ShapeDtypeStruct(halves, jnp.bfloat16),
        ],
        scratch_shapes=[
            pltpu.VMEM((key_rows, HD), jnp.float32),
            pltpu.VMEM((key_rows, HD), jnp.float32),
        ],
        name="attend_back",
    )(query_low, key_low, value, grad, lse, *turns)


def store_kernel(place_ref, mine_ref, theirs_ref, *refs, outs):
    width = mine_ref.shape[1] // outs
    for side, half_ref in enumerate((mine_ref, theirs_ref)):

        @pl.when(pl.program_id(0) == side)
        def _():
            for k, out_ref in enumerate(refs[-outs:]):
                out_ref[...] = half_ref[:, k * width : (k + 1) * width].astype(jnp.float32)


def store_chunk(buffers, mine, theirs, shapes, where_to):
    place = lax.axis_index("ctx").astype(jnp.int32).reshape(1)
    rows, columns = mine.shape
    outs = len(shapes)
    block = min(512, rows)
    steps = rows // block
    operands = [place, mine, theirs]
    in_specs = [
        pl.BlockSpec((block, columns), lambda i, r, p: (r * (1 - i) + (steps - 1) * i, 0)),
        pl.BlockSpec((block, columns), lambda i, r, p: (r * i, 0)),
    ]
    aliases = {}
    if buffers is not None:
        operands.extend(buffers)
        in_specs.extend([pl.BlockSpec(memory_space=pl.ANY)] * outs)
        aliases = {3 + k: k for k in range(outs)}

    def out_at(i, r, p):
        row, column = where_to(p[0] ^ i)
        return row * steps + r, column

    return pl.pallas_call(
        functools.partial(store_kernel, outs=outs),
        grid_spec=pltpu.PrefetchScalarGridSpec(
            num_scalar_prefetch=1,
            grid=(2, steps),
            in_specs=in_specs,
            out_specs=[pl.BlockSpec((block, columns // outs), out_at)] * outs,
        ),
        out_shape=[jax.ShapeDtypeStruct(shape, jnp.float32) for shape in shapes],
        input_output_aliases=aliases,
        name="store",
    )(*operands)


class Gradients:
    def __init__(self, shapes, row_chunks, column_chunks, by_rows):
        self.shapes, self.by_rows = shapes, by_rows
        self.row_chunks, self.column_chunks = row_chunks, column_chunks
        self.chunks = row_chunks * column_chunks
        self.buffers = None
        self.kept = []

    def part(self, sides, index):
        left, grad = sides
        row, column = divmod(index, self.column_chunks)
        rows, columns = left.shape[1] // self.row_chunks, grad.shape[1] // self.column_chunks
        left = lax.slice_in_dim(left, row * rows, (row + 1) * rows, axis=1)
        grad = lax.slice_in_dim(grad, column * columns, (column + 1) * columns, axis=1)
        return contract_rows(left, grad).astype(jnp.bfloat16)

    def store(self, index, mine, theirs):
        row, column = divmod(index, self.column_chunks)
        if (mine.shape[1] // len(self.shapes)) % 128:
            self.kept.append((mine, theirs))
            return
        if self.by_rows:
            where_to = lambda half: (half * self.row_chunks + row, column)
        else:
            where_to = lambda half: (row, half)
        self.buffers = store_chunk(self.buffers, mine, theirs, self.shapes, where_to)

    def results(self):
        if self.buffers is not None:
            return self.buffers
        first = lax.axis_index("ctx") == 0
        width = self.kept[0][0].shape[1] // len(self.shapes)
        found = []
        for k in range(len(self.shapes)):
            cut = lambda value: value[:, k * width : (k + 1) * width]
            pieces = [
                jnp.concatenate(
                    [
                        jnp.where(first, cut(mine), cut(theirs)),
                        jnp.where(first, cut(theirs), cut(mine)),
                    ],
                    axis=1,
                )
                for mine, theirs in self.kept
            ]
            found.append(jnp.concatenate(pieces, axis=0).astype(jnp.float32))
        return found


def added(left, right):
    return (left.astype(jnp.float32) + right.astype(jnp.float32)).astype(left.dtype)


def combine_kernel(
    middle_ref, part_ref, got_ref, pair_ref, across_ref, sent_ref, next_ref,
    pair_out_ref, sent_out_ref, final_out_ref,
):
    @pl.when(middle_ref[0] == 1)
    def _():
        pair_out_ref[...] = added(part_ref[...], got_ref[...])
        sent_out_ref[...] = added(pair_ref[...], across_ref[...])
        final_out_ref[...] = sent_ref[...]

    @pl.when(middle_ref[0] == 0)
    def _():
        pair_out_ref[...] = part_ref[...]
        sent_out_ref[...] = next_ref[...]
        final_out_ref[...] = got_ref[...]


def combine(middle, part, got, pair, across, sent, coming):
    rows, columns = part.shape
    block = min(256, rows)
    every = pl.BlockSpec((block, columns), lambda r, m: (r, 0))
    middles = pl.BlockSpec((block, columns), lambda r, m: (r * m[0], 0))
    ends = pl.BlockSpec((block, columns), lambda r, m: (r * (1 - m[0]), 0))
    return pl.pallas_call(
        combine_kernel,
        grid_spec=pltpu.PrefetchScalarGridSpec(
            num_scalar_prefetch=1,
            grid=(rows // block,),
            in_specs=[every, every, middles, middles, middles, ends],
            out_specs=[every] * 3,
        ),
        out_shape=[jax.ShapeDtypeStruct(part.shape, part.dtype)] * 3,
        name="combine",
    )(middle.astype(jnp.int32).reshape(1), part, got, pair, across, sent, coming)


def body(
    tokens,
    w_query,
    w_key,
    w_value,
    gain_query,
    gain_key,
    w_out,
    gain_attn,
    w_gate,
    w_up,
    w_down,
    gain_ffn,
    cotangent,
    source_ids,
    group_weights,
):
    seq_count = lax.axis_size("seq")
    seq_place = lax.axis_index("seq")
    ctx_place = lax.axis_index("ctx")
    dp_place = lax.axis_index("dp")
    middle = jnp.logical_or(dp_place == 1, dp_place == 2)
    tok_rows = tokens.shape[0]
    half_rows = tok_rows * seq_count
    head_width = w_query.shape[1]
    hidden_width = w_gate.shape[1]
    block_rows = min(512, half_rows) if half_rows <= 512 else 256
    owners = jnp.bitwise_xor(jnp.arange(seq_count, dtype=jnp.int32), seq_place)
    row_ids = (owners[:, None] * tok_rows + jnp.arange(tok_rows, dtype=jnp.int32)[None, :]).reshape(
        half_rows
    )
    at_query = (ctx_place * half_rows + row_ids).astype(jnp.float32)
    at_key = jnp.concatenate([at_query, ((1 - ctx_place) * half_rows + row_ids).astype(jnp.float32)])
    lane = jnp.arange(HD, dtype=jnp.int32)
    inverse = ROPE_BASE ** (-((lane % (HD // 2)).astype(jnp.float32) * 2.0 / HD))
    angles = at_key[:, None] * inverse[None, :]
    cosine = jnp.cos(angles)
    sine = jnp.sin(angles) * jnp.where(lane < HD // 2, -1.0, 1.0)[None, :]
    turns = (cosine, sine, cosine, sine, at_query[:, None], at_key[None, :])

    own_blocks, other_blocks, turns = gather_both(tokens, "seq", turns)
    tokens_own, query_proj, key_proj, value_own, sq_query, sq_key = project(
        own_blocks, (w_query, w_key), (w_value,)
    )
    tokens_other, key_other, value_other, sq_key_other = project(
        other_blocks, (w_key,), (w_value,)
    )

    def common_rows(parts):
        stacked = jnp.stack(parts).reshape(len(parts), seq_count, tok_rows)
        return jnp.take(stacked, owners, axis=1)

    def own_rows(sums):
        return jnp.take(sums, owners, axis=1).reshape(sums.shape[0], half_rows)

    sums = own_rows(lax.psum(common_rows((sq_query, sq_key, sq_key_other)), "seq"))
    inv_query = lax.rsqrt(sums[0] / D + EPS)[:, None]
    inv_key_both = lax.rsqrt(sums[1:].reshape(2 * half_rows) / D + EPS)[:, None]
    inv_key = inv_key_both[:half_rows]
    query_low, key_low, value_low, attn_low, lse = attend(
        query_proj, (key_proj, key_other), (value_own, value_other), inv_query, inv_key_both, gain_query[None, :],
        gain_key[None, :], turns, block_rows,
    )

    def to_owners(partial):
        return scatter_rows(row_blocks(partial, seq_count), "seq")

    attn_other = flip(attn_low, "ctx", 1)
    attn_proj = to_owners(jnp.dot(attn_low, w_out, preferred_element_type=jnp.float32))
    attn_proj, attn_other = lax.optimization_barrier((attn_proj, attn_other))
    inv_attn = lax.rsqrt(jnp.mean(attn_proj * attn_proj, axis=1, keepdims=True) + EPS)
    attn_unit = attn_proj * inv_attn
    hidden = tokens.astype(jnp.float32) + attn_unit * gain_attn
    hidden_low = hidden.astype(jnp.bfloat16)
    hidden_flip = flip(hidden_low, "ctx", 1)
    hidden_blocks, hidden_flip = gather_beside(hidden_low, "seq", hidden_flip)
    hidden_own = lax.optimization_barrier(stacked(hidden_blocks))
    hidden_rest = gather_rows(hidden_flip, "seq")
    gate_proj = jnp.dot(hidden_own, w_gate, preferred_element_type=jnp.float32)
    up_proj = jnp.dot(hidden_own, w_up, preferred_element_type=jnp.float32)
    gate_sig = jax.nn.sigmoid(gate_proj)
    swish = gate_proj * gate_sig
    inner_low = (swish * up_proj).astype(jnp.bfloat16)
    inner_low, hidden_rest = lax.optimization_barrier((inner_low, hidden_rest))
    inner_halves = both_halves(inner_low)
    ffn = to_owners(jnp.dot(inner_low, w_down, preferred_element_type=jnp.float32))
    ffn, inner_halves = lax.optimization_barrier((ffn, inner_halves))
    inv_ffn = lax.rsqrt(jnp.mean(ffn * ffn, axis=1, keepdims=True) + EPS)
    ffn_unit = ffn * inv_ffn
    out_tokens = (hidden + ffn_unit * gain_ffn).astype(jnp.bfloat16)
    picked = jnp.sum(
        jnp.where(
            jnp.arange(group_weights.shape[0], dtype=jnp.int32) == source_ids[0], group_weights, 0.0
        )
    )
    grad_out = cotangent.astype(jnp.float32) * picked
    gain_ffn_part = jnp.sum(grad_out * ffn_unit, axis=0)
    grad_ffn_low = norm_back(ffn_unit, inv_ffn, grad_out * gain_ffn).astype(jnp.bfloat16)
    grad_ffn_own, grad_ffn_other, _ = gather_both(grad_ffn_low, "seq")
    grad_ffn_both = stacked(grad_ffn_own + grad_ffn_other)

    grads = {
        "down": Gradients([w_down.shape], 2, 2, True),
        "gate": Gradients([w_gate.shape], 4, 1, False),
        "up": Gradients([w_up.shape], 4, 1, False),
        "out": Gradients([w_out.shape], 1, 1, False),
        "in": Gradients([w_query.shape, w_key.shape, w_value.shape], 4, 1, False),
    }
    sides = {"down": (stacked(inner_halves), grad_ffn_both)}
    results = {}

    def stages():
        (grad_ffn,) = yield (grad_ffn_both[:half_rows],)
        grad_inner = times_transpose(grad_ffn, w_down)
        grad_gate = (grad_inner * up_proj * gate_sig * (1.0 + gate_proj * (1.0 - gate_sig))).astype(
            jnp.bfloat16
        )
        grad_up = (grad_inner * swish).astype(jnp.bfloat16)
        grad_gate, grad_up = yield (grad_gate, grad_up)
        gate_halves = both_halves(grad_gate)
        up_halves = both_halves(grad_up)
        gate_share = times_transpose(grad_gate, w_gate)
        gate_share, gate_halves = yield (gate_share, gate_halves)
        hidden_both = stacked([hidden_own] + hidden_rest)
        sides["gate"] = (hidden_both, stacked(gate_halves))
        partial = gate_share + times_transpose(grad_up, w_up)
        (partial,) = yield (partial,)
        grad_hidden = grad_out + to_owners(partial)
        grad_hidden, up_halves = yield (grad_hidden, up_halves)
        sides["up"] = (hidden_both, stacked(up_halves))
        gain_attn_part = jnp.sum(grad_hidden * attn_unit, axis=0)
        grad_proj_low = norm_back(attn_unit, inv_attn, grad_hidden * gain_attn).astype(jnp.bfloat16)
        grad_proj_own = stacked(gather_rows(grad_proj_low, "seq"))
        (grad_proj_own,) = yield (grad_proj_own,)
        proj_halves = both_halves(grad_proj_own)
        grad_attn_low = times_transpose(grad_proj_own, w_out).astype(jnp.bfloat16)
        backs = attend_back(query_low, key_low, value_low, grad_attn_low, lse, turns, block_rows)
        backs = yield backs
        grad_query_norm, own_dk, own_dv, prev_dk, prev_dv = backs
        back_dk, back_dv = lax.ppermute((prev_dk, prev_dv), "ctx", [(1, 0)])
        grad_query_norm, own_dk, own_dv, back_dk, back_dv, proj_halves = yield (
            grad_query_norm, own_dk, own_dv, back_dk, back_dv, proj_halves
        )
        sides["out"] = (stacked([attn_low, attn_other]), stacked(proj_halves))
        grad_value_low = (own_dv + back_dv.astype(jnp.float32)).astype(jnp.bfloat16)
        grad_key_norm = own_dk + back_dk.astype(jnp.float32)
        query_unit = query_proj * inv_query
        key_unit = key_proj * inv_key
        gain_query_part = jnp.sum(grad_query_norm * query_unit, axis=0)
        gain_key_part = jnp.sum(grad_key_norm * key_unit, axis=0)
        query_scaled = grad_query_norm * gain_query
        key_scaled = grad_key_norm * gain_key
        dots, gain_sums = lax.psum(
            (
                common_rows(
                    (
                        jnp.sum(query_scaled * query_unit, axis=1),
                        jnp.sum(key_scaled * key_unit, axis=1),
                    )
                ),
                jnp.concatenate([gain_attn_part, gain_ffn_part]),
            ),
            "seq",
        )
        dots_query, dots_key = own_rows(dots)
        grad_query_low = (
            inv_query * (query_scaled - query_unit * (dots_query / D)[:, None])
        ).astype(jnp.bfloat16)
        grad_key_low = (inv_key * (key_scaled - key_unit * (dots_key / D)[:, None])).astype(
            jnp.bfloat16
        )
        gains = jnp.concatenate([gain_sums, gain_query_part, gain_key_part]).reshape(-1, 128)
        grad_value_low, grad_key_low, grad_query_low, gains = yield (
            grad_value_low, grad_key_low, grad_query_low, gains
        )
        lows = (grad_query_low, grad_key_low, grad_value_low)
        mine = jnp.concatenate([half_columns(low, ctx_place) for low in lows], axis=1)
        given = jnp.concatenate([half_columns(low, 1 - ctx_place) for low in lows], axis=1)
        theirs = flip(given, "ctx", 1)
        gains_other = flip(gains, "ctx", 1)
        partial = (
            times_transpose(grad_query_low, w_query)
            + times_transpose(grad_key_low, w_key)
            + times_transpose(grad_value_low, w_value)
        )
        partial, gains, gains_other = yield (partial, gains, gains_other)
        gains = gains + gains_other
        gains_pair = lax.ppermute(gains, "dp", PAIRS)
        grad_tokens = grad_hidden + to_owners(partial)
        grad_tokens, gains, gains_pair, theirs = yield (grad_tokens, gains, gains_pair, theirs)
        sides["in"] = (stacked([tokens_own, tokens_other]), stacked([mine, theirs]))
        results["tokens"] = grad_tokens
        gains = gains + gains_pair
        gains_across = lax.ppermute(gains, "dp", ACROSS)
        gains, gains_across = yield (gains, gains_across)
        gains = gains + gains_across
        gains_out = lax.ppermute(gains, "dp", PAIRS)
        gains, gains_out = yield (gains, gains_out)
        results["gains"] = jnp.where(middle, gains, gains_out)

    plan = [(name, index) for name in grads for index in range(grads[name].chunks)]
    count = len(plan)
    part, pair, sent, final = {}, {}, {}, {}
    got_in, got_across, got_out, got_half = {}, {}, {}, {}
    main = stages()
    state = next(main)
    last_name, last_buffers = None, None
    token = picked
    part[0] = grads[plan[0][0]].part(sides[plan[0][0]], 0)

    for tick in range(count + 4 * STEP + 1):
        coming = sides.get(plan[tick + 1][0]) if tick + 1 < count else None
        arrived = (got_in.get(tick - STEP), got_out.get(tick - 3 * STEP), got_across.get(tick - 2 * STEP))
        if tick - STEP in got_in and got_in[tick - STEP] is arrived[1]:
            arrived = (arrived[0], None, arrived[2])
        held = (arrived, part.get(tick), coming, last_buffers, token)
        arrived, entering, coming, last_buffers, token = lax.optimization_barrier(held)
        if last_name:
            grads[last_name].buffers = last_buffers
        if entering is not None:
            part[tick] = entering
        if tick - STEP in part:
            got_in[tick - STEP] = arrived[0]
        if tick - 3 * STEP in sent:
            got_out[tick - 3 * STEP] = arrived[0] if arrived[1] is None else arrived[1]
        if tick - 2 * STEP in pair:
            got_across[tick - 2 * STEP] = arrived[2]
        alike = entering is not None and tick - 2 * STEP in pair and entering.shape == pair[tick - 2 * STEP].shape
        if alike and tick - 3 * STEP in sent and arrived[1] is None and arrived[0].shape == entering.shape:
            pair[tick - STEP], sent[tick - 2 * STEP], final[tick - 3 * STEP] = combine(
                middle, part[tick - STEP], arrived[0], pair[tick - 2 * STEP], arrived[2], sent[tick - 3 * STEP],
                entering,
            )
        else:
            if tick - STEP in part:
                pair[tick - STEP] = added(part[tick - STEP], got_in[tick - STEP])
            if tick - 2 * STEP in pair:
                leaving = added(pair[tick - 2 * STEP], got_across[tick - 2 * STEP])
                sent[tick - 2 * STEP] = jnp.where(middle, leaving, entering) if alike else leaving
            if tick - 3 * STEP in sent:
                final[tick - 3 * STEP] = jnp.where(middle, sent[tick - 3 * STEP], got_out[tick - 3 * STEP])
        held = (pair.get(tick - STEP), sent.get(tick - 2 * STEP), final.get(tick - 3 * STEP), state, token)
        crossing, leaving, swapping, state, token = lax.optimization_barrier(held)
        if crossing is not None:
            pair[tick - STEP] = crossing
            got_across[tick - STEP] = lax.ppermute(crossing, "dp", ACROSS)
        if leaving is not None:
            sent[tick - 2 * STEP] = leaving
        if alike:
            got_in[tick] = got_out[tick - 2 * STEP] = lax.ppermute(leaving, "dp", PAIRS)
        else:
            if entering is not None:
                got_in[tick] = lax.ppermute(entering, "dp", PAIRS if leaving is None else INWARD)
            if leaving is not None:
                got_out[tick - 2 * STEP] = lax.ppermute(
                    leaving, "dp", PAIRS if entering is None else OUTWARD
                )
        if swapping is not None:
            final[tick - 3 * STEP] = swapping
            got_half[tick - 3 * STEP] = flip(swapping, "ctx", 1)
        if tick - 4 * STEP in final:
            theirs, token = lax.optimization_barrier((got_half[tick - 4 * STEP], token))
            last_name, index = plan[tick - 4 * STEP]
            grads[last_name].store(index, final[tick - 4 * STEP], theirs)
            last_buffers = grads[last_name].buffers
        try:
            state = main.send(state)
        except StopIteration:
            state = ()
        if tick + 1 < count:
            name, index = plan[tick + 1]
            coming = sides[name] if coming is None else coming
            part[tick + 1] = grads[name].part(coming, index)

    gains = results["gains"].reshape(-1)
    grad_w_query, grad_w_key, grad_w_value = grads["in"].results()
    grad_gain_attn = gains[:D]
    grad_gain_ffn = gains[D : 2 * D]
    grad_gain_query = gains[2 * D : 2 * D + head_width]
    grad_gain_key = gains[2 * D + head_width :]
    return (
        out_tokens,
        results["tokens"],
        grad_w_query,
        grad_w_key,
        grad_w_value,
        grad_gain_query,
        grad_gain_key,
        *grads["out"].results(),
        grad_gain_attn,
        *grads["gate"].results(),
        *grads["up"].results(),
        *grads["down"].results(),
        grad_gain_ffn,
    )


def solution(mesh):
    in_specs = (
        P(("dp", "ctx", "seq"), None),
        P(None, "seq"),
        P(None, "seq"),
        P(None, "seq"),
        P("seq"),
        P("seq"),
        P("seq", None),
        P(),
        P(None, "seq"),
        P(None, "seq"),
        P("seq", None),
        P(),
        P(("dp", "ctx", "seq"), None),
        P("dp"),
        P(),
    )
    out_specs = (
        P(("dp", "ctx", "seq"), None),
        P(("dp", "ctx", "seq"), None),
        P(None, "seq"),
        P(None, "seq"),
        P(None, "seq"),
        P("seq"),
        P("seq"),
        P("seq", None),
        P(),
        P(None, "seq"),
        P(None, "seq"),
        P("seq", None),
        P(),
    )
    return jax.shard_map(body, mesh=mesh, in_specs=in_specs, out_specs=out_specs, check_vma=False)
```

```python
import functools

import jax
import jax.numpy as jnp
from jax import lax
from jax.experimental import pallas as pl
from jax.experimental.pallas import tpu as pltpu
from jax.sharding import PartitionSpec as P

D = 2048
HD = 128


EPS = 1e-06
STEP = 2
ROPE_BASE = 500000.0
NEG_FILL = -1e30
PAIRS = [(0, 1), (1, 0), (2, 3), (3, 2)]
INWARD = [(0, 1), (3, 2)]
OUTWARD = [(1, 0), (2, 3)]
ACROSS = [(1, 2), (2, 1)]


def flip(value, axis, distance):
    count = lax.axis_size(axis)
    return lax.ppermute(value, axis, [(place, place ^ distance) for place in range(count)])


def distances(axis):
    count = lax.axis_size(axis)
    found = []
    step = 1
    while step < count:
        found.append(step)
        step *= 2
    return found


def gather_rows(own, axis):
    parts = {0: own}
    for distance in reversed(distances(axis)):
        parts.update({o ^ distance: flip(block, axis, distance) for o, block in parts.items()})
    return [parts[o] for o in range(len(parts))]


def gather_both(own, axis, beside=None):
    mine, theirs = {0: own}, {0: flip(own, "ctx", 1)}
    for far, distance in enumerate(reversed(distances(axis))):
        for o in list(mine):
            mine[o ^ distance] = flip(mine[o], axis, distance)
            if far == 0 and distance > 1:
                rows = own.shape[0] // 2
                theirs[o ^ distance] = stacked(
                    [
                        flip(theirs[o][:rows], axis, distance),
                        flip(mine[o ^ distance][rows:], "ctx", 1),
                    ]
                )
                held = (mine[o ^ distance], beside)
                mine[o ^ distance], beside = lax.optimization_barrier(held)
            else:
                theirs[o ^ distance] = flip(theirs[o], axis, distance)
    blocks = range(len(mine))
    return [mine[o] for o in blocks], [theirs[o] for o in blocks], beside


def gather_beside(own, axis, beside):
    parts = {0: own}
    for distance in reversed(distances(axis)):
        parts.update({o ^ distance: flip(block, axis, distance) for o, block in parts.items()})
        if len(parts) == 2:
            held = (parts[distance], beside)
            parts[distance], beside = lax.optimization_barrier(held)
    return [parts[o] for o in range(len(parts))], beside


def stacked(blocks):
    return jnp.concatenate(blocks, axis=0)


def scatter_rows(blocks, axis):
    parts = dict(enumerate(blocks))
    for distance in distances(axis):
        kept = {o: block for o, block in parts.items() if not o & distance}
        for o in sorted(kept, reverse=True):
            sent = parts[o ^ distance].astype(jnp.bfloat16)
            kept[o] = kept[o] + flip(sent, axis, distance).astype(jnp.float32)
        parts = kept
    return parts[0]


def row_blocks(value, count):
    rows = value.shape[0] // count
    return [lax.slice_in_dim(value, o * rows, (o + 1) * rows, axis=0) for o in range(count)]


def norm_back(unit_val, inverse, grad_unit):
    return inverse * (grad_unit - unit_val * jnp.mean(grad_unit * unit_val, axis=-1, keepdims=True))


def contract_rows(left, right):
    return lax.dot_general(
        left, right, (((0,), (0,)), ((), ())), preferred_element_type=jnp.float32
    )


def times_transpose(left, right):
    return lax.dot_general(
        left, right, (((1,), (1,)), ((), ())), preferred_element_type=jnp.float32
    )


def half_columns(value, place):
    width = value.shape[1] // 2
    return lax.dynamic_slice_in_dim(value, place * width, width, axis=1)


def both_halves(value):
    place = lax.axis_index("ctx")
    return half_columns(value, place), flip(half_columns(value, 1 - place), "ctx", 1)


def turned(values, cosine, sine):
    return values * cosine + pltpu.roll(values, HD // 2, 1) * sine


def project_kernel(*refs, blocks, square, plain):
    rows_ref = refs[blocks + square + plain]
    outs = refs[blocks + square + plain + 1 :]
    weights = refs[blocks : blocks + square + plain]

    @pl.when(pl.program_id(0) == 0)
    def _():
        rows = refs[0].shape[0]
        for o in range(blocks):
            rows_ref[o * rows : (o + 1) * rows, :] = refs[o][...]
        for sum_ref in outs[square + plain :]:
            sum_ref[...] = jnp.zeros_like(sum_ref)

    for k in range(square + plain):
        product = jnp.dot(rows_ref[...], weights[k][...], preferred_element_type=jnp.float32)
        outs[k][...] = product.astype(outs[k].dtype)
        if k < square:
            outs[square + plain + k][...] += jnp.sum(product * product, axis=1, keepdims=True)


def project(blocks, square, plain):
    rows, depth = blocks[0].shape
    count = len(blocks)
    width = square[0].shape[1]
    wide = min(256, width)
    whole = pl.BlockSpec((count * rows, depth), lambda i: (0, 0))
    column = pl.BlockSpec((depth, wide), lambda i: (0, i))
    product = pl.BlockSpec((count * rows, wide), lambda i: (0, i))
    sums = pl.BlockSpec((count * rows, 1), lambda i: (0, 0))
    return pl.pallas_call(
        functools.partial(project_kernel, blocks=count, square=len(square), plain=len(plain)),
        grid=(width // wide,),
        in_specs=[pl.BlockSpec((rows, depth), lambda i: (0, 0))] * count
        + [column] * (len(square) + len(plain)),
        out_specs=[whole] + [product] * (len(square) + len(plain)) + [sums] * len(square),
        out_shape=[jax.ShapeDtypeStruct((count * rows, depth), jnp.bfloat16)]
        + [jax.ShapeDtypeStruct((count * rows, width), jnp.float32)] * len(square)
        + [jax.ShapeDtypeStruct((count * rows, width), jnp.bfloat16)] * len(plain)
        + [jax.ShapeDtypeStruct((count * rows, 1), jnp.float32)] * len(square),
        name="project",
    )(*blocks, *square, *plain)


def attend_kernel(
    query_ref, key_ref, key_other_ref, value_own_ref, value_other_ref,
    inv_query_ref, inv_key_ref, gain_query_ref, gain_key_ref,
    cos_query_ref, sin_query_ref, cos_key_ref, sin_key_ref, at_query_ref, at_key_ref,
    query_low_ref, key_low_ref, value_ref, mixed_ref, lse_ref,
):
    @pl.when(pl.program_id(1) == 0)
    def _():
        half = key_ref.shape[0]
        value_ref[:half] = value_own_ref[...]
        value_ref[half:] = value_other_ref[...]
        for side, ref in ((slice(0, half), key_ref), (slice(half, 2 * half), key_other_ref)):
            scaled = ref[...] * inv_key_ref[side] * gain_key_ref[...]
            key_low_ref[side] = turned(scaled, cos_key_ref[side], sin_key_ref[side]).astype(
                jnp.bfloat16
            )

    scaled = query_ref[...] * inv_query_ref[...] * gain_query_ref[...]
    query_low = turned(scaled, cos_query_ref[...], sin_query_ref[...]).astype(jnp.bfloat16)
    query_low_ref[...] = query_low
    scores = HD ** (-0.5) * times_transpose(query_low, key_low_ref[...])
    scores = jnp.where(at_key_ref[...] <= at_query_ref[...], scores, NEG_FILL)
    peak = jnp.max(scores, axis=1, keepdims=True)
    exps = jnp.exp(scores - peak)
    total = jnp.sum(exps, axis=1, keepdims=True)
    probs = (exps * (1.0 / total)).astype(jnp.bfloat16)
    mixed_ref[...] = jnp.dot(
        probs, value_ref[...], preferred_element_type=jnp.float32
    ).astype(jnp.bfloat16)
    lse_ref[0] = peak + jnp.log(total)


def attend_back_kernel(
    query_low_ref, key_low_ref, value_ref, grad_ref, lse_ref,
    cos_query_ref, sin_query_ref, cos_key_ref, sin_key_ref, at_query_ref, at_key_ref,
    grad_query_ref, grad_key_ref, grad_value_ref, prev_key_ref, prev_value_ref,
    key_sum, value_sum,
):
    scale = HD ** (-0.5)
    query_low = query_low_ref[...]
    key_low = key_low_ref[...]
    grad_low = grad_ref[...]
    scores = scale * times_transpose(query_low, key_low)
    allowed = at_key_ref[...] <= at_query_ref[...]
    probs = jnp.exp(jnp.where(allowed, scores, NEG_FILL) - lse_ref[0])
    grad_probs = times_transpose(grad_low, value_ref[...])
    delta = jnp.sum(probs * grad_probs, axis=1, keepdims=True)
    grad_scores = (probs * (grad_probs - delta)).astype(jnp.bfloat16)
    grad_query = scale * jnp.dot(grad_scores, key_low, preferred_element_type=jnp.float32)
    grad_query_ref[...] = turned(grad_query, cos_query_ref[...], -sin_query_ref[...])
    key_part = scale * contract_rows(grad_scores, query_low)
    value_part = contract_rows(probs.astype(jnp.bfloat16), grad_low)

    @pl.when(pl.program_id(1) == 0)
    def _():
        key_sum[...] = key_part
        value_sum[...] = value_part

    @pl.when(pl.program_id(1) > 0)
    def _():
        key_sum[...] += key_part
        value_sum[...] += value_part

    @pl.when(pl.program_id(1) == pl.num_programs(1) - 1)
    def _():
        half = key_sum.shape[0] // 2
        turned_back = turned(key_sum[...], cos_key_ref[...], -sin_key_ref[...])
        grad_key_ref[...] = turned_back[:half]
        prev_key_ref[...] = turned_back[half:].astype(jnp.bfloat16)
        grad_value_ref[...] = value_sum[:half]
        prev_value_ref[...] = value_sum[half:].astype(jnp.bfloat16)


def attention_specs(half_rows, key_rows, block_rows):
    spec = {
        "query": pl.BlockSpec((block_rows, HD), lambda h, i: (i, h)),
        "key": pl.BlockSpec((key_rows, HD), lambda h, i: (0, h)),
        "half": pl.BlockSpec((half_rows, HD), lambda h, i: (0, h)),
        "gain": pl.BlockSpec((1, HD), lambda h, i: (0, h)),
        "query_column": pl.BlockSpec((block_rows, 1), lambda h, i: (i, 0)),
        "key_column": pl.BlockSpec((key_rows, 1), lambda h, i: (0, 0)),
        "key_row": pl.BlockSpec((1, key_rows), lambda h, i: (0, 0)),
        "query_turn": pl.BlockSpec((block_rows, HD), lambda h, i: (i, 0)),
        "key_turn": pl.BlockSpec((key_rows, HD), lambda h, i: (0, 0)),
        "lse": pl.BlockSpec((1, block_rows, 1), lambda h, i: (h, i, 0)),
    }
    return spec


def attend(query, keys, values, inv_query, inv_key, gain_query, gain_key, turns, block_rows):
    half_rows, width = query.shape
    key_rows = 2 * half_rows
    heads = width // HD
    s = attention_specs(half_rows, key_rows, block_rows)
    return pl.pallas_call(
        attend_kernel,
        grid=(heads, half_rows // block_rows),
        in_specs=[
            s["query"], s["half"], s["half"], s["half"], s["half"],
            s["query_column"], s["key_column"], s["gain"], s["gain"],
            s["query_turn"], s["query_turn"], s["key_turn"], s["key_turn"],
            s["query_column"], s["key_row"],
        ],
        out_specs=[s["query"], s["key"], s["key"], s["query"], s["lse"]],
        out_shape=[
            jax.ShapeDtypeStruct(query.shape, jnp.bfloat16),
            jax.ShapeDtypeStruct((key_rows, width), jnp.bfloat16),
            jax.ShapeDtypeStruct((key_rows, width), jnp.bfloat16),
            jax.ShapeDtypeStruct(query.shape, jnp.bfloat16),
            jax.ShapeDtypeStruct((heads, half_rows, 1), jnp.float32),
        ],
        name="attend",
    )(query, *keys, *values, inv_query, inv_key, gain_query, gain_key, *turns)


def attend_back(query_low, key_low, value, grad, lse, turns, block_rows):
    half_rows, width = query_low.shape
    key_rows = key_low.shape[0]
    heads = width // HD
    s = attention_specs(half_rows, key_rows, block_rows)
    halves = (half_rows, width)
    return pl.pallas_call(
        attend_back_kernel,
        grid=(heads, half_rows // block_rows),
        in_specs=[
            s["query"], s["key"], s["key"], s["query"], s["lse"],
            s["query_turn"], s["query_turn"], s["key_turn"], s["key_turn"],
            s["query_column"], s["key_row"],
        ],
        out_specs=[s["query"], s["half"], s["half"], s["half"], s["half"]],
        out_shape=[
            jax.ShapeDtypeStruct(halves, jnp.float32),
            jax.ShapeDtypeStruct(halves, jnp.float32),
            jax.ShapeDtypeStruct(halves, jnp.float32),
            jax.ShapeDtypeStruct(halves, jnp.bfloat16),
            jax.ShapeDtypeStruct(halves, jnp.bfloat16),
        ],
        scratch_shapes=[
            pltpu.VMEM((key_rows, HD), jnp.float32),
            pltpu.VMEM((key_rows, HD), jnp.float32),
        ],
        name="attend_back",
    )(query_low, key_low, value, grad, lse, *turns)


def store_kernel(place_ref, mine_ref, theirs_ref, *refs, outs):
    width = mine_ref.shape[1] // outs
    for side, half_ref in enumerate((mine_ref, theirs_ref)):

        @pl.when(pl.program_id(0) == side)
        def _():
            for k, out_ref in enumerate(refs[-outs:]):
                out_ref[...] = half_ref[:, k * width : (k + 1) * width].astype(jnp.float32)


def store_chunk(buffers, mine, theirs, shapes, where_to):
    place = lax.axis_index("ctx").astype(jnp.int32).reshape(1)
    rows, columns = mine.shape
    outs = len(shapes)
    block = min(512, rows)
    steps = rows // block
    operands = [place, mine, theirs]
    in_specs = [
        pl.BlockSpec((block, columns), lambda i, r, p: (r * (1 - i) + (steps - 1) * i, 0)),
        pl.BlockSpec((block, columns), lambda i, r, p: (r * i, 0)),
    ]
    aliases = {}
    if buffers is not None:
        operands.extend(buffers)
        in_specs.extend([pl.BlockSpec(memory_space=pl.ANY)] * outs)
        aliases = {3 + k: k for k in range(outs)}

    def out_at(i, r, p):
        row, column = where_to(p[0] ^ i)
        return row * steps + r, column

    return pl.pallas_call(
        functools.partial(store_kernel, outs=outs),
        grid_spec=pltpu.PrefetchScalarGridSpec(
            num_scalar_prefetch=1,
            grid=(2, steps),
            in_specs=in_specs,
            out_specs=[pl.BlockSpec((block, columns // outs), out_at)] * outs,
        ),
        out_shape=[jax.ShapeDtypeStruct(shape, jnp.float32) for shape in shapes],
        input_output_aliases=aliases,
        name="store",
    )(*operands)


class Gradients:
    def __init__(self, shapes, row_chunks, column_chunks, by_rows):
        self.shapes, self.by_rows = shapes, by_rows
        self.row_chunks, self.column_chunks = row_chunks, column_chunks
        self.chunks = row_chunks * column_chunks
        self.buffers = None
        self.kept = []

    def part(self, sides, index):
        left, grad = sides
        row, column = divmod(index, self.column_chunks)
        rows, columns = left.shape[1] // self.row_chunks, grad.shape[1] // self.column_chunks
        left = lax.slice_in_dim(left, row * rows, (row + 1) * rows, axis=1)
        grad = lax.slice_in_dim(grad, column * columns, (column + 1) * columns, axis=1)
        return contract_rows(left, grad).astype(jnp.bfloat16)

    def store(self, index, mine, theirs):
        row, column = divmod(index, self.column_chunks)
        if (mine.shape[1] // len(self.shapes)) % 128:
            self.kept.append((mine, theirs))
            return
        if self.by_rows:
            where_to = lambda half: (half * self.row_chunks + row, column)
        else:
            where_to = lambda half: (row, half)
        self.buffers = store_chunk(self.buffers, mine, theirs, self.shapes, where_to)

    def results(self):
        if self.buffers is not None:
            return self.buffers
        first = lax.axis_index("ctx") == 0
        width = self.kept[0][0].shape[1] // len(self.shapes)
        found = []
        for k in range(len(self.shapes)):
            cut = lambda value: value[:, k * width : (k + 1) * width]
            pieces = [
                jnp.concatenate(
                    [
                        jnp.where(first, cut(mine), cut(theirs)),
                        jnp.where(first, cut(theirs), cut(mine)),
                    ],
                    axis=1,
                )
                for mine, theirs in self.kept
            ]
            found.append(jnp.concatenate(pieces, axis=0).astype(jnp.float32))
        return found


def added(left, right):
    return (left.astype(jnp.float32) + right.astype(jnp.float32)).astype(left.dtype)


def combine_kernel(
    middle_ref, part_ref, got_ref, pair_ref, across_ref, sent_ref, next_ref,
    pair_out_ref, sent_out_ref, final_out_ref,
):
    @pl.when(middle_ref[0] == 1)
    def _():
        pair_out_ref[...] = added(part_ref[...], got_ref[...])
        sent_out_ref[...] = added(pair_ref[...], across_ref[...])
        final_out_ref[...] = sent_ref[...]

    @pl.when(middle_ref[0] == 0)
    def _():
        pair_out_ref[...] = part_ref[...]
        sent_out_ref[...] = next_ref[...]
        final_out_ref[...] = got_ref[...]


def combine(middle, part, got, pair, across, sent, coming):
    rows, columns = part.shape
    block = min(256, rows)
    every = pl.BlockSpec((block, columns), lambda r, m: (r, 0))
    middles = pl.BlockSpec((block, columns), lambda r, m: (r * m[0], 0))
    ends = pl.BlockSpec((block, columns), lambda r, m: (r * (1 - m[0]), 0))
    return pl.pallas_call(
        combine_kernel,
        grid_spec=pltpu.PrefetchScalarGridSpec(
            num_scalar_prefetch=1,
            grid=(rows // block,),
            in_specs=[every, every, middles, middles, middles, ends],
            out_specs=[every] * 3,
        ),
        out_shape=[jax.ShapeDtypeStruct(part.shape, part.dtype)] * 3,
        name="combine",
    )(middle.astype(jnp.int32).reshape(1), part, got, pair, across, sent, coming)


def body(
    tokens,
    w_query,
    w_key,
    w_value,
    gain_query,
    gain_key,
    w_out,
    gain_attn,
    w_gate,
    w_up,
    w_down,
    gain_ffn,
    cotangent,
    source_ids,
    group_weights,
):
    seq_count = lax.axis_size("seq")
    seq_place = lax.axis_index("seq")
    ctx_place = lax.axis_index("ctx")
    dp_place = lax.axis_index("dp")
    middle = jnp.logical_or(dp_place == 1, dp_place == 2)
    tok_rows = tokens.shape[0]
    half_rows = tok_rows * seq_count
    head_width = w_query.shape[1]
    hidden_width = w_gate.shape[1]
    block_rows = min(512, half_rows) if half_rows <= 512 else 256
    owners = jnp.bitwise_xor(jnp.arange(seq_count, dtype=jnp.int32), seq_place)
    row_ids = (owners[:, None] * tok_rows + jnp.arange(tok_rows, dtype=jnp.int32)[None, :]).reshape(
        half_rows
    )
    at_query = (ctx_place * half_rows + row_ids).astype(jnp.float32)
    at_key = jnp.concatenate([at_query, ((1 - ctx_place) * half_rows + row_ids).astype(jnp.float32)])
    lane = jnp.arange(HD, dtype=jnp.int32)
    inverse = ROPE_BASE ** (-((lane % (HD // 2)).astype(jnp.float32) * 2.0 / HD))
    angles = at_key[:, None] * inverse[None, :]
    cosine = jnp.cos(angles)
    sine = jnp.sin(angles) * jnp.where(lane < HD // 2, -1.0, 1.0)[None, :]
    turns = (cosine, sine, cosine, sine, at_query[:, None], at_key[None, :])

    own_blocks, other_blocks, turns = gather_both(tokens, "seq", turns)
    tokens_own, query_proj, key_proj, value_own, sq_query, sq_key = project(
        own_blocks, (w_query, w_key), (w_value,)
    )
    tokens_other, key_other, value_other, sq_key_other = project(
        other_blocks, (w_key,), (w_value,)
    )

    def common_rows(parts):
        stacked = jnp.stack(parts).reshape(len(parts), seq_count, tok_rows)
        return jnp.take(stacked, owners, axis=1)

    def own_rows(sums):
        return jnp.take(sums, owners, axis=1).reshape(sums.shape[0], half_rows)

    sums = own_rows(lax.psum(common_rows((sq_query, sq_key, sq_key_other)), "seq"))
    inv_query = lax.rsqrt(sums[0] / D + EPS)[:, None]
    inv_key_both = lax.rsqrt(sums[1:].reshape(2 * half_rows) / D + EPS)[:, None]
    inv_key = inv_key_both[:half_rows]
    query_low, key_low, value_low, attn_low, lse = attend(
        query_proj, (key_proj, key_other), (value_own, value_other), inv_query, inv_key_both, gain_query[None, :],
        gain_key[None, :], turns, block_rows,
    )

    def to_owners(partial):
        return scatter_rows(row_blocks(partial, seq_count), "seq")

    attn_other = flip(attn_low, "ctx", 1)
    attn_proj = to_owners(jnp.dot(attn_low, w_out, preferred_element_type=jnp.float32))
    attn_proj, attn_other = lax.optimization_barrier((attn_proj, attn_other))
    inv_attn = lax.rsqrt(jnp.mean(attn_proj * attn_proj, axis=1, keepdims=True) + EPS)
    attn_unit = attn_proj * inv_attn
    hidden = tokens.astype(jnp.float32) + attn_unit * gain_attn
    hidden_low = hidden.astype(jnp.bfloat16)
    hidden_flip = flip(hidden_low, "ctx", 1)
    hidden_blocks, hidden_flip = gather_beside(hidden_low, "seq", hidden_flip)
    hidden_own = lax.optimization_barrier(stacked(hidden_blocks))
    hidden_rest = gather_rows(hidden_flip, "seq")
    gate_proj = jnp.dot(hidden_own, w_gate, preferred_element_type=jnp.float32)
    up_proj = jnp.dot(hidden_own, w_up, preferred_element_type=jnp.float32)
    gate_sig = jax.nn.sigmoid(gate_proj)
    swish = gate_proj * gate_sig
    inner_low = (swish * up_proj).astype(jnp.bfloat16)
    inner_low, hidden_rest = lax.optimization_barrier((inner_low, hidden_rest))
    inner_given = row_blocks(half_columns(inner_low, 1 - ctx_place), 2)
    inner_first = flip(inner_given[0], "ctx", 1)
    inner_second = flip(inner_given[1], "ctx", 1)
    ffn = to_owners(jnp.dot(inner_low, w_down, preferred_element_type=jnp.float32))
    ffn, inner_first = lax.optimization_barrier((ffn, inner_first))
    inv_ffn = lax.rsqrt(jnp.mean(ffn * ffn, axis=1, keepdims=True) + EPS)
    ffn_unit = ffn * inv_ffn
    out_tokens = (hidden + ffn_unit * gain_ffn).astype(jnp.bfloat16)
    picked = jnp.sum(
        jnp.where(
            jnp.arange(group_weights.shape[0], dtype=jnp.int32) == source_ids[0], group_weights, 0.0
        )
    )
    grad_out = cotangent.astype(jnp.float32) * picked
    gain_ffn_part = jnp.sum(grad_out * ffn_unit, axis=0)
    grad_ffn_low = norm_back(ffn_unit, inv_ffn, grad_out * gain_ffn).astype(jnp.bfloat16)
    grad_ffn_own, grad_ffn_other, inner_second = gather_both(grad_ffn_low, "seq", inner_second)
    inner_both = stacked([half_columns(inner_low, ctx_place), inner_first, inner_second])
    grad_ffn_both = stacked(grad_ffn_own + grad_ffn_other)

    grads = {
        "down": Gradients([w_down.shape], 2, 2, True),
        "gate": Gradients([w_gate.shape], 4, 1, False),
        "up": Gradients([w_up.shape], 4, 1, False),
        "out": Gradients([w_out.shape], 1, 1, False),
        "in": Gradients([w_query.shape, w_key.shape, w_value.shape], 4, 1, False),
    }
    sides = {"down": (inner_both, grad_ffn_both)}
    results = {}

    def stages():
        (grad_ffn,) = yield (grad_ffn_both[:half_rows],)
        grad_inner = times_transpose(grad_ffn, w_down)
        grad_gate = (grad_inner * up_proj * gate_sig * (1.0 + gate_proj * (1.0 - gate_sig))).astype(
            jnp.bfloat16
        )
        grad_up = (grad_inner * swish).astype(jnp.bfloat16)
        grad_gate, grad_up = yield (grad_gate, grad_up)
        gate_halves = both_halves(grad_gate)
        up_halves = both_halves(grad_up)
        gate_share = times_transpose(grad_gate, w_gate)
        gate_share, gate_halves = yield (gate_share, gate_halves)
        hidden_both = stacked([hidden_own] + hidden_rest)
        sides["gate"] = (hidden_both, stacked(gate_halves))
        partial = gate_share + times_transpose(grad_up, w_up)
        (partial,) = yield (partial,)
        grad_hidden = grad_out + to_owners(partial)
        grad_hidden, up_halves = yield (grad_hidden, up_halves)
        sides["up"] = (hidden_both, stacked(up_halves))
        gain_attn_part = jnp.sum(grad_hidden * attn_unit, axis=0)
        grad_proj_low = norm_back(attn_unit, inv_attn, grad_hidden * gain_attn).astype(jnp.bfloat16)
        grad_proj_own = stacked(gather_rows(grad_proj_low, "seq"))
        (grad_proj_own,) = yield (grad_proj_own,)
        proj_halves = both_halves(grad_proj_own)
        grad_attn_low = times_transpose(grad_proj_own, w_out).astype(jnp.bfloat16)
        backs = attend_back(query_low, key_low, value_low, grad_attn_low, lse, turns, block_rows)
        backs = yield backs
        grad_query_norm, own_dk, own_dv, prev_dk, prev_dv = backs
        back_dk, back_dv = lax.ppermute((prev_dk, prev_dv), "ctx", [(1, 0)])
        grad_query_norm, own_dk, own_dv, back_dk, back_dv, proj_halves = yield (
            grad_query_norm, own_dk, own_dv, back_dk, back_dv, proj_halves
        )
        sides["out"] = (stacked([attn_low, attn_other]), stacked(proj_halves))
        grad_value_low = (own_dv + back_dv.astype(jnp.float32)).astype(jnp.bfloat16)
        grad_key_norm = own_dk + back_dk.astype(jnp.float32)
        query_unit = query_proj * inv_query
        key_unit = key_proj * inv_key
        gain_query_part = jnp.sum(grad_query_norm * query_unit, axis=0)
        gain_key_part = jnp.sum(grad_key_norm * key_unit, axis=0)
        query_scaled = grad_query_norm * gain_query
        key_scaled = grad_key_norm * gain_key
        dots, gain_sums = lax.psum(
            (
                common_rows(
                    (
                        jnp.sum(query_scaled * query_unit, axis=1),
                        jnp.sum(key_scaled * key_unit, axis=1),
                    )
                ),
                jnp.concatenate([gain_attn_part, gain_ffn_part]),
            ),
            "seq",
        )
        dots_query, dots_key = own_rows(dots)
        grad_query_low = (
            inv_query * (query_scaled - query_unit * (dots_query / D)[:, None])
        ).astype(jnp.bfloat16)
        grad_key_low = (inv_key * (key_scaled - key_unit * (dots_key / D)[:, None])).astype(
            jnp.bfloat16
        )
        gains = jnp.concatenate([gain_sums, gain_query_part, gain_key_part]).reshape(-1, 128)
        grad_value_low, grad_key_low, grad_query_low, gains = yield (
            grad_value_low, grad_key_low, grad_query_low, gains
        )
        lows = (grad_query_low, grad_key_low, grad_value_low)
        mine = jnp.concatenate([half_columns(low, ctx_place) for low in lows], axis=1)
        given = jnp.concatenate([half_columns(low, 1 - ctx_place) for low in lows], axis=1)
        theirs = flip(given, "ctx", 1)
        gains_other = flip(gains, "ctx", 1)
        partial = (
            times_transpose(grad_query_low, w_query)
            + times_transpose(grad_key_low, w_key)
            + times_transpose(grad_value_low, w_value)
        )
        partial, gains, gains_other = yield (partial, gains, gains_other)
        gains = gains + gains_other
        gains_pair = lax.ppermute(gains, "dp", PAIRS)
        grad_tokens = grad_hidden + to_owners(partial)
        grad_tokens, gains, gains_pair, theirs = yield (grad_tokens, gains, gains_pair, theirs)
        sides["in"] = (stacked([tokens_own, tokens_other]), stacked([mine, theirs]))
        results["tokens"] = grad_tokens
        gains = gains + gains_pair
        gains_across = lax.ppermute(gains, "dp", ACROSS)
        gains, gains_across = yield (gains, gains_across)
        gains = gains + gains_across
        gains_out = lax.ppermute(gains, "dp", PAIRS)
        gains, gains_out = yield (gains, gains_out)
        results["gains"] = jnp.where(middle, gains, gains_out)

    plan = [(name, index) for name in grads for index in range(grads[name].chunks)]
    count = len(plan)
    part, pair, sent, final = {}, {}, {}, {}
    got_in, got_across, got_out, got_half = {}, {}, {}, {}
    main = stages()
    state = next(main)
    last_name, last_buffers = None, None
    token = picked
    part[0] = grads[plan[0][0]].part(sides[plan[0][0]], 0)

    for tick in range(count + 4 * STEP + 1):
        coming = sides.get(plan[tick + 1][0]) if tick + 1 < count else None
        arrived = (got_in.get(tick - STEP), got_out.get(tick - 3 * STEP), got_across.get(tick - 2 * STEP))
        if tick - STEP in got_in and got_in[tick - STEP] is arrived[1]:
            arrived = (arrived[0], None, arrived[2])
        held = (arrived, part.get(tick), coming, last_buffers, token)
        arrived, entering, coming, last_buffers, token = lax.optimization_barrier(held)
        if last_name:
            grads[last_name].buffers = last_buffers
        if entering is not None:
            part[tick] = entering
        if tick - STEP in part:
            got_in[tick - STEP] = arrived[0]
        if tick - 3 * STEP in sent:
            got_out[tick - 3 * STEP] = arrived[0] if arrived[1] is None else arrived[1]
        if tick - 2 * STEP in pair:
            got_across[tick - 2 * STEP] = arrived[2]
        alike = entering is not None and tick - 2 * STEP in pair and entering.shape == pair[tick - 2 * STEP].shape
        if alike and tick - 3 * STEP in sent and arrived[1] is None and arrived[0].shape == entering.shape:
            pair[tick - STEP], sent[tick - 2 * STEP], final[tick - 3 * STEP] = combine(
                middle, part[tick - STEP], arrived[0], pair[tick - 2 * STEP], arrived[2], sent[tick - 3 * STEP],
                entering,
            )
        else:
            if tick - STEP in part:
                pair[tick - STEP] = added(part[tick - STEP], got_in[tick - STEP])
            if tick - 2 * STEP in pair:
                leaving = added(pair[tick - 2 * STEP], got_across[tick - 2 * STEP])
                sent[tick - 2 * STEP] = jnp.where(middle, leaving, entering) if alike else leaving
            if tick - 3 * STEP in sent:
                final[tick - 3 * STEP] = jnp.where(middle, sent[tick - 3 * STEP], got_out[tick - 3 * STEP])
        held = (pair.get(tick - STEP), sent.get(tick - 2 * STEP), final.get(tick - 3 * STEP), state, token)
        crossing, leaving, swapping, state, token = lax.optimization_barrier(held)
        if crossing is not None:
            pair[tick - STEP] = crossing
            got_across[tick - STEP] = lax.ppermute(crossing, "dp", ACROSS)
        if leaving is not None:
            sent[tick - 2 * STEP] = leaving
        if alike:
            got_in[tick] = got_out[tick - 2 * STEP] = lax.ppermute(leaving, "dp", PAIRS)
        else:
            if entering is not None:
                got_in[tick] = lax.ppermute(entering, "dp", PAIRS if leaving is None else INWARD)
            if leaving is not None:
                got_out[tick - 2 * STEP] = lax.ppermute(
                    leaving, "dp", PAIRS if entering is None else OUTWARD
                )
        if swapping is not None:
            final[tick - 3 * STEP] = swapping
            got_half[tick - 3 * STEP] = flip(swapping, "ctx", 1)
        if tick - 4 * STEP in final:
            theirs, token = lax.optimization_barrier((got_half[tick - 4 * STEP], token))
            last_name, index = plan[tick - 4 * STEP]
            grads[last_name].store(index, final[tick - 4 * STEP], theirs)
            last_buffers = grads[last_name].buffers
        try:
            state = main.send(state)
        except StopIteration:
            state = ()
        if tick + 1 < count:
            name, index = plan[tick + 1]
            coming = sides[name] if coming is None else coming
            part[tick + 1] = grads[name].part(coming, index)

    gains = results["gains"].reshape(-1)
    grad_w_query, grad_w_key, grad_w_value = grads["in"].results()
    grad_gain_attn = gains[:D]
    grad_gain_ffn = gains[D : 2 * D]
    grad_gain_query = gains[2 * D : 2 * D + head_width]
    grad_gain_key = gains[2 * D + head_width :]
    return (
        out_tokens,
        results["tokens"],
        grad_w_query,
        grad_w_key,
        grad_w_value,
        grad_gain_query,
        grad_gain_key,
        *grads["out"].results(),
        grad_gain_attn,
        *grads["gate"].results(),
        *grads["up"].results(),
        *grads["down"].results(),
        grad_gain_ffn,
    )


def solution(mesh):
    in_specs = (
        P(("dp", "ctx", "seq"), None),
        P(None, "seq"),
        P(None, "seq"),
        P(None, "seq"),
        P("seq"),
        P("seq"),
        P("seq", None),
        P(),
        P(None, "seq"),
        P(None, "seq"),
        P("seq", None),
        P(),
        P(("dp", "ctx", "seq"), None),
        P("dp"),
        P(),
    )
    out_specs = (
        P(("dp", "ctx", "seq"), None),
        P(("dp", "ctx", "seq"), None),
        P(None, "seq"),
        P(None, "seq"),
        P(None, "seq"),
        P("seq"),
        P("seq"),
        P("seq", None),
        P(),
        P(None, "seq"),
        P(None, "seq"),
        P("seq", None),
        P(),
    )
    return jax.shard_map(body, mesh=mesh, in_specs=in_specs, out_specs=out_specs, check_vma=False)
```
